256 devices in a mesh: gx: 4 (over x_hi, core), gy: 8 (over y, x_lo), gz: 8 (over z).
Axes of the slice: x: 4 (x_hi: 2, x_lo: 2; x = x_hi * 2 + x_lo), y: 4, z: 8, core: 2. Of those that a mesh axis runs over, the one named last changes fastest.
Arguments:
- primal_states: float32 [2, 19, 16, 128, 1024], P(None, None, 'gx', 'gy', 'gz'), as said below
- adjoint_last: float32 [19, 16, 128, 1024], P(None, 'gx', 'gy', 'gz'), may hold values from -6 to 6
- porosity: float32 [16, 128, 1024], P('gx', 'gy', 'gz'), may hold values from 0 to 0.9
- solid_mask: int32 [16, 128, 1024], P('gx', 'gy', 'gz'), may hold values from 0 to 1, as said below
Outputs:
- adjoint_first: float32 [19, 16, 128, 1024], P(None, 'gx', 'gy', 'gz')
- porosity_grad: float32 [16, 128, 1024], P('gx', 'gy', 'gz')
- drag: float32 [], replicated
The draws below stay inside these ranges and needn't reach their ends.
Inputs may be any that keep to these rules, and one draw needn't show every extreme that they name: `primal_states`: every population is positive. `solid_mask`: every cell on the planes y = 0 and y = 127 is solid; elsewhere cells are solid at random.
All inputs are finite; a program needn't handle non-finite values.
Results may differ from the reference program's by a relative error of at most 0.00013.
Values sent between devices are 32-bit elements; how exact they have to be, the bound alone decides.
A program may use at most 128 MiB of HBM per device.

```python
import jax
import jax.numpy as jnp
import numpy as np
from jax import lax

WINDOW = 2
NX = 16
NY = 128
NZ = 1024


def lattice_parts():
    velocity = np.array([(0, 0, 0), (1, 0, 0), (-1, 0, 0), (0, 1, 0), (0, -1, 0), (0, 0, 1), (0, 0, -1), (1, 1, 0), (-1, -1, 0), (1, -1, 0), (-1, 1, 0), (1, 0, 1), (-1, 0, -1), (1, 0, -1), (-1, 0, 1), (0, 1, 1), (0, -1, -1), (0, 1, -1), (0, -1, 1)]) * 1.0
    speeds = np.sum(np.abs(velocity), axis=1)
    weights = np.where(speeds == 0, 1.0 / 3.0, np.where(speeds == 1, 1.0 / 18.0, 1.0 / 36.0))
    return (velocity, weights)


def draw_primal_states(key, part):
    velocity, weights = lattice_parts()
    key_rho, key_vel, key_noise = jax.random.split(key, 3)
    shape = (WINDOW, 1, NX, NY, NZ)
    density = 1.0 + 0.1 * jax.random.uniform(key_rho, shape, jnp.float32, -1.0, 1.0)
    speed = 0.03 * jnp.clip(jax.random.normal(key_vel, (3,) + shape, jnp.float32), -3.0, 3.0)
    speed = speed.at[0].add(0.1)
    noise = 0.05 * jnp.clip(jax.random.normal(key_noise, (WINDOW, 19, NX, NY, NZ), jnp.float32), -3.0, 3.0)
    shaped = (1, 19, 1, 1, 1)
    along = jnp.asarray(velocity[:, 0], jnp.float32).reshape(shaped) * speed[0] + jnp.asarray(velocity[:, 1], jnp.float32).reshape(shaped) * speed[1] + jnp.asarray(velocity[:, 2], jnp.float32).reshape(shaped) * speed[2]
    usquare = speed[0] * speed[0] + speed[1] * speed[1] + speed[2] * speed[2]
    equilibrium = jnp.asarray(weights, jnp.float32).reshape(shaped) * density * (1.0 + 3.0 * along + 4.5 * along * along - 1.5 * usquare)
    return (equilibrium * (1.0 + noise)).astype(jnp.float32)


def draw_solid_mask(key, part):
    picks = jax.random.randint(key, (NX, NY, NZ), 0, 8)
    rows_y = lax.broadcasted_iota(jnp.int32, (NX, NY, NZ), 1)
    solid = (picks == 0) | (rows_y == 0) | (rows_y == NY - 1)
    return jnp.where(solid, 1, 0).astype(jnp.int32)


def level_of(stream_key, extent, cuts, low, largest):
    gain = 1.0
    for dim, shards_of in cuts:
        heights = jax.random.uniform(jax.random.fold_in(jax.random.fold_in(stream_key, 6), dim), (shards_of,), jnp.float32, low / len(cuts), largest / len(cuts))
        gain = gain * jnp.repeat(jnp.exp(heights), extent[dim] // shards_of).reshape((-1,) + (1,) * (len(extent) - 1 - dim))
    return gain


def centred(stream_key, extent, deviation, reach, shards=(), kind=jnp.bfloat16):
    drawn = deviation * jax.random.normal(stream_key, extent, jnp.float32)
    if shards:
        drawn = drawn * level_of(stream_key, extent, shards, -0.22, 0.18)
    return jnp.clip(drawn, -reach, reach).astype(kind)


def setup_inputs(seed: int = 0) -> dict:
    streams_of = jax.random.split(jax.random.key(seed), 5)
    primal_states = draw_primal_states(jax.random.fold_in(streams_of[4], 71), 0)
    adjoint_last = centred(streams_of[1], (19, NX, NY, NZ), 1.0, 6.0, ((1, 4), (2, 8), (3, 8)), jnp.float32)
    porosity = jnp.clip(0.9 * jax.random.uniform(streams_of[2], (NX, NY, NZ), jnp.float32) ** level_of(streams_of[2], (NX, NY, NZ), ((0, 4), (1, 8), (2, 8)), -0.2, 0.2), 0.0, 0.9)
    solid_mask = draw_solid_mask(jax.random.fold_in(streams_of[4], 71), 0)
    return dict(primal_states=primal_states, adjoint_last=adjoint_last, porosity=porosity, solid_mask=solid_mask)


def orthonormal_rows(monomials):
    rows = []
    for column in range(monomials.shape[1]):
        vector = monomials[:, column] * 1.0
        for sweep in range(2):
            for earlier in rows:
                vector = vector - np.dot(earlier, vector) * earlier
        vector = vector / np.sqrt(np.dot(vector, vector))
        rows.append(vector)
    return np.stack(rows)

def lattice_tables():
    velocity = np.array([(0, 0, 0), (1, 0, 0), (-1, 0, 0), (0, 1, 0), (0, -1, 0), (0, 0, 1), (0, 0, -1), (1, 1, 0), (-1, -1, 0), (1, -1, 0), (-1, 1, 0), (1, 0, 1), (-1, 0, -1), (1, 0, -1), (-1, 0, 1), (0, 1, 1), (0, -1, -1), (0, 1, -1), (0, -1, 1)]) * 1.0
    speeds = np.sum(np.abs(velocity), axis=1)
    weights = np.where(speeds == 0, 1.0 / 3.0, np.where(speeds == 1, 1.0 / 18.0, 1.0 / 36.0))
    opposite = np.zeros((19, 19))
    for member in range(19):
        for other in range(19):
            if np.all(velocity[other] == -velocity[member]):
                opposite[member, other] = 1.0
    vx = velocity[:, 0]
    vy = velocity[:, 1]
    vz = velocity[:, 2]
    columns = [np.ones(19), vx, vy, vz, vx * vx, vy * vy, vz * vz, vx * vy, vx * vz, vy * vz, vx * vy * vy, vx * vz * vz, vy * vx * vx, vy * vz * vz, vz * vx * vx, vz * vy * vy, vx * vx * vy * vy, vx * vx * vz * vz, vy * vy * vz * vz]
    monomials = np.stack(columns, axis=1)
    basis = orthonormal_rows(monomials)
    rates = np.array([0.0] * 4 + [1.6] * 6 + [1.2] * 9)
    return (velocity, weights, opposite, basis, rates)

def collide(state, blocking):
    velocity, weights, opposite, basis, rates = lattice_tables()
    highest = lax.Precision.HIGHEST
    vel = jnp.asarray(velocity, jnp.float32)
    density = lax.optimization_barrier(jnp.sum(state, axis=0))
    momentum = jnp.dot(vel.T, state, precision=highest)
    speed = momentum / density[None, :]
    along = jnp.dot(vel, speed, precision=highest)
    usquare = lax.optimization_barrier(jnp.sum(speed * speed, axis=0))
    equilibrium = jnp.asarray(weights, jnp.float32)[:, None] * density[None, :] * (1.0 + 3.0 * along + 4.5 * along * along - 1.5 * usquare[None, :])
    basis_rows = jnp.asarray(basis, jnp.float32)
    moments = jnp.dot(basis_rows, state - equilibrium, precision=highest)
    relaxed = jnp.asarray(rates, jnp.float32)[:, None] * moments
    post = state - jnp.dot(basis_rows.T, relaxed, precision=highest)
    bounced = jnp.dot(jnp.asarray(opposite, jnp.float32), state, precision=highest)
    return (1.0 - blocking[None, :]) * post + blocking[None, :] * bounced

def adjoint_step(read, state, blocking):
    velocity = jnp.asarray(lattice_tables()[0], jnp.float32)
    unused, pull = jax.vjp(collide, state, blocking)
    d_state, d_block = pull(read)
    flux_x = jnp.dot(velocity[:, 0], state, precision=lax.Precision.HIGHEST)
    adjoint = d_state + velocity[:, 0:1] * blocking[None, :]
    return (adjoint, d_block + flux_x, jnp.sum(blocking * flux_x))

def reference(primal_states, adjoint_last, porosity, solid_mask):
    velocity = lattice_tables()[0]
    fluid = solid_mask == 0
    blocking = jnp.where(fluid, porosity, jnp.ones_like(porosity))
    adjoint = adjoint_last
    gradient = jnp.zeros_like(porosity)
    total = jnp.zeros((), jnp.float32)
    for instant in (1, 0):
        read = jnp.stack([jnp.roll(adjoint[member], (-int(velocity[member, 0]), -int(velocity[member, 1]), -int(velocity[member, 2])), axis=(0, 1, 2)) for member in range(19)])
        items = (jnp.moveaxis(read, 1, 0).reshape(NX, 19, NY * NZ), jnp.moveaxis(primal_states[instant], 1, 0).reshape(NX, 19, NY * NZ), blocking.reshape(NX, NY * NZ))

        def plane(pieces):
            return adjoint_step(pieces[0], pieces[1], pieces[2])
        fresh, d_block, drag_parts = lax.map(plane, items)
        adjoint = jnp.moveaxis(fresh.reshape(NX, 19, NY, NZ), 0, 1)
        gradient = gradient + d_block.reshape(NX, NY, NZ)
        total = total + jnp.sum(drag_parts)
    porosity_grad = jnp.where(fluid, gradient, jnp.zeros_like(gradient))
    return (adjoint, porosity_grad, total / (NX * NY * NZ))
```

```python
import functools

import jax
import jax.numpy as jnp
import numpy as np
from jax import lax
from jax.experimental import pallas as pl
from jax.experimental.pallas import tpu as pltpu
from jax.sharding import PartitionSpec as P

MESH = pl.DeviceIdType.MESH
F32 = jnp.float32

VELOCITY = (
    (0, 0, 0),
    (1, 0, 0),
    (-1, 0, 0),
    (0, 1, 0),
    (0, -1, 0),
    (0, 0, 1),
    (0, 0, -1),
    (1, 1, 0),
    (-1, -1, 0),
    (1, -1, 0),
    (-1, 1, 0),
    (1, 0, 1),
    (-1, 0, -1),
    (1, 0, -1),
    (-1, 0, 1),
    (0, 1, 1),
    (0, -1, -1),
    (0, 1, -1),
    (0, -1, 1),
)
ALONG = tuple(
    {sign: tuple(i for i in range(19) if VELOCITY[i][dim] == sign) for sign in (1, -1)} for dim in range(3)
)
FACES = ((1, 2), (3, 4), (5, 6))
EDGES = (((0, 1), (7, 8), (9, 10)), ((0, 2), (11, 12), (13, 14)), ((1, 2), (15, 16), (17, 18)))


def orthonormal_rows(monomials):
    rows = []
    for column in range(monomials.shape[1]):
        vector = monomials[:, column] * 1.0
        for sweep in range(2):
            for earlier in rows:
                vector = vector - np.dot(earlier, vector) * earlier
        vector = vector / np.sqrt(np.dot(vector, vector))
        rows.append(vector)
    return np.stack(rows)


def coefficients():
    vel = np.array(VELOCITY) * 1.0
    speeds = np.sum(np.abs(vel), axis=1)
    weights = np.where(speeds == 0, 1.0 / 3.0, np.where(speeds == 1, 1.0 / 18.0, 1.0 / 36.0))
    x, y, z = vel[:, 0], vel[:, 1], vel[:, 2]
    columns = [np.ones(19), x, y, z, x * x, y * y, z * z, x * y, x * z, y * z]
    columns += [x * y * y, x * z * z, y * x * x, y * z * z, z * x * x, z * y * y]
    columns += [x * x * y * y, x * x * z * z, y * y * z * z]
    basis = orthonormal_rows(np.stack(columns, axis=1))
    rates = np.array([0.0] * 4 + [1.6] * 6 + [1.2] * 9)
    relax = basis.T @ np.diag(rates) @ basis
    kept = 1.2 * np.eye(19) - relax
    scalar = relax @ weights
    square = relax @ (weights * x * x)
    first = relax @ (weights * x)
    face = (kept[1] + kept[2]) / 2 - kept[0]
    return dict(
        s0=(scalar[0], scalar[1], scalar[7]),
        s1=(first[1], first[7]),
        s2=(square[0], square[3], square[15], square[1] - square[3], square[7] - square[15]),
        s2_mixed=(relax @ (weights * x * y))[7],
        even=(kept[0][0], kept[0][1], kept[0][7]),
        odd=kept[1][1] / 2 - kept[1][2] / 2,
        square=(face[0], face[3], face[15], face[1] - face[3], face[7] - face[15]),
        mixed=(kept[7][7] + kept[8][7] - kept[9][7] - kept[10][7]) / 4,
    )


COEF = {name: tuple(np.asarray(v, np.float64).reshape(-1).tolist()) for name, v in coefficients().items()}


def pair_sums(members):
    face_sum = [members[a] + members[b] for a, b in FACES]
    face_diff = [members[a] - members[b] for a, b in FACES]
    edge = []
    for dims, (a, b), (c, d) in EDGES:
        edge.append((members[a] + members[b], members[a] - members[b], members[c] + members[d], members[c] - members[d]))
    plane = [e[0] + e[2] for e in edge]
    mixed = [e[0] - e[2] for e in edge]
    lean = [(e[1] + e[3], e[1] - e[3]) for e in edge]
    edge_square = [plane[0] + plane[1], plane[0] + plane[2], plane[1] + plane[2]]
    edge_diff = [lean[0][0] + lean[1][0], lean[0][1] + lean[2][0], lean[1][1] + lean[2][1]]
    face_total = face_sum[0] + face_sum[1] + face_sum[2]
    edge_total = plane[0] + plane[1] + plane[2]
    return face_sum, face_diff, edge, mixed, edge_square, edge_diff, face_total, edge_total


def primal_terms(state):
    face_sum, face_diff, edge, mixed, edge_square, edge_diff, face_total, edge_total = pair_sums(state)
    rho = state[0] + face_total + edge_total
    inverse = 1.0 / rho
    flux = [face_diff[a] + edge_diff[a] for a in range(3)]
    vel = [flux[a] * inverse for a in range(3)]
    third = rho * (1.0 / 3.0)
    press = [face_sum[a] + edge_square[a] - third - flux[a] * vel[a] for a in range(3)]
    total = press[0] + press[1] + press[2]
    centre = total * (2.0 / 21.0)
    stress = [0.4 * (press[a] * (1.0 / 6.0) + centre) for a in range(3)]
    shear = [0.1 * (mixed[e] - flux[dims[0]] * vel[dims[1]]) for e, (dims, _, _) in enumerate(EDGES)]
    flat = (stress[0] + stress[1] + stress[2]) * (-10.0 / 19.0)
    usq = vel[0] * vel[0] + vel[1] * vel[1] + vel[2] * vel[2]
    still = rho * (1.0 - 1.5 * usq)
    rest = 1.2 * state[0] + flat - 0.4 * still
    even, odd = [], []
    for a in range(3):
        feq_even = still + (4.5 * flux[a]) * vel[a]
        even.append(0.6 * face_sum[a] + (flat + stress[a]) - (1.2 / 18.0) * feq_even)
        odd.append(-0.4 * face_diff[a] - (3.6 / 18.0) * flux[a])
    for e, (dims, _, _) in enumerate(EDGES):
        p, q = dims
        bend = flat + stress[p] + stress[q]
        for sign, total_pair, diff_pair in ((1, edge[e][0], edge[e][1]), (-1, edge[e][2], edge[e][3])):
            along_flux = flux[p] + flux[q] if sign == 1 else flux[p] - flux[q]
            along_vel = vel[p] + vel[q] if sign == 1 else vel[p] - vel[q]
            feq_even = still + (4.5 * along_flux) * along_vel
            twist = bend + shear[e] if sign == 1 else bend - shear[e]
            even.append(0.6 * total_pair + twist - (1.2 / 36.0) * feq_even)
            odd.append(-0.4 * diff_pair - (3.6 / 36.0) * along_flux)
    return vel, flux[0], [rest] + even + odd


def pull_back(read, vel, blocking):
    c = COEF
    face_sum, face_diff, edge, mixed, edge_square, edge_diff, face_total, edge_total = pair_sums(read)
    rest = read[0]

    def by_class(f):
        return f[0] * rest + f[1] * face_total + f[2] * edge_total

    s0 = by_class(c["s0"])
    s2_flat = by_class(c["s2"][:3])
    s2 = [s2_flat + c["s2"][3] * face_sum[a] + c["s2"][4] * edge_square[a] for a in range(3)]
    shear = [c["s2_mixed"][0] * mixed[e] for e in range(3)]
    xy, xz, yz = shear
    turned = [
        s2[0] * vel[0] + xy * vel[1] + xz * vel[2],
        xy * vel[0] + s2[1] * vel[1] + yz * vel[2],
        xz * vel[0] + yz * vel[1] + s2[2] * vel[2],
    ]
    bend = [3.0 * turned[a] - vel[a] * s0 for a in range(3)]
    density = s0 - 1.5 * (vel[0] * bend[0] + vel[1] * bend[1] + vel[2] * bend[2])
    open_part = 1.0 - blocking
    momentum = []
    for a in range(3):
        s1 = c["s1"][0] * face_diff[a] + c["s1"][1] * edge_diff[a]
        slope = c["odd"][0] * (face_diff[a] + edge_diff[a]) + 3.0 * (s1 + bend[a])
        slope = open_part * slope
        momentum.append(slope + blocking if a == 0 else slope)
    even = open_part * (by_class(c["even"]) + density)
    sq_flat = by_class(c["square"][:3])
    square = [open_part * (sq_flat + c["square"][3] * face_sum[a] + c["square"][4] * edge_square[a]) for a in range(3)]
    cross = [(c["mixed"][0] * open_part) * mixed[e] for e in range(3)]
    keep_sum = 0.6 * blocking - 0.1
    keep_diff = -0.1 - 0.4 * blocking
    out = [None] * 19
    out[0] = (2.0 * keep_sum) * rest + even
    for a, (i, j) in enumerate(FACES):
        half = keep_sum * face_sum[a] + (even + square[a])
        tilt = keep_diff * face_diff[a] + momentum[a]
        out[i], out[j] = half + tilt, half - tilt
    for e, (dims, same, cross_pair) in enumerate(EDGES):
        p, q = dims
        level = even + square[p] + square[q]
        half = keep_sum * edge[e][0] + (level + cross[e])
        tilt = keep_diff * edge[e][1] + (momentum[p] + momentum[q])
        out[same[0]], out[same[1]] = half + tilt, half - tilt
        half = keep_sum * edge[e][2] + (level - cross[e])
        tilt = keep_diff * edge[e][3] + (momentum[p] - momentum[q])
        out[cross_pair[0]], out[cross_pair[1]] = half + tilt, half - tilt
    sums = list(face_sum) + [s for e in edge for s in (e[0], e[2])]
    diffs = list(face_diff) + [d for e in edge for d in (e[1], e[3])]
    return out, [rest] + sums + diffs


def slot(sign):
    return 0 if sign == 1 else 1


def member_at(velocity):
    return VELOCITY.index(velocity)


BODY = 8


def kernel(
    mesh_sizes,
    extent,
    primal,
    adjoint,
    porosity,
    solid,
    out_adjoint,
    out_grad,
    out_drag,
    level_two,
    level_one,
    states,
    porous,
    marks,
    block,
    grad,
    terms,
    result,
    face_send,
    rows_send,
    columns_send,
    face_recv,
    rows_recv,
    columns_recv,
    rows_edge,
    columns_edge,
    drag_row,
    drag_first,
    drag_second,
    load_sem,
    store_sem,
    send_sem,
    recv_sem,
    drag_send_sem,
    drag_recv_sem,
):
    sx, sy, sz = mesh_sizes
    nx, ny, nz = extent
    halves = ny // 8
    body = pl.ds(BODY, ny)
    me = (lax.axis_index("gx"), lax.axis_index("gy"), lax.axis_index("gz"))

    def shifted(offset):
        return tuple(lax.rem(me[d] + mesh_sizes[d] + offset[d], mesh_sizes[d]) for d in range(3))

    faces = [tuple(s if d == dim else 0 for d in range(3)) for dim in range(3) for s in (1, -1)]
    edges = [
        tuple(s if d == p else t if d == q else 0 for d in range(3))
        for p, q in ((0, 2), (0, 1), (1, 2))
        for s in (1, -1)
        for t in (1, -1)
    ]
    around = faces + edges

    pair, core = me[0] // 2, me[0] % 2
    pairs = sx // 2
    first_group = [(c, z) for c in range(2) for z in range(sz) if (c, z) != (0, 0)]
    second_group = [(h, y) for h in range(pairs) for y in range(sy) if (h, y) != (0, 0)]

    def first_partner(c, z):
        return (pair * 2 + lax.rem(core + c, 2), me[1], lax.rem(me[2] + z, sz))

    def second_partner(h, y):
        return (lax.rem(pair + h, pairs) * 2 + core, lax.rem(me[1] + y, sy), me[2])

    barrier = pltpu.get_barrier_semaphore()
    targets = [first_partner(c, z) for c, z in first_group if (c, z) not in ((0, 1), (0, sz - 1))]
    targets += [second_partner(h, y) for h, y in second_group if (h, y) not in ((0, 1), (0, sy - 1))]
    targets += [shifted(offset) for offset in around]
    for target in targets:
        pl.semaphore_signal(barrier, inc=1, device_id=target, device_id_type=MESH)

    loads = [
        pltpu.make_async_copy(adjoint, level_two.at[:, :, body, :], load_sem.at[0]),
        pltpu.make_async_copy(porosity, porous, load_sem.at[1]),
        pltpu.make_async_copy(solid, marks, load_sem.at[2]),
        pltpu.make_async_copy(primal, states, load_sem.at[3]),
    ]
    for load in loads:
        load.start()

    lane = lax.broadcasted_iota(jnp.int32, (8, nz), 1)

    def pack(step, cells):
        for sign in (1, -1):
            at = slot(sign)
            edge_row = BODY if sign == 1 else BODY + ny - 1
            for k, i in enumerate(ALONG[1][sign]):
                for x in range(nx):
                    rows_send[step, at, k * nx + x : k * nx + x + 1, :] = cells[i, x, edge_row : edge_row + 1, :]
            for h in range(halves):
                packed = jnp.zeros((8, nz), F32)
                for k, i in enumerate(ALONG[2][sign]):
                    for x in range(nx):
                        spot = k * nx + x
                        column = cells[i, x, BODY + 8 * h : BODY + 8 * h + 8, :]
                        turn = (spot if sign == 1 else spot + 1) % nz
                        column = pltpu.roll(column, turn, 1) if turn else column
                        packed = jnp.where(lane == spot, column, packed)
                columns_send[step, at, 8 * h : 8 * h + 8, :] = packed

    def messages(step, cells):
        made = {}
        count = 0

        def add(direction, source, target):
            nonlocal count
            back = tuple(-d for d in direction)
            copy = pltpu.make_async_remote_copy(
                src_ref=source,
                dst_ref=target,
                send_sem=send_sem.at[step, count],
                recv_sem=recv_sem.at[step, count],
                device_id=shifted(back),
                device_id_type=MESH,
            )
            made.setdefault(direction, []).append(copy)
            count += 1

        for direction in around:
            dx, dy, dz = direction
            if dx and not dy and not dz:
                near = 0 if dx == 1 else nx - 1
                if step == 0:
                    for k, i in enumerate(ALONG[0][dx]):
                        add(direction, cells.at[i, near, body, :], face_recv.at[step, slot(dx), k, body, :])
                else:
                    add(direction, face_send.at[slot(dx)], face_recv.at[step, slot(dx), :, body, :])
            elif dy and not dx and not dz:
                add(direction, rows_send.at[step, slot(dy)], rows_recv.at[step, slot(dy)])
            elif dz and not dx and not dy:
                add(direction, columns_send.at[step, slot(dz)], columns_recv.at[step, slot(dz), body, :])
            elif not dz:
                row = xy_row(dx, dy)
                source = rows_send.at[step, slot(dy), pl.ds(row // 8 * 8, 8), :]
                add(direction, source, rows_edge.at[step, slot(dx) * 2 + slot(dy)])
            elif not dy:
                source = columns_send.at[step, slot(dz)]
                add(direction, source, columns_edge.at[step, slot(dx) * 2 + slot(dz)])
            else:
                near, far = (0, BODY + ny) if dy == 1 else (ny - 8, BODY - 8)
                source = columns_send.at[step, slot(dz), pl.ds(near, 8), :]
                add(direction, source, columns_recv.at[step, slot(dz), pl.ds(far, 8), :])
        return made

    def xy_row(dx, dy):
        k = ALONG[1][dy].index(member_at((dx, dy, 0)))
        return k * nx + (0 if dx == 1 else nx - 1)

    def halo_row(sign):
        return BODY + ny if sign == 1 else BODY - 1

    def insert_rows(step, cells):
        for sign in (1, -1):
            row = halo_row(sign)
            for k, i in enumerate(ALONG[1][sign]):
                for x in range(nx):
                    if 0 <= x - VELOCITY[i][0] < nx:
                        got = rows_recv[step, slot(sign), k * nx + x : k * nx + x + 1, :]
                        cells[i, x, row : row + 1, :] = got

    def insert_edges(step):
        for dx in (1, -1):
            for dy in (1, -1):
                k = ALONG[0][dx].index(member_at((dx, dy, 0)))
                r = xy_row(dx, dy) % 8
                row = halo_row(dy)
                face_recv[step, slot(dx), k, row : row + 1, :] = rows_edge[step, slot(dx) * 2 + slot(dy), r : r + 1, :]

    def read_cells(step, cells, x, h):
        read = []
        for i, (dx, dy, dz) in enumerate(VELOCITY):
            from_x = x + dx
            outside = not 0 <= from_x < nx
            rows = slice(BODY + 8 * h + dy, BODY + 8 * h + dy + 8)
            if outside:
                value = face_recv[step, slot(dx), ALONG[0][dx].index(i), rows, :]
            else:
                value = cells[i, from_x, rows, :]
            if dz:
                spot = ALONG[2][dz].index(i) * nx + from_x % nx
                if outside:
                    column = columns_edge[step, slot(dx) * 2 + slot(dz), 8 * h : 8 * h + 8, :]
                else:
                    column = columns_recv[step, slot(dz), rows, :]
                last = nz - 1 if dz == 1 else 0
                turn = (last - spot) % nz
                column = pltpu.roll(column, turn, 1) if turn else column
                value = jnp.where(lane == last, column, pltpu.roll(value, nz - 1 if dz == 1 else 1, 1))
            read.append(value)
        return read

    def level(step, cells, x, h):
        rows = slice(8 * h, 8 * h + 8)
        read = read_cells(step, cells, x, h)
        vel = [terms[step, a, x, rows, :] for a in range(3)]
        fresh, weighed = pull_back(read, vel, block[x, rows, :])
        total = grad[x, rows, :]
        for j, value in enumerate(weighed):
            total = total + value * terms[step, 3 + j, x, rows, :]
        grad[x, rows, :] = total
        return fresh

    loads[0].wait()
    pack(0, level_two)
    loads[1].wait()
    loads[2].wait()
    loads[3].wait()
    total = jnp.zeros((8, nz), F32)
    for x in range(nx):
        for h in range(halves):
            rows = slice(8 * h, 8 * h + 8)
            closed = jnp.where(marks[x, rows, :] == 0, porous[x, rows, :], 1.0)
            block[x, rows, :] = closed
            flux = None
            for t in range(2):
                gain = sum(states[t, i, x, rows, :] for i in ALONG[0][1])
                loss = sum(states[t, i, x, rows, :] for i in ALONG[0][-1])
                flux = gain - loss if flux is None else flux + (gain - loss)
            grad[x, rows, :] = flux
            total = total + closed * flux
    drag_row[0] = jnp.sum(total, axis=0, keepdims=True)

    pl.semaphore_wait(barrier, len(targets))

    first = messages(0, level_two)
    for direction in around:
        for copy in first[direction]:
            copy.start()

    mine_first = core * sz + me[2]
    mine_second = pair * sy + me[1]

    def drag_copies(stage, source, target, mine, group, partner, base):
        return [
            pltpu.make_async_remote_copy(
                src_ref=source,
                dst_ref=target.at[mine],
                send_sem=drag_send_sem.at[base + n],
                recv_sem=drag_recv_sem.at[base + n],
                device_id=partner(*offset),
                device_id_type=MESH,
            )
            for n, offset in enumerate(group)
        ]

    gather_first = drag_copies(0, drag_row.at[0], drag_first, mine_first, first_group, first_partner, 0)
    for copy in gather_first:
        copy.start()
    drag_first[mine_first] = drag_row[0]

    for step, t in ((0, 1), (1, 0)):
        for x in range(nx):
            for h in range(halves):
                rows = slice(8 * h, 8 * h + 8)
                vel, _, weights = primal_terms([states[t, i, x, rows, :] for i in range(19)])
                for j, value in enumerate(vel + weights):
                    terms[step, j, x, rows, :] = value

    for direction in around:
        for copy in first[direction]:
            copy.wait_recv()
    insert_rows(0, level_two)
    insert_edges(0)

    second = messages(1, level_one)

    def first_level(x):
        for h in range(halves):
            fresh = level(0, level_two, x, h)
            for i in range(19):
                level_one[i, x, BODY + 8 * h : BODY + 8 * h + 8, :] = fresh[i]
            for sign, near in ((1, 0), (-1, nx - 1)):
                if x == near:
                    for k, i in enumerate(ALONG[0][sign]):
                        face_send[slot(sign), k, 8 * h : 8 * h + 8, :] = fresh[i]

    first_level(0)
    first_level(nx - 1)
    for direction in faces[:2]:
        for copy in second[direction]:
            copy.start()
    for x in range(1, nx - 1):
        first_level(x)
    pack(1, level_one)
    for direction in around[2:]:
        for copy in second[direction]:
            copy.start()

    for copy in gather_first:
        copy.wait_recv()
    drag_row[1] = jnp.sum(drag_first[...], axis=0)
    gather_second = drag_copies(1, drag_row.at[1], drag_second, mine_second, second_group, second_partner, len(first_group))
    for copy in gather_second:
        copy.start()
    drag_second[mine_second] = drag_row[1]

    def second_level(x):
        for h in range(halves):
            rows = slice(8 * h, 8 * h + 8)
            fresh = level(1, level_one, x, h)
            for i in range(19):
                result[i, x, rows, :] = fresh[i]
        store = pltpu.make_async_copy(result.at[:, x], out_adjoint.at[:, x], store_sem.at[x])
        store.start()
        return store

    stores = []
    late = [d for d in around if d[0]]
    for direction in around:
        if direction not in late:
            for copy in second[direction]:
                copy.wait_recv()
    insert_rows(1, level_one)
    for x in range(1, nx - 1):
        stores.append(second_level(x))
    for direction in late:
        for copy in second[direction]:
            copy.wait_recv()
    insert_edges(1)
    for x in (0, nx - 1):
        stores.append(second_level(x))

    for x in range(nx):
        out_grad[x] = jnp.where(marks[x] == 0, grad[x], 0.0)

    for copy in gather_second:
        copy.wait_recv()
    everyone = jnp.sum(jnp.sum(drag_second[...], axis=0)) * (1.0 / (nx * ny * nz * sx * sy * sz))
    out_drag[0, 0] = everyone

    for store in stores:
        store.wait()
    for sent in (first, second):
        for direction in around:
            for copy in sent[direction]:
                copy.wait_send()
    for copy in gather_first + gather_second:
        copy.wait_send()


def solution(mesh):
    sizes = tuple(mesh.shape[name] for name in ("gx", "gy", "gz"))

    def body(primal_states, adjoint_last, porosity, solid_mask):
        nx, ny, nz = porosity.shape
        padded = ny + 16
        row_tiles = -(-5 * nx // 8) * 8
        copies = 26
        links = (2 * sizes[2] - 1) + (sizes[0] // 2 * sizes[1] - 1)
        hbm = pl.BlockSpec(memory_space=pl.ANY)
        adjoint, gradient, drag = pl.pallas_call(
            functools.partial(kernel, sizes, (nx, ny, nz)),
            name="adjoint_window",
            out_shape=(
                jax.ShapeDtypeStruct((19, nx, ny, nz), F32),
                jax.ShapeDtypeStruct((nx, ny, nz), F32),
                jax.ShapeDtypeStruct((1, 1), F32),
            ),
            in_specs=[hbm] * 4,
            out_specs=(
                hbm,
                pl.BlockSpec(memory_space=pltpu.VMEM),
                pl.BlockSpec(memory_space=pltpu.SMEM),
            ),
            scratch_shapes=[
                pltpu.VMEM((19, nx, padded, nz), F32),
                pltpu.VMEM((19, nx, padded, nz), F32),
                pltpu.VMEM((2, 19, nx, ny, nz), F32),
                pltpu.VMEM((nx, ny, nz), F32),
                pltpu.VMEM((nx, ny, nz), jnp.int32),
                pltpu.VMEM((nx, ny, nz), F32),
                pltpu.VMEM((nx, ny, nz), F32),
                pltpu.VMEM((2, 22, nx, ny, nz), F32),
                pltpu.VMEM((19, nx, ny, nz), F32),
                pltpu.VMEM((2, 5, ny, nz), F32),
                pltpu.VMEM((2, 2, row_tiles, nz), F32),
                pltpu.VMEM((2, 2, ny, nz), F32),
                pltpu.VMEM((2, 2, 5, padded, nz), F32),
                pltpu.VMEM((2, 2, row_tiles, nz), F32),
                pltpu.VMEM((2, 2, padded, nz), F32),
                pltpu.VMEM((2, 4, 8, nz), F32),
                pltpu.VMEM((2, 4, ny, nz), F32),
                pltpu.VMEM((2, 1, nz), F32),
                pltpu.VMEM((2 * sizes[2], 1, nz), F32),
                pltpu.VMEM((sizes[0] // 2 * sizes[1], 1, nz), F32),
                pltpu.SemaphoreType.DMA((4,)),
                pltpu.SemaphoreType.DMA((nx,)),
                pltpu.SemaphoreType.DMA((2, copies)),
                pltpu.SemaphoreType.DMA((2, copies)),
                pltpu.SemaphoreType.DMA((links,)),
                pltpu.SemaphoreType.DMA((links,)),
            ],
            compiler_params=pltpu.CompilerParams(collective_id=0, has_side_effects=True),
        )(primal_states, adjoint_last, porosity, solid_mask)
        return adjoint, gradient, drag.reshape(())

    return jax.shard_map(
        body,
        mesh=mesh,
        in_specs=(
            P(None, None, "gx", "gy", "gz"),
            P(None, "gx", "gy", "gz"),
            P("gx", "gy", "gz"),
            P("gx", "gy", "gz"),
        ),
        out_specs=(P(None, "gx", "gy", "gz"), P("gx", "gy", "gz"), P()),
        check_vma=False,
    )
```

```python
import functools

import jax
import jax.numpy as jnp
import numpy as np
from jax import lax
from jax.experimental import pallas as pl
from jax.experimental.pallas import tpu as pltpu
from jax.sharding import PartitionSpec as P

MESH = pl.DeviceIdType.MESH
F32 = jnp.float32

VELOCITY = (
    (0, 0, 0),
    (1, 0, 0),
    (-1, 0, 0),
    (0, 1, 0),
    (0, -1, 0),
    (0, 0, 1),
    (0, 0, -1),
    (1, 1, 0),
    (-1, -1, 0),
    (1, -1, 0),
    (-1, 1, 0),
    (1, 0, 1),
    (-1, 0, -1),
    (1, 0, -1),
    (-1, 0, 1),
    (0, 1, 1),
    (0, -1, -1),
    (0, 1, -1),
    (0, -1, 1),
)
ALONG = tuple(
    {sign: tuple(i for i in range(19) if VELOCITY[i][dim] == sign) for sign in (1, -1)} for dim in range(3)
)
FACES = ((1, 2), (3, 4), (5, 6))
EDGES = (((0, 1), (7, 8), (9, 10)), ((0, 2), (11, 12), (13, 14)), ((1, 2), (15, 16), (17, 18)))


def orthonormal_rows(monomials):
    rows = []
    for column in range(monomials.shape[1]):
        vector = monomials[:, column] * 1.0
        for sweep in range(2):
            for earlier in rows:
                vector = vector - np.dot(earlier, vector) * earlier
        vector = vector / np.sqrt(np.dot(vector, vector))
        rows.append(vector)
    return np.stack(rows)


def coefficients():
    vel = np.array(VELOCITY) * 1.0
    speeds = np.sum(np.abs(vel), axis=1)
    weights = np.where(speeds == 0, 1.0 / 3.0, np.where(speeds == 1, 1.0 / 18.0, 1.0 / 36.0))
    x, y, z = vel[:, 0], vel[:, 1], vel[:, 2]
    columns = [np.ones(19), x, y, z, x * x, y * y, z * z, x * y, x * z, y * z]
    columns += [x * y * y, x * z * z, y * x * x, y * z * z, z * x * x, z * y * y]
    columns += [x * x * y * y, x * x * z * z, y * y * z * z]
    basis = orthonormal_rows(np.stack(columns, axis=1))
    rates = np.array([0.0] * 4 + [1.6] * 6 + [1.2] * 9)
    relax = basis.T @ np.diag(rates) @ basis
    kept = 1.2 * np.eye(19) - relax
    scalar = relax @ weights
    square = relax @ (weights * x * x)
    first = relax @ (weights * x)
    face = (kept[1] + kept[2]) / 2 - kept[0]
    return dict(
        s0=(scalar[0], scalar[1], scalar[7]),
        s1=(first[1], first[7]),
        s2=(square[0], square[3], square[15], square[1] - square[3], square[7] - square[15]),
        s2_mixed=(relax @ (weights * x * y))[7],
        even=(kept[0][0], kept[0][1], kept[0][7]),
        odd=kept[1][1] / 2 - kept[1][2] / 2,
        square=(face[0], face[3], face[15], face[1] - face[3], face[7] - face[15]),
        mixed=(kept[7][7] + kept[8][7] - kept[9][7] - kept[10][7]) / 4,
    )


COEF = {name: tuple(np.asarray(v, np.float64).reshape(-1).tolist()) for name, v in coefficients().items()}


def pair_sums(members):
    face_sum = [members[a] + members[b] for a, b in FACES]
    face_diff = [members[a] - members[b] for a, b in FACES]
    edge = []
    for dims, (a, b), (c, d) in EDGES:
        edge.append((members[a] + members[b], members[a] - members[b], members[c] + members[d], members[c] - members[d]))
    plane = [e[0] + e[2] for e in edge]
    mixed = [e[0] - e[2] for e in edge]
    lean = [(e[1] + e[3], e[1] - e[3]) for e in edge]
    edge_square = [plane[0] + plane[1], plane[0] + plane[2], plane[1] + plane[2]]
    edge_diff = [lean[0][0] + lean[1][0], lean[0][1] + lean[2][0], lean[1][1] + lean[2][1]]
    face_total = face_sum[0] + face_sum[1] + face_sum[2]
    edge_total = plane[0] + plane[1] + plane[2]
    return face_sum, face_diff, edge, mixed, edge_square, edge_diff, face_total, edge_total


def primal_terms(state):
    face_sum, face_diff, edge, mixed, edge_square, edge_diff, face_total, edge_total = pair_sums(state)
    rho = state[0] + face_total + edge_total
    inverse = 1.0 / rho
    flux = [face_diff[a] + edge_diff[a] for a in range(3)]
    vel = [flux[a] * inverse for a in range(3)]
    third = rho * (1.0 / 3.0)
    press = [face_sum[a] + edge_square[a] - third - flux[a] * vel[a] for a in range(3)]
    total = press[0] + press[1] + press[2]
    centre = total * (2.0 / 21.0)
    stress = [0.4 * (press[a] * (1.0 / 6.0) + centre) for a in range(3)]
    shear = [0.1 * (mixed[e] - flux[dims[0]] * vel[dims[1]]) for e, (dims, _, _) in enumerate(EDGES)]
    flat = (stress[0] + stress[1] + stress[2]) * (-10.0 / 19.0)
    usq = vel[0] * vel[0] + vel[1] * vel[1] + vel[2] * vel[2]
    still = rho * (1.0 - 1.5 * usq)
    rest = 1.2 * state[0] + flat - 0.4 * still
    even, odd = [], []
    for a in range(3):
        feq_even = still + (4.5 * flux[a]) * vel[a]
        even.append(0.6 * face_sum[a] + (flat + stress[a]) - (1.2 / 18.0) * feq_even)
        odd.append(-0.4 * face_diff[a] - (3.6 / 18.0) * flux[a])
    for e, (dims, _, _) in enumerate(EDGES):
        p, q = dims
        bend = flat + stress[p] + stress[q]
        for sign, total_pair, diff_pair in ((1, edge[e][0], edge[e][1]), (-1, edge[e][2], edge[e][3])):
            along_flux = flux[p] + flux[q] if sign == 1 else flux[p] - flux[q]
            along_vel = vel[p] + vel[q] if sign == 1 else vel[p] - vel[q]
            feq_even = still + (4.5 * along_flux) * along_vel
            twist = bend + shear[e] if sign == 1 else bend - shear[e]
            even.append(0.6 * total_pair + twist - (1.2 / 36.0) * feq_even)
            odd.append(-0.4 * diff_pair - (3.6 / 36.0) * along_flux)
    return vel, flux[0], [rest] + even + odd


def pull_back(read, vel, blocking):
    c = COEF
    face_sum, face_diff, edge, mixed, edge_square, edge_diff, face_total, edge_total = pair_sums(read)
    rest = read[0]

    def by_class(f):
        return f[0] * rest + f[1] * face_total + f[2] * edge_total

    s0 = by_class(c["s0"])
    s2_flat = by_class(c["s2"][:3])
    s2 = [s2_flat + c["s2"][3] * face_sum[a] + c["s2"][4] * edge_square[a] for a in range(3)]
    shear = [c["s2_mixed"][0] * mixed[e] for e in range(3)]
    xy, xz, yz = shear
    turned = [
        s2[0] * vel[0] + xy * vel[1] + xz * vel[2],
        xy * vel[0] + s2[1] * vel[1] + yz * vel[2],
        xz * vel[0] + yz * vel[1] + s2[2] * vel[2],
    ]
    bend = [3.0 * turned[a] - vel[a] * s0 for a in range(3)]
    density = s0 - 1.5 * (vel[0] * bend[0] + vel[1] * bend[1] + vel[2] * bend[2])
    open_part = 1.0 - blocking
    momentum = []
    for a in range(3):
        s1 = c["s1"][0] * face_diff[a] + c["s1"][1] * edge_diff[a]
        slope = c["odd"][0] * (face_diff[a] + edge_diff[a]) + 3.0 * (s1 + bend[a])
        slope = open_part * slope
        momentum.append(slope + blocking if a == 0 else slope)
    even = open_part * (by_class(c["even"]) + density)
    sq_flat = by_class(c["square"][:3])
    square = [open_part * (sq_flat + c["square"][3] * face_sum[a] + c["square"][4] * edge_square[a]) for a in range(3)]
    cross = [(c["mixed"][0] * open_part) * mixed[e] for e in range(3)]
    keep_sum = 0.6 * blocking - 0.1
    keep_diff = -0.1 - 0.4 * blocking
    out = [None] * 19
    out[0] = (2.0 * keep_sum) * rest + even
    for a, (i, j) in enumerate(FACES):
        half = keep_sum * face_sum[a] + (even + square[a])
        tilt = keep_diff * face_diff[a] + momentum[a]
        out[i], out[j] = half + tilt, half - tilt
    for e, (dims, same, cross_pair) in enumerate(EDGES):
        p, q = dims
        level = even + square[p] + square[q]
        half = keep_sum * edge[e][0] + (level + cross[e])
        tilt = keep_diff * edge[e][1] + (momentum[p] + momentum[q])
        out[same[0]], out[same[1]] = half + tilt, half - tilt
        half = keep_sum * edge[e][2] + (level - cross[e])
        tilt = keep_diff * edge[e][3] + (momentum[p] - momentum[q])
        out[cross_pair[0]], out[cross_pair[1]] = half + tilt, half - tilt
    sums = list(face_sum) + [s for e in edge for s in (e[0], e[2])]
    diffs = list(face_diff) + [d for e in edge for d in (e[1], e[3])]
    return out, [rest] + sums + diffs


def slot(sign):
    return 0 if sign == 1 else 1


def member_at(velocity):
    return VELOCITY.index(velocity)


BODY = 8


def kernel(
    mesh_sizes,
    extent,
    primal,
    adjoint,
    porosity,
    solid,
    out_adjoint,
    out_grad,
    out_drag,
    level_two,
    level_one,
    states,
    porous,
    marks,
    block,
    terms,
    sums,
    face_send,
    rows_send,
    columns_send,
    face_recv,
    rows_recv,
    columns_recv,
    rows_edge,
    columns_edge,
    drag_row,
    drag_slots,
    meter,
    load_sem,
    send_sem,
    recv_sem,
    drag_sem,
):
    sx, sy, sz = mesh_sizes
    nx, ny, nz = extent
    halves = ny // 8
    body = pl.ds(BODY, ny)
    inner = tuple(range(1, nx - 1))
    outer = (0, nx - 1)
    me = (lax.axis_index("gx"), lax.axis_index("gy"), lax.axis_index("gz"))
    loads = [
        pltpu.make_async_copy(adjoint, level_two.at[:, :, body, :], load_sem.at[0]),
        pltpu.make_async_copy(primal, states, load_sem.at[1]),
        pltpu.make_async_copy(porosity, porous, load_sem.at[2]),
        pltpu.make_async_copy(solid, marks, load_sem.at[3]),
    ]
    for load in loads:
        load.start()

    stepped = tuple(
        {
            0: me[d],
            1: jnp.where(me[d] == mesh_sizes[d] - 1, 0, me[d] + 1),
            -1: jnp.where(me[d] == 0, mesh_sizes[d] - 1, me[d] - 1),
        }
        for d in range(3)
    )

    def shifted(offset):
        return tuple(stepped[d][offset[d]] for d in range(3))

    faces = [tuple(s if d == dim else 0 for d in range(3)) for dim in range(3) for s in (1, -1)]
    edges = [
        tuple(s if d == p else t if d == q else 0 for d in range(3))
        for p, q in ((0, 2), (1, 2), (0, 1))
        for s in (1, -1)
        for t in (1, -1)
    ]
    around = edges + faces
    near_part = [d for d in around if not d[0]]
    side_part = [d for d in around if d[0]]

    pair, core = me[0] // 2, me[0] % 2
    pairs = sx // 2
    first_group = [(c, z) for c in range(2) for z in range(sz) if (c, z) != (0, 0)]
    second_group = [(h, y) for h in range(pairs) for y in range(sy) if (h, y) != (0, 0)]

    def first_partner(c, z):
        return (pair * 2 + lax.rem(core + c, 2), me[1], lax.rem(me[2] + z, sz))

    def second_partner(h, y):
        return (lax.rem(pair + h, pairs) * 2 + core, lax.rem(me[1] + y, sy), me[2])

    barrier = pltpu.get_barrier_semaphore()
    targets = [first_partner(c, z) for c, z in first_group if (c, z) not in ((0, 1), (0, sz - 1))]
    targets += [second_partner(h, y) for h, y in second_group if (h, y) not in ((0, 1), (0, sy - 1))]
    targets += [shifted(offset) for offset in around]
    for target in targets:
        pl.semaphore_signal(barrier, inc=1, device_id=target, device_id_type=MESH)

    for sign in (1, -1):
        for k, i in enumerate(ALONG[0][sign]):
            source = adjoint.at[i, 0 if sign == 1 else nx - 1]
            pltpu.make_async_copy(source, face_send.at[0, slot(sign), k], load_sem.at[4]).start()

    lane = lax.broadcasted_iota(jnp.int32, (8, nz), 1)

    def pack(step, cells, planes, again):
        for sign in (1, -1):
            at = slot(sign)
            for h in range(halves):
                rows = slice(8 * h, 8 * h + 8)
                packed = columns_send[step, at, rows, :] if again else jnp.zeros((8, nz), F32)
                for k, i in enumerate(ALONG[2][sign]):
                    for x in planes:
                        spot = k * nx + x
                        column = cells[i, x, BODY + 8 * h : BODY + 8 * h + 8, :]
                        turn = (spot if sign == 1 else spot + 1) % nz
                        column = pltpu.roll(column, turn, 1) if turn else column
                        packed = jnp.where(lane == spot, column, packed)
                columns_send[step, at, rows, :] = packed
            edge_row = BODY if sign == 1 else BODY + ny - 1
            for k, i in enumerate(ALONG[1][sign]):
                for x in planes:
                    rows_send[step, at, k * nx + x : k * nx + x + 1, :] = cells[i, x, edge_row : edge_row + 1, :]

    def message(step, direction):
        dx, dy, dz = direction
        if dx and not dy and not dz:
            source = face_send.at[step, slot(dx)]
            target = face_recv.at[step, slot(dx), :, body, :]
            tiles = 5 * halves
        elif dy and not dx and not dz:
            source = rows_send.at[step, slot(dy)]
            target = rows_recv.at[step, slot(dy)]
            tiles = rows_send.shape[2] // 8
        elif dz and not dx and not dy:
            source = columns_send.at[step, slot(dz)]
            target = columns_recv.at[step, slot(dz), body, :]
            tiles = halves
        elif not dz:
            source = rows_send.at[step, slot(dy), pl.ds(xy_row(dx, dy) // 8 * 8, 8), :]
            target = rows_edge.at[step, slot(dx) * 2 + slot(dy)]
            tiles = 1
        elif not dy:
            source = columns_send.at[step, slot(dz)]
            target = columns_edge.at[step, slot(dx) * 2 + slot(dz)]
            tiles = halves
        else:
            near, far = (0, BODY + ny) if dy == 1 else (ny - 8, BODY - 8)
            source = columns_send.at[step, slot(dz), pl.ds(near, 8), :]
            target = columns_recv.at[step, slot(dz), pl.ds(far, 8), :]
            tiles = 1
        copy = pltpu.make_async_remote_copy(
            src_ref=source,
            dst_ref=target,
            send_sem=send_sem.at[0],
            recv_sem=recv_sem.at[step, 1 if dx else 0],
            device_id=shifted(tuple(-d for d in direction)),
            device_id_type=MESH,
        )
        return copy, tiles

    def send(step, directions):
        total = 0
        for direction in directions:
            copy, tiles = message(step, direction)
            copy.start()
            total += tiles
        return total

    def await_tiles(tiles, semaphore):
        whole = meter.at[pl.ds(0, tiles)]
        pltpu.make_async_copy(whole, whole, semaphore).wait()

    def xy_row(dx, dy):
        k = ALONG[1][dy].index(member_at((dx, dy, 0)))
        return k * nx + (0 if dx == 1 else nx - 1)

    def halo_row(sign):
        return BODY + ny if sign == 1 else BODY - 1

    def insert_rows(step, cells):
        for sign in (1, -1):
            row = halo_row(sign)
            for k, i in enumerate(ALONG[1][sign]):
                for x in range(nx):
                    if 0 <= x - VELOCITY[i][0] < nx:
                        got = rows_recv[step, slot(sign), k * nx + x : k * nx + x + 1, :]
                        cells[i, x, row : row + 1, :] = got

    def insert_edges(step):
        for dx in (1, -1):
            for dy in (1, -1):
                k = ALONG[0][dx].index(member_at((dx, dy, 0)))
                r = xy_row(dx, dy) % 8
                row = halo_row(dy)
                face_recv[step, slot(dx), k, row : row + 1, :] = rows_edge[step, slot(dx) * 2 + slot(dy), r : r + 1, :]

    def read_cells(step, cells, x, h):
        read = []
        for i, (dx, dy, dz) in enumerate(VELOCITY):
            from_x = x + dx
            outside = not 0 <= from_x < nx
            rows = slice(BODY + 8 * h + dy, BODY + 8 * h + dy + 8)
            if outside:
                value = face_recv[step, slot(dx), ALONG[0][dx].index(i), rows, :]
            else:
                value = cells[i, from_x, rows, :]
            if dz:
                spot = ALONG[2][dz].index(i) * nx + from_x % nx
                if outside:
                    column = columns_edge[step, slot(dx) * 2 + slot(dz), 8 * h : 8 * h + 8, :]
                else:
                    column = columns_recv[step, slot(dz), rows, :]
                last = nz - 1 if dz == 1 else 0
                turn = (last - spot) % nz
                column = pltpu.roll(column, turn, 1) if turn else column
                value = jnp.where(lane == last, column, pltpu.roll(value, nz - 1 if dz == 1 else 1, 1))
            read.append(value)
        return read

    def level(step, cells, x, h):
        rows = slice(8 * h, 8 * h + 8)
        read = read_cells(step, cells, x, h)
        vel = [terms[step, a, x, rows, :] for a in range(3)]
        return pull_back(read, vel, block[x, rows, :])

    def gradient(step, weighed, x, rows):
        total = weighed[0] * terms[step, 3, x, rows, :]
        for j in range(1, 19):
            total = total + weighed[j] * terms[step, 3 + j, x, rows, :]
        return total

    loads[0].wait()
    pack(0, level_two, range(nx), False)
    for load in loads[1:]:
        load.wait()
    total = jnp.zeros((8, nz), F32)
    for x in range(nx):
        for h in range(halves):
            rows = slice(8 * h, 8 * h + 8)
            closed = jnp.where(marks[x, rows, :] == 0, porous[x, rows, :], 1.0)
            block[x, rows, :] = closed
            flux = None
            for t in range(2):
                gain = sum(states[t, i, x, rows, :] for i in ALONG[0][1])
                loss = sum(states[t, i, x, rows, :] for i in ALONG[0][-1])
                flux = gain - loss if flux is None else flux + (gain - loss)
            out_grad[x, rows, :] = flux
            total = total + closed * flux
    drag_row[0] = jnp.sum(total, axis=0, keepdims=True)
    faces_in = face_send.at[0]
    pltpu.make_async_copy(faces_in, faces_in, load_sem.at[4]).wait()

    pl.semaphore_wait(barrier, len(targets))

    sent = send(0, around)
    near_tiles = sum(message_tiles(d, nx, halves) for d in near_part)
    side_tiles = sum(message_tiles(d, nx, halves) for d in side_part)

    mine_first = core * sz + me[2]
    mine_second = pair * sy + me[1]
    drag_first = drag_slots.at[pl.ds(0, 2 * sz)]
    drag_second = drag_slots.at[pl.ds(2 * sz, pairs * sy)]

    def drag_send(stage, target, mine, group, partner):
        target[mine] = drag_row[stage]
        for offset in group:
            pltpu.make_async_remote_copy(
                src_ref=drag_row.at[stage],
                dst_ref=target.at[mine],
                send_sem=drag_sem.at[2],
                recv_sem=drag_sem.at[stage],
                device_id=partner(*offset),
                device_id_type=MESH,
            ).start()

    def await_rows(target, count, semaphore):
        whole = target.at[pl.ds(0, count)]
        pltpu.make_async_copy(whole, whole, semaphore).wait()

    drag_send(0, drag_first, mine_first, first_group, first_partner)

    for step, t in ((0, 1), (1, 0)):
        for x in range(nx):
            for h in range(halves):
                rows = slice(8 * h, 8 * h + 8)
                vel, _, weights = primal_terms([states[t, i, x, rows, :] for i in range(19)])
                for j, value in enumerate(vel + weights):
                    terms[step, j, x, rows, :] = value

    def first_level(x):
        for h in range(halves):
            fresh, weighed = level(0, level_two, x, h)
            rows = slice(8 * h, 8 * h + 8)
            for i in range(19):
                level_one[i, x, BODY + 8 * h : BODY + 8 * h + 8, :] = fresh[i]
                sums[i, x, rows, :] = weighed[i]
            for sign, near in ((1, 0), (-1, nx - 1)):
                if x == near:
                    for k, i in enumerate(ALONG[0][sign]):
                        face_send[1, slot(sign), k, rows, :] = fresh[i]

    await_tiles(near_tiles, recv_sem.at[0, 0])
    insert_rows(0, level_two)
    for x in inner:
        first_level(x)
    pack(1, level_one, inner, False)
    await_tiles(side_tiles, recv_sem.at[0, 1])
    insert_edges(0)
    for x in outer:
        first_level(x)
    pack(1, level_one, outer, True)
    sent += send(1, around)

    await_rows(drag_first, len(first_group), drag_sem.at[0])
    drag_row[1] = jnp.sum(drag_first[...], axis=0)
    drag_send(1, drag_second, mine_second, second_group, second_partner)

    for x in range(nx):
        for h in range(halves):
            rows = slice(8 * h, 8 * h + 8)
            weighed = [sums[j, x, rows, :] for j in range(19)]
            out_grad[x, rows, :] = out_grad[x, rows, :] + gradient(0, weighed, x, rows)

    def second_level(x):
        for h in range(halves):
            rows = slice(8 * h, 8 * h + 8)
            fresh, weighed = level(1, level_one, x, h)
            for i in range(19):
                out_adjoint[i, x, rows, :] = fresh[i]
            total = out_grad[x, rows, :] + gradient(1, weighed, x, rows)
            out_grad[x, rows, :] = jnp.where(marks[x, rows, :] == 0, total, 0.0)

    await_tiles(near_tiles, recv_sem.at[1, 0])
    insert_rows(1, level_one)
    for x in inner:
        second_level(x)
    await_tiles(side_tiles, recv_sem.at[1, 1])
    insert_edges(1)
    for x in outer:
        second_level(x)

    await_rows(drag_second, len(second_group), drag_sem.at[1])
    everyone = jnp.sum(drag_second[...], axis=0)
    cells_in_all = nx * ny * nz * sx * sy * sz
    out_drag[...] = jnp.broadcast_to(everyone * (1.0 / cells_in_all), (8, nz))

    await_tiles(sent, send_sem.at[0])
    await_rows(drag_slots, len(first_group) + len(second_group), drag_sem.at[2])


def message_tiles(direction, nx, halves):
    dx, dy, dz = (d != 0 for d in direction)
    if dx and not dy and not dz:
        return 5 * halves
    if dy and not dx and not dz:
        return -(-5 * nx // 8)
    return halves if dz and not dy else 1


def put_out(adjoint, gradient, drag, out_adjoint, out_gradient, out_drag, sem):
    copies = [
        pltpu.make_async_copy(adjoint, out_adjoint, sem.at[0]),
        pltpu.make_async_copy(gradient, out_gradient, sem.at[1]),
    ]
    for copy in copies:
        copy.start()
    out_drag[...] = jnp.sum(drag[0:1, :], axis=1, keepdims=True)
    for copy in copies:
        copy.wait()


def solution(mesh):
    sizes = tuple(mesh.shape[name] for name in ("gx", "gy", "gz"))

    def body(primal_states, adjoint_last, porosity, solid_mask):
        nx, ny, nz = porosity.shape
        padded = ny + 16
        row_tiles = -(-5 * nx // 8) * 8
        hbm = pl.BlockSpec(memory_space=pltpu.HBM)
        vmem = pl.BlockSpec(memory_space=pltpu.VMEM)
        arguments = [
            pltpu.with_memory_space_constraint(v, pltpu.HBM)
            for v in (primal_states, adjoint_last, porosity, solid_mask)
        ]
        results = pl.pallas_call(
            functools.partial(kernel, sizes, (nx, ny, nz)),
            name="adjoint_window",
            out_shape=(
                pltpu.VMEM((19, nx, ny, nz), F32),
                pltpu.VMEM((nx, ny, nz), F32),
                pltpu.VMEM((8, nz), F32),
            ),
            in_specs=[hbm] * 4,
            out_specs=(vmem, vmem, vmem),
            scratch_shapes=[
                pltpu.VMEM((19, nx, padded, nz), F32),
                pltpu.VMEM((19, nx, padded, nz), F32),
                pltpu.VMEM((2, 19, nx, ny, nz), F32),
                pltpu.VMEM((nx, ny, nz), F32),
                pltpu.VMEM((nx, ny, nz), jnp.int32),
                pltpu.VMEM((nx, ny, nz), F32),
                pltpu.VMEM((2, 22, nx, ny, nz), F32),
                pltpu.VMEM((19, nx, ny, nz), F32),
                pltpu.VMEM((2, 2, 5, ny, nz), F32),
                pltpu.VMEM((2, 2, row_tiles, nz), F32),
                pltpu.VMEM((2, 2, ny, nz), F32),
                pltpu.VMEM((2, 2, 5, padded, nz), F32),
                pltpu.VMEM((2, 2, row_tiles, nz), F32),
                pltpu.VMEM((2, 2, padded, nz), F32),
                pltpu.VMEM((2, 4, 8, nz), F32),
                pltpu.VMEM((2, 4, ny, nz), F32),
                pltpu.VMEM((2, 1, nz), F32),
                pltpu.VMEM((2 * sizes[2] + sizes[0] // 2 * sizes[1], 1, nz), F32),
                pltpu.VMEM((128, 8, nz), F32),
                pltpu.SemaphoreType.DMA((5,)),
                pltpu.SemaphoreType.DMA((1,)),
                pltpu.SemaphoreType.DMA((2, 2)),
                pltpu.SemaphoreType.DMA((3,)),
            ],
            compiler_params=pltpu.CompilerParams(
                collective_id=0, has_side_effects=True, vmem_limit_bytes=16 << 20
            ),
        )(*arguments)
        adjoint, gradient, drag = pl.pallas_call(
            put_out,
            name="put_out",
            out_shape=(
                jax.ShapeDtypeStruct((19, nx, ny, nz), F32),
                jax.ShapeDtypeStruct((nx, ny, nz), F32),
                jax.ShapeDtypeStruct((1, 1), F32),
            ),
            in_specs=[vmem] * 3,
            out_specs=(hbm, hbm, vmem),
            scratch_shapes=[pltpu.SemaphoreType.DMA((2,))],
            compiler_params=pltpu.CompilerParams(vmem_limit_bytes=1 << 20),
        )(*results)
        return adjoint, gradient, drag.reshape(())

    return jax.shard_map(
        body,
        mesh=mesh,
        in_specs=(
            P(None, None, "gx", "gy", "gz"),
            P(None, "gx", "gy", "gz"),
            P("gx", "gy", "gz"),
            P("gx", "gy", "gz"),
        ),
        out_specs=(P(None, "gx", "gy", "gz"), P("gx", "gy", "gz"), P()),
        check_vma=False,
    )
```

```python
import functools

import jax
import jax.numpy as jnp
import numpy as np
from jax import lax
from jax.experimental import pallas as pl
from jax.experimental.pallas import tpu as pltpu
from jax.sharding import PartitionSpec as P

MESH = pl.DeviceIdType.MESH
F32 = jnp.float32

VELOCITY = (
    (0, 0, 0),
    (1, 0, 0),
    (-1, 0, 0),
    (0, 1, 0),
    (0, -1, 0),
    (0, 0, 1),
    (0, 0, -1),
    (1, 1, 0),
    (-1, -1, 0),
    (1, -1, 0),
    (-1, 1, 0),
    (1, 0, 1),
    (-1, 0, -1),
    (1, 0, -1),
    (-1, 0, 1),
    (0, 1, 1),
    (0, -1, -1),
    (0, 1, -1),
    (0, -1, 1),
)
ALONG = tuple(
    {sign: tuple(i for i in range(19) if VELOCITY[i][dim] == sign) for sign in (1, -1)} for dim in range(3)
)
FACES = ((1, 2), (3, 4), (5, 6))
EDGES = (((0, 1), (7, 8), (9, 10)), ((0, 2), (11, 12), (13, 14)), ((1, 2), (15, 16), (17, 18)))


def orthonormal_rows(monomials):
    rows = []
    for column in range(monomials.shape[1]):
        vector = monomials[:, column] * 1.0
        for sweep in range(2):
            for earlier in rows:
                vector = vector - np.dot(earlier, vector) * earlier
        vector = vector / np.sqrt(np.dot(vector, vector))
        rows.append(vector)
    return np.stack(rows)


def coefficients():
    vel = np.array(VELOCITY) * 1.0
    speeds = np.sum(np.abs(vel), axis=1)
    weights = np.where(speeds == 0, 1.0 / 3.0, np.where(speeds == 1, 1.0 / 18.0, 1.0 / 36.0))
    x, y, z = vel[:, 0], vel[:, 1], vel[:, 2]
    columns = [np.ones(19), x, y, z, x * x, y * y, z * z, x * y, x * z, y * z]
    columns += [x * y * y, x * z * z, y * x * x, y * z * z, z * x * x, z * y * y]
    columns += [x * x * y * y, x * x * z * z, y * y * z * z]
    basis = orthonormal_rows(np.stack(columns, axis=1))
    rates = np.array([0.0] * 4 + [1.6] * 6 + [1.2] * 9)
    relax = basis.T @ np.diag(rates) @ basis
    kept = 1.2 * np.eye(19) - relax
    scalar = relax @ weights
    square = relax @ (weights * x * x)
    first = relax @ (weights * x)
    face = (kept[1] + kept[2]) / 2 - kept[0]
    return dict(
        s0=(scalar[0], scalar[1], scalar[7]),
        s1=(first[1], first[7]),
        s2=(square[0], square[3], square[15], square[1] - square[3], square[7] - square[15]),
        s2_mixed=(relax @ (weights * x * y))[7],
        even=(kept[0][0], kept[0][1], kept[0][7]),
        odd=kept[1][1] / 2 - kept[1][2] / 2,
        square=(face[0], face[3], face[15], face[1] - face[3], face[7] - face[15]),
        mixed=(kept[7][7] + kept[8][7] - kept[9][7] - kept[10][7]) / 4,
    )


COEF = {name: tuple(np.asarray(v, np.float64).reshape(-1).tolist()) for name, v in coefficients().items()}


def pair_sums(members):
    face_sum = [members[a] + members[b] for a, b in FACES]
    face_diff = [members[a] - members[b] for a, b in FACES]
    edge = []
    for dims, (a, b), (c, d) in EDGES:
        edge.append((members[a] + members[b], members[a] - members[b], members[c] + members[d], members[c] - members[d]))
    plane = [e[0] + e[2] for e in edge]
    mixed = [e[0] - e[2] for e in edge]
    lean = [(e[1] + e[3], e[1] - e[3]) for e in edge]
    edge_square = [plane[0] + plane[1], plane[0] + plane[2], plane[1] + plane[2]]
    edge_diff = [lean[0][0] + lean[1][0], lean[0][1] + lean[2][0], lean[1][1] + lean[2][1]]
    face_total = face_sum[0] + face_sum[1] + face_sum[2]
    edge_total = plane[0] + plane[1] + plane[2]
    return face_sum, face_diff, edge, mixed, edge_square, edge_diff, face_total, edge_total


def primal_terms(state):
    face_sum, face_diff, edge, mixed, edge_square, edge_diff, face_total, edge_total = pair_sums(state)
    rho = state[0] + face_total + edge_total
    inverse = 1.0 / rho
    flux = [face_diff[a] + edge_diff[a] for a in range(3)]
    vel = [flux[a] * inverse for a in range(3)]
    third = rho * (1.0 / 3.0)
    press = [face_sum[a] + edge_square[a] - third - flux[a] * vel[a] for a in range(3)]
    total = press[0] + press[1] + press[2]
    centre = total * (2.0 / 21.0)
    stress = [0.4 * (press[a] * (1.0 / 6.0) + centre) for a in range(3)]
    shear = [0.1 * (mixed[e] - flux[dims[0]] * vel[dims[1]]) for e, (dims, _, _) in enumerate(EDGES)]
    flat = (stress[0] + stress[1] + stress[2]) * (-10.0 / 19.0)
    usq = vel[0] * vel[0] + vel[1] * vel[1] + vel[2] * vel[2]
    still = rho * (1.0 - 1.5 * usq)
    rest = 1.2 * state[0] + flat - 0.4 * still
    even, odd = [], []
    for a in range(3):
        feq_even = still + (4.5 * flux[a]) * vel[a]
        even.append(0.6 * face_sum[a] + (flat + stress[a]) - (1.2 / 18.0) * feq_even)
        odd.append(-0.4 * face_diff[a] - (3.6 / 18.0) * flux[a])
    for e, (dims, _, _) in enumerate(EDGES):
        p, q = dims
        bend = flat + stress[p] + stress[q]
        for sign, total_pair, diff_pair in ((1, edge[e][0], edge[e][1]), (-1, edge[e][2], edge[e][3])):
            along_flux = flux[p] + flux[q] if sign == 1 else flux[p] - flux[q]
            along_vel = vel[p] + vel[q] if sign == 1 else vel[p] - vel[q]
            feq_even = still + (4.5 * along_flux) * along_vel
            twist = bend + shear[e] if sign == 1 else bend - shear[e]
            even.append(0.6 * total_pair + twist - (1.2 / 36.0) * feq_even)
            odd.append(-0.4 * diff_pair - (3.6 / 36.0) * along_flux)
    return vel, flux[0], [rest] + even + odd


FACTORS = 6


def blocking_factors(blocking):
    open_part = 1.0 - blocking
    return [
        blocking,
        open_part,
        COEF["square"][3] * open_part,
        COEF["mixed"][0] * open_part,
        0.6 * blocking - 0.1,
        -0.1 - 0.4 * blocking,
    ]


def pull_back(read, vel, factors):
    c = COEF
    blocking, open_part, open_square, open_mixed, keep_sum, keep_diff = factors
    face_sum, face_diff, edge, mixed, edge_square, edge_diff, face_total, edge_total = pair_sums(read)
    rest = read[0]
    twice = face_total + 2.0 * edge_total
    count = rest + (face_total + edge_total)

    def by_class(f):
        return f[0] * count + (f[1] - f[0]) * twice

    s0 = c["s0"][0] * rest + c["s0"][1] * face_total + c["s0"][2] * edge_total
    s2_flat = by_class([9.0 * f for f in c["s2"][:3]])
    s2 = [s2_flat + (9.0 * c["s2"][3]) * face_sum[a] + (9.0 * c["s2"][4]) * edge_square[a] for a in range(3)]
    xy, xz, yz = [(9.0 * c["s2_mixed"][0]) * mixed[e] for e in range(3)]
    s0_thrice = 3.0 * s0
    bend = [
        (s2[0] - s0_thrice) * vel[0] + xy * vel[1] + xz * vel[2],
        xy * vel[0] + (s2[1] - s0_thrice) * vel[1] + yz * vel[2],
        xz * vel[0] + yz * vel[1] + (s2[2] - s0_thrice) * vel[2],
    ]
    density = s0 - 0.5 * (vel[0] * bend[0] + vel[1] * bend[1] + vel[2] * bend[2])
    by_face, by_edge = c["odd"][0] + 3.0 * c["s1"][0], c["odd"][0] + 3.0 * c["s1"][1]
    momentum = [open_part * (by_face * face_diff[a] + by_edge * edge_diff[a] + bend[a]) for a in range(3)]
    momentum[0] = momentum[0] + blocking
    even = open_part * (by_class(c["even"]) + density)
    flat = open_part * by_class(c["square"][:3])
    square = [open_square * (face_sum[a] + edge_square[a]) for a in range(3)]
    cross = [open_mixed * mixed[e] for e in range(3)]
    at_face = even + flat
    at_edge = at_face + flat
    out = [None] * 19
    out[0] = (keep_sum + keep_sum) * rest + even
    for a, (i, j) in enumerate(FACES):
        half = keep_sum * face_sum[a] + (at_face + square[a])
        tilt = keep_diff * face_diff[a] + momentum[a]
        out[i], out[j] = half + tilt, half - tilt
    for e, (dims, same, cross_pair) in enumerate(EDGES):
        p, q = dims
        level = at_edge + (square[p] + square[q])
        half = keep_sum * edge[e][0] + (level + cross[e])
        tilt = keep_diff * edge[e][1] + (momentum[p] + momentum[q])
        out[same[0]], out[same[1]] = half + tilt, half - tilt
        half = keep_sum * edge[e][2] + (level - cross[e])
        tilt = keep_diff * edge[e][3] + (momentum[p] - momentum[q])
        out[cross_pair[0]], out[cross_pair[1]] = half + tilt, half - tilt
    sums = list(face_sum) + [s for e in edge for s in (e[0], e[2])]
    diffs = list(face_diff) + [d for e in edge for d in (e[1], e[3])]
    return out, [rest] + sums + diffs


def slot(sign):
    return 0 if sign == 1 else 1


def read_cells(cells, face, columns, corner, extent, x, h):
    nx, ny, nz = extent
    lane = lax.broadcasted_iota(jnp.int32, (8, nz), 1)
    read = []
    for i, (dx, dy, dz) in enumerate(VELOCITY):
        from_x = x + dx
        outside = not 0 <= from_x < nx
        rows = slice(BODY + 8 * h + dy, BODY + 8 * h + dy + 8)
        if outside:
            value = face[slot(dx), ALONG[0][dx].index(i), rows, :]
        else:
            value = cells[i, from_x, rows, :]
        if dz:
            last = nz - 1 if dz == 1 else 0
            if outside:
                column = corner[slot(dx) * 2 + slot(dz)]
                turn = (last - h) % nz
            else:
                column = columns[slot(dz), rows, :]
                turn = (last - ALONG[2][dz].index(i) * nx - from_x) % nz
            column = pltpu.roll(column, turn, 1) if turn else column
            value = jnp.where(lane == last, column, pltpu.roll(value, nz - 1 if dz == 1 else 1, 1))
        read.append(value)
    return read


def one_level(cells, face, columns, corner, terms, factors, extent, x, h):
    rows = slice(8 * h, 8 * h + 8)
    read = read_cells(cells, face, columns, corner, extent, x, h)
    vel = [terms[a, x, rows, :] for a in range(3)]
    return pull_back(read, vel, [factors[j, x, rows, :] for j in range(FACTORS)])


def weigh(terms, weighed, x, rows):
    total = weighed[0] * terms[3, x, rows, :]
    for j in range(1, 19):
        total = total + weighed[j] * terms[3 + j, x, rows, :]
    return total


def member_at(velocity):
    return VELOCITY.index(velocity)


BODY = 8


def kernel(
    mesh_sizes,
    extent,
    primal,
    adjoint,
    porosity,
    solid,
    out_inner,
    out_grad,
    out_drag,
    level_one,
    marks,
    factors,
    terms_last,
    face_last,
    columns_last,
    corner_last,
    level_two,
    states,
    porous,
    terms_first,
    sums,
    face_send,
    rows_send,
    columns_send,
    xy_send,
    xz_send,
    yz_send,
    face_first,
    rows_recv,
    columns_first,
    xy_recv,
    corner_first,
    yz_recv,
    drag_row,
    drag_slots,
    meter,
    load_sem,
    send_sem,
    recv_sem,
    drag_sem,
):
    sx, sy, sz = mesh_sizes
    nx, ny, nz = extent
    halves = ny // 8
    terms = (terms_first, terms_last)
    face_recv = (face_first, face_last)
    columns_recv = (columns_first, columns_last)
    xz_recv = (corner_first, corner_last)
    body = pl.ds(BODY, ny)
    inner = tuple(range(1, nx - 1))
    outer = (0, nx - 1)
    me = (lax.axis_index("gx"), lax.axis_index("gy"), lax.axis_index("gz"))
    loads = [
        pltpu.make_async_copy(adjoint, level_two.at[:, :, body, :], load_sem.at[0]),
        pltpu.make_async_copy(primal, states, load_sem.at[1]),
        pltpu.make_async_copy(porosity, porous, load_sem.at[2]),
        pltpu.make_async_copy(solid, marks, load_sem.at[3]),
    ]
    for load in loads:
        load.start()

    stepped = tuple(
        {
            0: me[d],
            1: jnp.where(me[d] == mesh_sizes[d] - 1, 0, me[d] + 1),
            -1: jnp.where(me[d] == 0, mesh_sizes[d] - 1, me[d] - 1),
        }
        for d in range(3)
    )

    def shifted(offset):
        return tuple(stepped[d][offset[d]] for d in range(3))

    faces = [tuple(s if d == dim else 0 for d in range(3)) for dim in range(3) for s in (1, -1)]
    edges = [
        tuple(s if d == p else t if d == q else 0 for d in range(3))
        for p, q in ((0, 2), (1, 2), (0, 1))
        for s in (1, -1)
        for t in (1, -1)
    ]
    around = edges + faces
    near_part = [d for d in around if not d[0]]
    side_part = [d for d in around if d[0]]

    pair, core = me[0] // 2, me[0] % 2
    pairs = sx // 2
    first_group = [(c, z) for c in range(2) for z in range(sz) if (c, z) != (0, 0)]
    second_group = [(h, y) for h in range(pairs) for y in range(sy) if (h, y) != (0, 0)]

    def first_partner(c, z):
        return (pair * 2 + lax.rem(core + c, 2), me[1], lax.rem(me[2] + z, sz))

    def second_partner(h, y):
        return (lax.rem(pair + h, pairs) * 2 + core, lax.rem(me[1] + y, sy), me[2])

    barrier = pltpu.get_barrier_semaphore()
    far = [(z, 1, first_partner(c, z)) for c, z in first_group if (c, z) not in ((0, 1), (0, sz - 1))]
    far = [(min(z, sz - z), n, target) for z, n, target in far]
    for h, y in second_group:
        if (h, y) not in ((0, 1), (0, sy - 1)):
            far.append((2 * h + (min(y, sy - y) + 1) // 2, 2, second_partner(h, y)))
    for offset in around:
        far.append((2 * abs(offset[0]) + abs(offset[1]) + abs(offset[2]), 3, shifted(offset)))
    targets = [entry[2] for entry in sorted(far, key=lambda entry: -entry[0])]
    for target in targets:
        pl.semaphore_signal(barrier, inc=1, device_id=target, device_id_type=MESH)

    for sign in (1, -1):
        for k, i in enumerate(ALONG[0][sign]):
            source = adjoint.at[i, 0 if sign == 1 else nx - 1]
            pltpu.make_async_copy(source, face_send.at[0, slot(sign), k], load_sem.at[4]).start()

    lane = lax.broadcasted_iota(jnp.int32, (8, nz), 1)

    def pack(step, cells, planes, again):
        for sign in (1, -1):
            at = slot(sign)
            for h in range(halves):
                rows = slice(8 * h, 8 * h + 8)
                packed = columns_send[step, at, rows, :] if again else jnp.zeros((8, nz), F32)
                for k, i in enumerate(ALONG[2][sign]):
                    for x in planes:
                        spot = k * nx + x
                        column = cells[i, x, BODY + 8 * h : BODY + 8 * h + 8, :]
                        turn = (spot if sign == 1 else spot + 1) % nz
                        column = pltpu.roll(column, turn, 1) if turn else column
                        packed = jnp.where(lane == spot, column, packed)
                columns_send[step, at, rows, :] = packed
            edge_row = BODY if sign == 1 else BODY + ny - 1
            for k, i in enumerate(ALONG[1][sign]):
                for x in planes:
                    rows_send[step, at, k * nx + x : k * nx + x + 1, :] = cells[i, x, edge_row : edge_row + 1, :]

    def pack_edges(step, cells):
        for p in (1, -1):
            near = 0 if p == 1 else nx - 1
            for q in (1, -1):
                i = member_at((p, q, 0))
                row = BODY if q == 1 else BODY + ny - 1
                xy_send[step, slot(p) * 2 + slot(q)] = cells[i, near, row : row + 1, :]
                i = member_at((p, 0, q))
                packed = None
                for h in range(halves):
                    column = cells[i, near, BODY + 8 * h : BODY + 8 * h + 8, :]
                    turn = (h if q == 1 else h + 1) % nz
                    column = pltpu.roll(column, turn, 1) if turn else column
                    packed = column if packed is None else jnp.where(lane == h, column, packed)
                xz_send[step, slot(p) * 2 + slot(q)] = packed
                row = 0 if p == 1 else ny - 1
                yz_send[step, slot(p) * 2 + slot(q)] = columns_send[step, slot(q), row : row + 1, :]

    def message(step, direction):
        dx, dy, dz = direction
        if dx and not dy and not dz:
            source = face_send.at[step, slot(dx)]
            target = face_recv[step].at[slot(dx), :, body, :]
        elif dy and not dx and not dz:
            source = rows_send.at[step, slot(dy)]
            target = rows_recv.at[step, slot(dy)]
        elif dz and not dx and not dy:
            source = columns_send.at[step, slot(dz)]
            target = columns_recv[step].at[slot(dz), body, :]
        elif not dz:
            source = xy_send.at[step, slot(dx) * 2 + slot(dy)]
            target = xy_recv.at[step, slot(dx) * 2 + slot(dy)]
        elif not dy:
            source = xz_send.at[step, slot(dx) * 2 + slot(dz)]
            target = xz_recv[step].at[slot(dx) * 2 + slot(dz)]
        else:
            source = yz_send.at[step, slot(dy) * 2 + slot(dz)]
            target = yz_recv.at[step, slot(dy) * 2 + slot(dz)]
        copy = pltpu.make_async_remote_copy(
            src_ref=source,
            dst_ref=target,
            send_sem=send_sem.at[0],
            recv_sem=recv_sem.at[step, 1 if dx else 0],
            device_id=shifted(tuple(-d for d in direction)),
            device_id_type=MESH,
        )
        return copy

    def send(step, directions):
        for direction in directions:
            message(step, direction).start()

    def await_rows(rows, semaphore):
        whole = meter.at[pl.ds(0, rows)]
        pltpu.make_async_copy(whole, whole, semaphore).wait()

    def halo_row(sign):
        return BODY + ny if sign == 1 else BODY - 1

    def insert_rows(step, cells):
        for sign in (1, -1):
            row = halo_row(sign)
            for k, i in enumerate(ALONG[1][sign]):
                for x in range(nx):
                    if 0 <= x - VELOCITY[i][0] < nx:
                        got = rows_recv[step, slot(sign), k * nx + x : k * nx + x + 1, :]
                        cells[i, x, row : row + 1, :] = got
            for t in (1, -1):
                columns_recv[step][slot(t), row : row + 1, :] = yz_recv[step, slot(sign) * 2 + slot(t)]

    def insert_edges(step):
        for dx in (1, -1):
            for dy in (1, -1):
                k = ALONG[0][dx].index(member_at((dx, dy, 0)))
                row = halo_row(dy)
                face_recv[step][slot(dx), k, row : row + 1, :] = xy_recv[step, slot(dx) * 2 + slot(dy)]

    def level(step, cells, x, h):
        return one_level(cells, face_recv[step], columns_recv[step], xz_recv[step], terms[step], factors, extent, x, h)

    loads[0].wait()
    pack(0, level_two, range(nx), False)
    pack_edges(0, level_two)
    for load in loads[1:]:
        load.wait()
    total = jnp.zeros((8, nz), F32)
    for x in range(nx):
        for h in range(halves):
            rows = slice(8 * h, 8 * h + 8)
            closed = jnp.where(marks[x, rows, :] == 0, porous[x, rows, :], 1.0)
            for j, value in enumerate(blocking_factors(closed)):
                factors[j, x, rows, :] = value
            flux = None
            for t in range(2):
                gain = sum(states[t, i, x, rows, :] for i in ALONG[0][1])
                loss = sum(states[t, i, x, rows, :] for i in ALONG[0][-1])
                flux = gain - loss if flux is None else flux + (gain - loss)
            out_grad[x, rows, :] = flux
            total = total + closed * flux
    drag_row[0] = jnp.sum(total, axis=0, keepdims=True)
    faces_in = face_send.at[0]
    pltpu.make_async_copy(faces_in, faces_in, load_sem.at[4]).wait()

    pl.semaphore_wait(barrier, len(targets))

    send(0, around)
    near_rows = sum(message_rows(d, extent) for d in near_part)
    side_rows = sum(message_rows(d, extent) for d in side_part)

    mine_first = core * sz + me[2]
    mine_second = pair * sy + me[1]
    drag_first = drag_slots.at[pl.ds(0, 2 * sz)]
    drag_second = drag_slots.at[pl.ds(2 * sz, pairs * sy)]

    def drag_send(stage, target, mine, group, partner):
        target[mine] = drag_row[stage]
        for offset in group:
            pltpu.make_async_remote_copy(
                src_ref=drag_row.at[stage],
                dst_ref=target.at[mine],
                send_sem=drag_sem.at[2],
                recv_sem=drag_sem.at[stage],
                device_id=partner(*offset),
                device_id_type=MESH,
            ).start()

    drag_send(0, drag_first, mine_first, first_group, first_partner)

    for step, t in ((0, 1), (1, 0)):
        for x in range(nx):
            for h in range(halves):
                rows = slice(8 * h, 8 * h + 8)
                vel, _, weights = primal_terms([states[t, i, x, rows, :] for i in range(19)])
                for j, value in enumerate(vel + weights):
                    terms[step][j, x, rows, :] = value

    def first_level(x):
        for h in range(halves):
            fresh, weighed = level(0, level_two, x, h)
            rows = slice(8 * h, 8 * h + 8)
            for i in range(19):
                level_one[i, x, BODY + 8 * h : BODY + 8 * h + 8, :] = fresh[i]
                sums[i, x, rows, :] = weighed[i]
            for sign, near in ((1, 0), (-1, nx - 1)):
                if x == near:
                    for k, i in enumerate(ALONG[0][sign]):
                        face_send[1, slot(sign), k, rows, :] = fresh[i]

    await_rows(near_rows, recv_sem.at[0, 0])
    insert_rows(0, level_two)
    for x in inner:
        first_level(x)
    pack(1, level_one, inner, False)
    await_rows(side_rows, recv_sem.at[0, 1])
    insert_edges(0)
    for x in outer:
        first_level(x)
    pack(1, level_one, outer, True)
    pack_edges(1, level_one)
    send(1, around)

    await_rows(len(first_group), drag_sem.at[0])
    drag_row[1] = jnp.sum(drag_first[...], axis=0)
    drag_send(1, drag_second, mine_second, second_group, second_partner)

    for x in range(nx):
        for h in range(halves):
            rows = slice(8 * h, 8 * h + 8)
            weighed = [sums[j, x, rows, :] for j in range(19)]
            out_grad[x, rows, :] = out_grad[x, rows, :] + weigh(terms[0], weighed, x, rows)

    def second_level(x):
        for h in range(halves):
            rows = slice(8 * h, 8 * h + 8)
            fresh, weighed = level(1, level_one, x, h)
            for i in range(19):
                out_inner[i, x - 1, rows, :] = fresh[i]
            total = out_grad[x, rows, :] + weigh(terms[1], weighed, x, rows)
            out_grad[x, rows, :] = jnp.where(marks[x, rows, :] == 0, total, 0.0)

    await_rows(near_rows, recv_sem.at[1, 0])
    insert_rows(1, level_one)
    for x in inner:
        second_level(x)
    await_rows(side_rows, recv_sem.at[1, 1])
    insert_edges(1)

    await_rows(len(second_group), drag_sem.at[1])
    everyone = jnp.sum(drag_second[...], axis=0)
    cells_in_all = nx * ny * nz * sx * sy * sz
    out_drag[...] = jnp.broadcast_to(jnp.sum(everyone, axis=1, keepdims=True) * (1.0 / cells_in_all), (8, nz))

    await_rows(2 * (near_rows + side_rows), send_sem.at[0])
    await_rows(len(first_group) + len(second_group), drag_sem.at[2])


def message_rows(direction, extent):
    nx, ny, nz = extent
    dx, dy, dz = (d != 0 for d in direction)
    if dx + dy + dz == 1:
        return 5 * ny if dx else -(-5 * nx // 8) * 8 if dy else ny
    return 8 if dx and dz else 1


def finish(
    extent,
    inner,
    grad,
    drag,
    cells,
    marks,
    factors,
    terms,
    face,
    columns,
    corner,
    out_adjoint,
    out_grad,
    out_drag,
    outer,
    grad_whole,
    total,
    sem,
):
    nx, ny, nz = extent
    copies = [pltpu.make_async_copy(inner, out_adjoint.at[:, pl.ds(1, nx - 2)], sem.at[0])]
    copies[0].start()
    total[...] = drag[0:1, 0:1]
    copies.append(pltpu.make_async_copy(total, out_drag, sem.at[1]))
    copies[1].start()
    for n, x in enumerate((0, nx - 1)):
        for h in range(ny // 8):
            rows = slice(8 * h, 8 * h + 8)
            fresh, weighed = one_level(cells, face, columns, corner, terms, factors, extent, x, h)
            for i in range(19):
                outer[n, i, rows, :] = fresh[i]
            slope = grad[x, rows, :] + weigh(terms, weighed, x, rows)
            grad_whole[x, rows, :] = jnp.where(marks[x, rows, :] == 0, slope, 0.0)
        copies.append(pltpu.make_async_copy(outer.at[n], out_adjoint.at[:, x], sem.at[2 + n]))
        copies[-1].start()
    for x in range(1, nx - 1):
        grad_whole[x] = grad[x]
    copies.append(pltpu.make_async_copy(grad_whole, out_grad, sem.at[4]))
    copies[-1].start()
    for copy in copies:
        copy.wait()


def solution(mesh):
    sizes = tuple(mesh.shape[name] for name in ("gx", "gy", "gz"))

    def body(primal_states, adjoint_last, porosity, solid_mask):
        nx, ny, nz = porosity.shape
        padded = ny + 16
        row_tiles = -(-5 * nx // 8) * 8
        hbm = pl.BlockSpec(memory_space=pltpu.HBM)
        vmem = pl.BlockSpec(memory_space=pltpu.VMEM)
        arguments = [
            pltpu.with_memory_space_constraint(v, pltpu.HBM)
            for v in (primal_states, adjoint_last, porosity, solid_mask)
        ]
        results = pl.pallas_call(
            functools.partial(kernel, sizes, (nx, ny, nz)),
            name="adjoint_window",
            out_shape=(
                pltpu.VMEM((19, nx - 2, ny, nz), F32),
                pltpu.VMEM((nx, ny, nz), F32),
                pltpu.VMEM((8, nz), F32),
                pltpu.VMEM((19, nx, padded, nz), F32),
                pltpu.VMEM((nx, ny, nz), jnp.int32),
                pltpu.VMEM((FACTORS, nx, ny, nz), F32),
                pltpu.VMEM((22, nx, ny, nz), F32),
                pltpu.VMEM((2, 5, padded, nz), F32),
                pltpu.VMEM((2, padded, nz), F32),
                pltpu.VMEM((4, 8, nz), F32),
            ),
            in_specs=[hbm] * 4,
            out_specs=(vmem,) * 10,
            scratch_shapes=[
                pltpu.VMEM((19, nx, padded, nz), F32),
                pltpu.VMEM((2, 19, nx, ny, nz), F32),
                pltpu.VMEM((nx, ny, nz), F32),
                pltpu.VMEM((22, nx, ny, nz), F32),
                pltpu.VMEM((19, nx, ny, nz), F32),
                pltpu.VMEM((2, 2, 5, ny, nz), F32),
                pltpu.VMEM((2, 2, row_tiles, nz), F32),
                pltpu.VMEM((2, 2, ny, nz), F32),
                pltpu.VMEM((2, 4, 1, nz), F32),
                pltpu.VMEM((2, 4, 8, nz), F32),
                pltpu.VMEM((2, 4, 1, nz), F32),
                pltpu.VMEM((2, 5, padded, nz), F32),
                pltpu.VMEM((2, 2, row_tiles, nz), F32),
                pltpu.VMEM((2, padded, nz), F32),
                pltpu.VMEM((2, 4, 1, nz), F32),
                pltpu.VMEM((4, 8, nz), F32),
                pltpu.VMEM((2, 4, 1, nz), F32),
                pltpu.VMEM((2, 1, nz), F32),
                pltpu.VMEM((2 * sizes[2] + sizes[0] // 2 * sizes[1], 1, nz), F32),
                pltpu.VMEM((1024, 1, nz), F32),
                pltpu.SemaphoreType.DMA((5,)),
                pltpu.SemaphoreType.DMA((1,)),
                pltpu.SemaphoreType.DMA((2, 2)),
                pltpu.SemaphoreType.DMA((3,)),
            ],
            compiler_params=pltpu.CompilerParams(
                collective_id=0, has_side_effects=True, vmem_limit_bytes=16 << 20
            ),
        )(*arguments)
        adjoint, gradient, drag = pl.pallas_call(
            functools.partial(finish, (nx, ny, nz)),
            name="finish",
            out_shape=(
                jax.ShapeDtypeStruct((19, nx, ny, nz), F32),
                jax.ShapeDtypeStruct((nx, ny, nz), F32),
                jax.ShapeDtypeStruct((1, 1), F32),
            ),
            in_specs=[vmem] * 10,
            out_specs=(hbm, hbm, hbm),
            scratch_shapes=[
                pltpu.VMEM((2, 19, ny, nz), F32),
                pltpu.VMEM((nx, ny, nz), F32),
                pltpu.VMEM((1, 1), F32),
                pltpu.SemaphoreType.DMA((5,)),
            ],
            compiler_params=pltpu.CompilerParams(vmem_limit_bytes=2 << 20),
        )(*results)
        return adjoint, gradient, drag.reshape(())

    return jax.shard_map(
        body,
        mesh=mesh,
        in_specs=(
            P(None, None, "gx", "gy", "gz"),
            P(None, "gx", "gy", "gz"),
            P("gx", "gy", "gz"),
            P("gx", "gy", "gz"),
        ),
        out_specs=(P(None, "gx", "gy", "gz"), P("gx", "gy", "gz"), P()),
        check_vma=False,
    )
```

```python
import functools

import jax
import jax.numpy as jnp
import numpy as np
from jax import lax
from jax.experimental import pallas as pl
from jax.experimental.pallas import tpu as pltpu
from jax.sharding import PartitionSpec as P

MESH = pl.DeviceIdType.MESH
F32 = jnp.float32

VELOCITY = (
    (0, 0, 0),
    (1, 0, 0),
    (-1, 0, 0),
    (0, 1, 0),
    (0, -1, 0),
    (0, 0, 1),
    (0, 0, -1),
    (1, 1, 0),
    (-1, -1, 0),
    (1, -1, 0),
    (-1, 1, 0),
    (1, 0, 1),
    (-1, 0, -1),
    (1, 0, -1),
    (-1, 0, 1),
    (0, 1, 1),
    (0, -1, -1),
    (0, 1, -1),
    (0, -1, 1),
)
ALONG = tuple(
    {sign: tuple(i for i in range(19) if VELOCITY[i][dim] == sign) for sign in (1, -1)} for dim in range(3)
)
FACES = ((1, 2), (3, 4), (5, 6))
EDGES = (((0, 1), (7, 8), (9, 10)), ((0, 2), (11, 12), (13, 14)), ((1, 2), (15, 16), (17, 18)))


def orthonormal_rows(monomials):
    rows = []
    for column in range(monomials.shape[1]):
        vector = monomials[:, column] * 1.0
        for sweep in range(2):
            for earlier in rows:
                vector = vector - np.dot(earlier, vector) * earlier
        vector = vector / np.sqrt(np.dot(vector, vector))
        rows.append(vector)
    return np.stack(rows)


def coefficients():
    vel = np.array(VELOCITY) * 1.0
    speeds = np.sum(np.abs(vel), axis=1)
    weights = np.where(speeds == 0, 1.0 / 3.0, np.where(speeds == 1, 1.0 / 18.0, 1.0 / 36.0))
    x, y, z = vel[:, 0], vel[:, 1], vel[:, 2]
    columns = [np.ones(19), x, y, z, x * x, y * y, z * z, x * y, x * z, y * z]
    columns += [x * y * y, x * z * z, y * x * x, y * z * z, z * x * x, z * y * y]
    columns += [x * x * y * y, x * x * z * z, y * y * z * z]
    basis = orthonormal_rows(np.stack(columns, axis=1))
    rates = np.array([0.0] * 4 + [1.6] * 6 + [1.2] * 9)
    relax = basis.T @ np.diag(rates) @ basis
    kept = 1.2 * np.eye(19) - relax
    scalar = relax @ weights
    square = relax @ (weights * x * x)
    first = relax @ (weights * x)
    face = (kept[1] + kept[2]) / 2 - kept[0]
    return dict(
        s0=(scalar[0], scalar[1], scalar[7]),
        s1=(first[1], first[7]),
        s2=(square[0], square[3], square[15], square[1] - square[3], square[7] - square[15]),
        s2_mixed=(relax @ (weights * x * y))[7],
        even=(kept[0][0], kept[0][1], kept[0][7]),
        odd=kept[1][1] / 2 - kept[1][2] / 2,
        square=(face[0], face[3], face[15], face[1] - face[3], face[7] - face[15]),
        mixed=(kept[7][7] + kept[8][7] - kept[9][7] - kept[10][7]) / 4,
    )


COEF = {name: tuple(np.asarray(v, np.float64).reshape(-1).tolist()) for name, v in coefficients().items()}


def pair_sums(members):
    face_sum = [members[a] + members[b] for a, b in FACES]
    face_diff = [members[a] - members[b] for a, b in FACES]
    edge = []
    for dims, (a, b), (c, d) in EDGES:
        edge.append((members[a] + members[b], members[a] - members[b], members[c] + members[d], members[c] - members[d]))
    plane = [e[0] + e[2] for e in edge]
    mixed = [e[0] - e[2] for e in edge]
    lean = [(e[1] + e[3], e[1] - e[3]) for e in edge]
    edge_square = [plane[0] + plane[1], plane[0] + plane[2], plane[1] + plane[2]]
    edge_diff = [lean[0][0] + lean[1][0], lean[0][1] + lean[2][0], lean[1][1] + lean[2][1]]
    face_total = face_sum[0] + face_sum[1] + face_sum[2]
    edge_total = plane[0] + plane[1] + plane[2]
    return face_sum, face_diff, edge, mixed, edge_square, edge_diff, face_total, edge_total


def primal_terms(state):
    face_sum, face_diff, edge, mixed, edge_square, edge_diff, face_total, edge_total = pair_sums(state)
    rho = state[0] + face_total + edge_total
    inverse = 1.0 / rho
    flux = [face_diff[a] + edge_diff[a] for a in range(3)]
    vel = [flux[a] * inverse for a in range(3)]
    third = rho * (1.0 / 3.0)
    press = [face_sum[a] + edge_square[a] - third - flux[a] * vel[a] for a in range(3)]
    total = press[0] + press[1] + press[2]
    centre = total * (2.0 / 21.0)
    stress = [0.4 * (press[a] * (1.0 / 6.0) + centre) for a in range(3)]
    shear = [0.1 * (mixed[e] - flux[dims[0]] * vel[dims[1]]) for e, (dims, _, _) in enumerate(EDGES)]
    flat = (stress[0] + stress[1] + stress[2]) * (-10.0 / 19.0)
    usq = vel[0] * vel[0] + vel[1] * vel[1] + vel[2] * vel[2]
    still = rho * (1.0 - 1.5 * usq)
    rest = 1.2 * state[0] + flat - 0.4 * still
    even, odd = [], []
    for a in range(3):
        feq_even = still + (4.5 * flux[a]) * vel[a]
        even.append(0.6 * face_sum[a] + (flat + stress[a]) - (1.2 / 18.0) * feq_even)
        odd.append(-0.4 * face_diff[a] - (3.6 / 18.0) * flux[a])
    for e, (dims, _, _) in enumerate(EDGES):
        p, q = dims
        bend = flat + stress[p] + stress[q]
        for sign, total_pair, diff_pair in ((1, edge[e][0], edge[e][1]), (-1, edge[e][2], edge[e][3])):
            along_flux = flux[p] + flux[q] if sign == 1 else flux[p] - flux[q]
            along_vel = vel[p] + vel[q] if sign == 1 else vel[p] - vel[q]
            feq_even = still + (4.5 * along_flux) * along_vel
            twist = bend + shear[e] if sign == 1 else bend - shear[e]
            even.append(0.6 * total_pair + twist - (1.2 / 36.0) * feq_even)
            odd.append(-0.4 * diff_pair - (3.6 / 36.0) * along_flux)
    return vel, flux[0], [rest] + even + odd


class Nothing:
    def __add__(self, other):
        return other

    __radd__ = __add__

    def __sub__(self, other):
        return -other

    def __rsub__(self, other):
        return other

    def __mul__(self, other):
        return self

    __rmul__ = __mul__

    def __neg__(self):
        return self


FACTORS = 6


def blocking_factors(blocking):
    open_part = 1.0 - blocking
    return [
        blocking,
        open_part,
        COEF["square"][3] * open_part,
        COEF["mixed"][0] * open_part,
        0.6 * blocking - 0.1,
        -0.1 - 0.4 * blocking,
    ]


def pull_back(read, vel, factors, source=True):
    c = COEF
    blocking, open_part, open_square, open_mixed, keep_sum, keep_diff = factors
    face_sum, face_diff, edge, mixed, edge_square, edge_diff, face_total, edge_total = pair_sums(read)
    rest = read[0]
    twice = face_total + 2.0 * edge_total
    count = rest + (face_total + edge_total)

    def by_class(f):
        return f[0] * count + (f[1] - f[0]) * twice

    s0 = c["s0"][0] * rest + c["s0"][1] * face_total + c["s0"][2] * edge_total
    s2_flat = by_class([9.0 * f for f in c["s2"][:3]])
    s2 = [s2_flat + (9.0 * c["s2"][3]) * face_sum[a] + (9.0 * c["s2"][4]) * edge_square[a] for a in range(3)]
    xy, xz, yz = [(9.0 * c["s2_mixed"][0]) * mixed[e] for e in range(3)]
    s0_thrice = 3.0 * s0
    bend = [
        (s2[0] - s0_thrice) * vel[0] + xy * vel[1] + xz * vel[2],
        xy * vel[0] + (s2[1] - s0_thrice) * vel[1] + yz * vel[2],
        xz * vel[0] + yz * vel[1] + (s2[2] - s0_thrice) * vel[2],
    ]
    density = s0 - 0.5 * (vel[0] * bend[0] + vel[1] * bend[1] + vel[2] * bend[2])
    by_face, by_edge = c["odd"][0] + 3.0 * c["s1"][0], c["odd"][0] + 3.0 * c["s1"][1]
    momentum = [open_part * (by_face * face_diff[a] + by_edge * edge_diff[a] + bend[a]) for a in range(3)]
    if source:
        momentum[0] = momentum[0] + blocking
    even = open_part * (by_class(c["even"]) + density)
    flat = open_part * by_class(c["square"][:3])
    square = [open_square * (face_sum[a] + edge_square[a]) for a in range(3)]
    cross = [open_mixed * mixed[e] for e in range(3)]
    at_face = even + flat
    at_edge = at_face + flat
    out = [None] * 19
    out[0] = (keep_sum + keep_sum) * rest + even
    for a, (i, j) in enumerate(FACES):
        half = keep_sum * face_sum[a] + (at_face + square[a])
        tilt = keep_diff * face_diff[a] + momentum[a]
        out[i], out[j] = half + tilt, half - tilt
    for e, (dims, same, cross_pair) in enumerate(EDGES):
        p, q = dims
        level = at_edge + (square[p] + square[q])
        half = keep_sum * edge[e][0] + (level + cross[e])
        tilt = keep_diff * edge[e][1] + (momentum[p] + momentum[q])
        out[same[0]], out[same[1]] = half + tilt, half - tilt
        half = keep_sum * edge[e][2] + (level - cross[e])
        tilt = keep_diff * edge[e][3] + (momentum[p] - momentum[q])
        out[cross_pair[0]], out[cross_pair[1]] = half + tilt, half - tilt
    sums = list(face_sum) + [s for e in edge for s in (e[0], e[2])]
    diffs = list(face_diff) + [d for e in edge for d in (e[1], e[3])]
    return out, [rest] + sums + diffs


def slot(sign):
    return 0 if sign == 1 else 1


def read_cells(cells, face, columns, corner, extent, x, h):
    nx, ny, nz = extent
    lane = lax.broadcasted_iota(jnp.int32, (8, nz), 1)
    read = []
    for i, (dx, dy, dz) in enumerate(VELOCITY):
        from_x = x + dx
        outside = not 0 <= from_x < nx
        rows = slice(BODY + 8 * h + dy, BODY + 8 * h + dy + 8)
        if outside:
            value = face[slot(dx), ALONG[0][dx].index(i), rows, :]
        else:
            value = cells[i, from_x, rows, :]
        if dz:
            last = nz - 1 if dz == 1 else 0
            if outside:
                column = corner[slot(dx) * 2 + slot(dz)]
                turn = (last - h) % nz
            else:
                column = columns[slot(dz), rows, :]
                turn = (last - ALONG[2][dz].index(i) * nx - from_x) % nz
            column = pltpu.roll(column, turn, 1) if turn else column
            value = jnp.where(lane == last, column, pltpu.roll(value, nz - 1 if dz == 1 else 1, 1))
        read.append(value)
    return read


def one_level(cells, face, columns, corner, terms, factors, extent, x, h):
    rows = slice(8 * h, 8 * h + 8)
    read = read_cells(cells, face, columns, corner, extent, x, h)
    vel = [terms[a, x, rows, :] for a in range(3)]
    return pull_back(read, vel, [factors[j, x, rows, :] for j in range(FACTORS)])


def corner_members(dy):
    return ((member_at((0, dy, dy)), dy), (member_at((0, dy, -dy)), -dy))


def corner_tile(extent, dy):
    return (extent[1] // 8 - 1, 7) if dy == 1 else (0, 0)


def corner_change(got, extent, dy, x):
    nx, ny, nz = extent
    lane = lax.broadcasted_iota(jnp.int32, (8, nz), 1)
    row = lax.broadcasted_iota(jnp.int32, (8, nz), 0)
    change = jnp.zeros((8, nz), F32)
    for i, dz in corner_members(dy):
        last = nz - 1 if dz == 1 else 0
        turn = (last - ALONG[2][dz].index(i) * nx - x) % nz
        value = jnp.broadcast_to(got[slot(dy) * 2 + slot(dz)], (8, nz))
        value = pltpu.roll(value, turn, 1) if turn else value
        change = jnp.where(lane == last, value, change)
    return jnp.where(row == corner_tile(extent, dy)[1], change, 0.0)


def corner_response(terms, factors, extent, dy, x):
    nx, ny, nz = extent
    h, at = corner_tile(extent, dy)
    rows = slice(8 * h, 8 * h + 8)
    lane = lax.broadcasted_iota(jnp.int32, (8, nz), 1)
    row = lax.broadcasted_iota(jnp.int32, (8, nz), 0)
    read = [Nothing()] * 19
    for i, dz in corner_members(dy):
        read[i] = jnp.where((row == at) & (lane == (nz - 1 if dz == 1 else 0)), 1.0, 0.0)
    vel = [terms[a, x, rows, :] for a in range(3)]
    return pull_back(read, vel, [factors[j, x, rows, :] for j in range(FACTORS)], source=False)[0]


def corner_weight(terms, extent, dy, x):
    nx, ny, nz = extent
    h = corner_tile(extent, dy)[0]
    rows = slice(8 * h, 8 * h + 8)
    lane = lax.broadcasted_iota(jnp.int32, (8, nz), 1)
    even, odd = 3 + 1 + 3 + 4, 3 + 1 + 9 + 3 + 4
    same, cross = [
        terms[even + n, x, rows, :] + terms[odd + n, x, rows, :]
        if dy == 1
        else terms[even + n, x, rows, :] - terms[odd + n, x, rows, :]
        for n in range(2)
    ]
    return jnp.where(lane == (nz - 1 if dy == 1 else 0), same, cross)


def weigh(terms, weighed, x, rows):
    total = weighed[0] * terms[3, x, rows, :]
    for j in range(1, 19):
        total = total + weighed[j] * terms[3 + j, x, rows, :]
    return total


def member_at(velocity):
    return VELOCITY.index(velocity)


BODY = 8


def kernel(
    mesh_sizes,
    extent,
    primal,
    adjoint,
    porosity,
    solid,
    out_inner,
    out_grad,
    out_drag,
    level_one,
    marks,
    factors,
    terms_last,
    face_last,
    columns_last,
    corner_last,
    level_two,
    states,
    porous,
    terms_first,
    sums,
    face_send,
    rows_send,
    columns_send,
    xy_send,
    xz_send,
    yz_send,
    face_first,
    rows_recv,
    columns_first,
    xy_recv,
    corner_first,
    yz_recv,
    response,
    drag_row,
    drag_slots,
    meter,
    load_sem,
    send_sem,
    recv_sem,
    drag_sem,
):
    sx, sy, sz = mesh_sizes
    nx, ny, nz = extent
    halves = ny // 8
    terms = (terms_first, terms_last)
    face_recv = (face_first, face_last)
    columns_recv = (columns_first, columns_last)
    xz_recv = (corner_first, corner_last)
    body = pl.ds(BODY, ny)
    inner = tuple(range(1, nx - 1))
    outer = (0, nx - 1)
    me = (lax.axis_index("gx"), lax.axis_index("gy"), lax.axis_index("gz"))
    loads = [
        pltpu.make_async_copy(adjoint, level_two.at[:, :, body, :], load_sem.at[0]),
        pltpu.make_async_copy(primal, states, load_sem.at[1]),
        pltpu.make_async_copy(porosity, porous, load_sem.at[2]),
        pltpu.make_async_copy(solid, marks, load_sem.at[3]),
    ]
    for load in loads:
        load.start()

    stepped = tuple(
        {
            0: me[d],
            1: jnp.where(me[d] == mesh_sizes[d] - 1, 0, me[d] + 1),
            -1: jnp.where(me[d] == 0, mesh_sizes[d] - 1, me[d] - 1),
        }
        for d in range(3)
    )

    def shifted(offset):
        return tuple(stepped[d][offset[d]] for d in range(3))

    faces = [tuple(s if d == dim else 0 for d in range(3)) for dim in range(3) for s in (1, -1)]
    edges = [
        tuple(s if d == p else t if d == q else 0 for d in range(3))
        for p, q in ((0, 2), (1, 2), (0, 1))
        for s in (1, -1)
        for t in (1, -1)
    ]
    around = edges + faces
    corner_part = [d for d in edges if not d[0]]
    near_part = [d for d in faces if not d[0]]
    side_part = [d for d in around if d[0]]

    pair, core = me[0] // 2, me[0] % 2
    pairs = sx // 2
    first_group = [(c, z) for c in range(2) for z in range(sz) if (c, z) != (0, 0)]
    second_group = [(h, y) for h in range(pairs) for y in range(sy) if (h, y) != (0, 0)]

    def first_partner(c, z):
        return (pair * 2 + lax.rem(core + c, 2), me[1], lax.rem(me[2] + z, sz))

    def second_partner(h, y):
        return (lax.rem(pair + h, pairs) * 2 + core, lax.rem(me[1] + y, sy), me[2])

    barrier = pltpu.get_barrier_semaphore()
    far = [(z, 1, first_partner(c, z)) for c, z in first_group if (c, z) not in ((0, 1), (0, sz - 1))]
    far = [(min(z, sz - z), n, target) for z, n, target in far]
    for h, y in second_group:
        if (h, y) not in ((0, 1), (0, sy - 1)):
            far.append((2 * h + (min(y, sy - y) + 1) // 2, 2, second_partner(h, y)))
    for offset in around:
        far.append((2 * abs(offset[0]) + abs(offset[1]) + abs(offset[2]), 3, shifted(offset)))
    targets = [entry[2] for entry in sorted(far, key=lambda entry: -entry[0])]
    for target in targets:
        pl.semaphore_signal(barrier, inc=1, device_id=target, device_id_type=MESH)

    for sign in (1, -1):
        for k, i in enumerate(ALONG[0][sign]):
            source = adjoint.at[i, 0 if sign == 1 else nx - 1]
            pltpu.make_async_copy(source, face_send.at[0, slot(sign), k], load_sem.at[4]).start()

    lane = lax.broadcasted_iota(jnp.int32, (8, nz), 1)

    def pack(step, cells, planes, again):
        for sign in (1, -1):
            at = slot(sign)
            for h in range(halves):
                rows = slice(8 * h, 8 * h + 8)
                packed = columns_send[step, at, rows, :] if again else jnp.zeros((8, nz), F32)
                for k, i in enumerate(ALONG[2][sign]):
                    for x in planes:
                        spot = k * nx + x
                        column = cells[i, x, BODY + 8 * h : BODY + 8 * h + 8, :]
                        turn = (spot if sign == 1 else spot + 1) % nz
                        column = pltpu.roll(column, turn, 1) if turn else column
                        packed = jnp.where(lane == spot, column, packed)
                columns_send[step, at, rows, :] = packed
            edge_row = BODY if sign == 1 else BODY + ny - 1
            for k, i in enumerate(ALONG[1][sign]):
                for x in planes:
                    rows_send[step, at, k * nx + x : k * nx + x + 1, :] = cells[i, x, edge_row : edge_row + 1, :]

    def pack_edges(step, cells):
        for p in (1, -1):
            near = 0 if p == 1 else nx - 1
            for q in (1, -1):
                i = member_at((p, q, 0))
                row = BODY if q == 1 else BODY + ny - 1
                xy_send[step, slot(p) * 2 + slot(q)] = cells[i, near, row : row + 1, :]
                i = member_at((p, 0, q))
                packed = None
                for h in range(halves):
                    column = cells[i, near, BODY + 8 * h : BODY + 8 * h + 8, :]
                    turn = (h if q == 1 else h + 1) % nz
                    column = pltpu.roll(column, turn, 1) if turn else column
                    packed = column if packed is None else jnp.where(lane == h, column, packed)
                xz_send[step, slot(p) * 2 + slot(q)] = packed
                row = 0 if p == 1 else ny - 1
                yz_send[step, slot(p) * 2 + slot(q)] = columns_send[step, slot(q), row : row + 1, :]

    def message(step, direction):
        dx, dy, dz = direction
        if dx and not dy and not dz:
            source = face_send.at[step, slot(dx)]
            target = face_recv[step].at[slot(dx), :, body, :]
        elif dy and not dx and not dz:
            source = rows_send.at[step, slot(dy)]
            target = rows_recv.at[step, slot(dy)]
        elif dz and not dx and not dy:
            source = columns_send.at[step, slot(dz)]
            target = columns_recv[step].at[slot(dz), body, :]
        elif not dz:
            source = xy_send.at[step, slot(dx) * 2 + slot(dy)]
            target = xy_recv.at[step, slot(dx) * 2 + slot(dy)]
        elif not dy:
            source = xz_send.at[step, slot(dx) * 2 + slot(dz)]
            target = xz_recv[step].at[slot(dx) * 2 + slot(dz)]
        else:
            source = yz_send.at[step, slot(dy) * 2 + slot(dz)]
            target = yz_recv.at[step, slot(dy) * 2 + slot(dz)]
        copy = pltpu.make_async_remote_copy(
            src_ref=source,
            dst_ref=target,
            send_sem=send_sem.at[0],
            recv_sem=recv_sem.at[step, 1 if dx else 2 if dy and dz else 0],
            device_id=shifted(tuple(-d for d in direction)),
            device_id_type=MESH,
        )
        return copy

    def send(step, directions):
        for direction in directions:
            message(step, direction).start()

    def await_rows(rows, semaphore):
        whole = meter.at[pl.ds(0, rows)]
        pltpu.make_async_copy(whole, whole, semaphore).wait()

    def halo_row(sign):
        return BODY + ny if sign == 1 else BODY - 1

    def insert_rows(step, cells):
        for sign in (1, -1):
            row = halo_row(sign)
            for k, i in enumerate(ALONG[1][sign]):
                for x in range(nx):
                    if 0 <= x - VELOCITY[i][0] < nx:
                        got = rows_recv[step, slot(sign), k * nx + x : k * nx + x + 1, :]
                        cells[i, x, row : row + 1, :] = got

    def insert_edges(step):
        for dx in (1, -1):
            for dy in (1, -1):
                k = ALONG[0][dx].index(member_at((dx, dy, 0)))
                row = halo_row(dy)
                face_recv[step][slot(dx), k, row : row + 1, :] = xy_recv[step, slot(dx) * 2 + slot(dy)]

    def level(step, cells, x, h):
        return one_level(cells, face_recv[step], columns_recv[step], xz_recv[step], terms[step], factors, extent, x, h)

    nothing = jnp.zeros((1, nz), F32)
    for columns in columns_recv:
        for at in range(2):
            columns[at, BODY - 1 : BODY, :] = nothing
            columns[at, BODY + ny : BODY + ny + 1, :] = nothing
    loads[0].wait()
    pack(0, level_two, range(nx), False)
    pack_edges(0, level_two)
    for load in loads[1:]:
        load.wait()
    total = jnp.zeros((8, nz), F32)
    for x in range(nx):
        for h in range(halves):
            rows = slice(8 * h, 8 * h + 8)
            closed = jnp.where(marks[x, rows, :] == 0, porous[x, rows, :], 1.0)
            for j, value in enumerate(blocking_factors(closed)):
                factors[j, x, rows, :] = value
            flux = None
            for t in range(2):
                gain = sum(states[t, i, x, rows, :] for i in ALONG[0][1])
                loss = sum(states[t, i, x, rows, :] for i in ALONG[0][-1])
                flux = gain - loss if flux is None else flux + (gain - loss)
            out_grad[x, rows, :] = flux
            total = total + closed * flux
    drag_row[0] = jnp.sum(total, axis=0, keepdims=True)
    faces_in = face_send.at[0]
    pltpu.make_async_copy(faces_in, faces_in, load_sem.at[4]).wait()

    pl.semaphore_wait(barrier, len(targets))

    send(0, around)
    near_rows = sum(message_rows(d, extent) for d in near_part)
    side_rows = sum(message_rows(d, extent) for d in side_part)
    corner_rows = sum(message_rows(d, extent) for d in corner_part)

    mine_first = core * sz + me[2]
    mine_second = pair * sy + me[1]
    drag_first = drag_slots.at[pl.ds(0, 2 * sz)]
    drag_second = drag_slots.at[pl.ds(2 * sz, pairs * sy)]

    def drag_send(stage, target, mine, group, partner):
        target[mine] = drag_row[stage]
        for offset in group:
            pltpu.make_async_remote_copy(
                src_ref=drag_row.at[stage],
                dst_ref=target.at[mine],
                send_sem=drag_sem.at[2],
                recv_sem=drag_sem.at[stage],
                device_id=partner(*offset),
                device_id_type=MESH,
            ).start()

    drag_send(0, drag_first, mine_first, first_group, first_partner)

    for step, t in ((0, 1), (1, 0)):
        for x in range(nx):
            for h in range(halves):
                rows = slice(8 * h, 8 * h + 8)
                vel, _, weights = primal_terms([states[t, i, x, rows, :] for i in range(19)])
                for j, value in enumerate(vel + weights):
                    terms[step][j, x, rows, :] = value

    for step in range(2):
        for x in range(nx) if step == 0 else inner:
            for dy in (1, -1):
                for i, value in enumerate(corner_response(terms[step], factors, extent, dy, x)):
                    response[step, slot(dy), i, x] = value

    def first_level(x):
        for h in range(halves):
            fresh, weighed = level(0, level_two, x, h)
            rows = slice(8 * h, 8 * h + 8)
            for i in range(19):
                level_one[i, x, BODY + 8 * h : BODY + 8 * h + 8, :] = fresh[i]
                sums[i, x, rows, :] = weighed[i]

    def first_corners(x):
        for dy in (1, -1):
            h = corner_tile(extent, dy)[0]
            change = corner_change(yz_recv[0], extent, dy, x)
            for i in range(19):
                rows = slice(BODY + 8 * h, BODY + 8 * h + 8)
                level_one[i, x, rows, :] = level_one[i, x, rows, :] + change * response[0, slot(dy), i, x]

    await_rows(near_rows, recv_sem.at[0, 0])
    insert_rows(0, level_two)
    for x in inner:
        first_level(x)
    await_rows(side_rows, recv_sem.at[0, 1])
    insert_edges(0)
    for x in outer:
        first_level(x)
    await_rows(corner_rows, recv_sem.at[0, 2])
    for x in outer + inner:
        first_corners(x)
    for sign, near in ((1, 0), (-1, nx - 1)):
        for k, i in enumerate(ALONG[0][sign]):
            face_send[1, slot(sign), k] = level_one[i, near, body, :]
    pack(1, level_one, range(nx), False)
    pack_edges(1, level_one)
    send(1, around)

    await_rows(len(first_group), drag_sem.at[0])
    drag_row[1] = jnp.sum(drag_first[...], axis=0)
    drag_send(1, drag_second, mine_second, second_group, second_partner)

    for x in range(nx):
        for h in range(halves):
            rows = slice(8 * h, 8 * h + 8)
            weighed = [sums[j, x, rows, :] for j in range(19)]
            total = out_grad[x, rows, :] + weigh(terms[0], weighed, x, rows)
            for dy in (1, -1):
                if h == corner_tile(extent, dy)[0]:
                    change = corner_change(yz_recv[0], extent, dy, x)
                    total = total + change * corner_weight(terms[0], extent, dy, x)
            out_grad[x, rows, :] = total

    def second_level(x):
        for h in range(halves):
            rows = slice(8 * h, 8 * h + 8)
            fresh, weighed = level(1, level_one, x, h)
            for i in range(19):
                out_inner[i, x - 1, rows, :] = fresh[i]
            total = out_grad[x, rows, :] + weigh(terms[1], weighed, x, rows)
            out_grad[x, rows, :] = jnp.where(marks[x, rows, :] == 0, total, 0.0)

    await_rows(near_rows, recv_sem.at[1, 0])
    insert_rows(1, level_one)
    for x in inner:
        second_level(x)
    await_rows(side_rows, recv_sem.at[1, 1])
    insert_edges(1)
    await_rows(corner_rows, recv_sem.at[1, 2])
    for x in inner:
        for dy in (1, -1):
            h = corner_tile(extent, dy)[0]
            rows = slice(8 * h, 8 * h + 8)
            change = corner_change(yz_recv[1], extent, dy, x)
            for i in range(19):
                out_inner[i, x - 1, rows, :] = out_inner[i, x - 1, rows, :] + change * response[1, slot(dy), i, x]
            slope = change * corner_weight(terms[1], extent, dy, x)
            out_grad[x, rows, :] = out_grad[x, rows, :] + jnp.where(marks[x, rows, :] == 0, slope, 0.0)
    for sign in (1, -1):
        row = halo_row(sign)
        for t in (1, -1):
            columns_recv[1][slot(t), row : row + 1, :] = yz_recv[1, slot(sign) * 2 + slot(t)]

    await_rows(len(second_group), drag_sem.at[1])
    everyone = jnp.sum(drag_second[...], axis=0)
    cells_in_all = nx * ny * nz * sx * sy * sz
    out_drag[...] = jnp.broadcast_to(jnp.sum(everyone, axis=1, keepdims=True) * (1.0 / cells_in_all), (8, nz))

    await_rows(2 * (near_rows + side_rows + corner_rows), send_sem.at[0])
    await_rows(len(first_group) + len(second_group), drag_sem.at[2])


def message_rows(direction, extent):
    nx, ny, nz = extent
    dx, dy, dz = (d != 0 for d in direction)
    if dx + dy + dz == 1:
        return 5 * ny if dx else -(-5 * nx // 8) * 8 if dy else ny
    return 8 if dx and dz else 1


def finish(
    extent,
    inner,
    grad,
    drag,
    cells,
    marks,
    factors,
    terms,
    face,
    columns,
    corner,
    out_adjoint,
    out_grad,
    out_drag,
    outer,
    grad_whole,
    total,
    sem,
):
    nx, ny, nz = extent
    copies = [pltpu.make_async_copy(inner, out_adjoint.at[:, pl.ds(1, nx - 2)], sem.at[0])]
    copies[0].start()
    total[...] = drag[0:1, 0:1]
    copies.append(pltpu.make_async_copy(total, out_drag, sem.at[1]))
    copies[1].start()
    for n, x in enumerate((0, nx - 1)):
        for h in range(ny // 8):
            rows = slice(8 * h, 8 * h + 8)
            fresh, weighed = one_level(cells, face, columns, corner, terms, factors, extent, x, h)
            for i in range(19):
                outer[n, i, rows, :] = fresh[i]
            slope = grad[x, rows, :] + weigh(terms, weighed, x, rows)
            grad_whole[x, rows, :] = jnp.where(marks[x, rows, :] == 0, slope, 0.0)
        copies.append(pltpu.make_async_copy(outer.at[n], out_adjoint.at[:, x], sem.at[2 + n]))
        copies[-1].start()
    for x in range(1, nx - 1):
        grad_whole[x] = grad[x]
    copies.append(pltpu.make_async_copy(grad_whole, out_grad, sem.at[4]))
    copies[-1].start()
    for copy in copies:
        copy.wait()


def solution(mesh):
    sizes = tuple(mesh.shape[name] for name in ("gx", "gy", "gz"))

    def body(primal_states, adjoint_last, porosity, solid_mask):
        nx, ny, nz = porosity.shape
        padded = ny + 16
        row_tiles = -(-5 * nx // 8) * 8
        hbm = pl.BlockSpec(memory_space=pltpu.HBM)
        vmem = pl.BlockSpec(memory_space=pltpu.VMEM)
        arguments = [
            pltpu.with_memory_space_constraint(v, pltpu.HBM)
            for v in (primal_states, adjoint_last, porosity, solid_mask)
        ]
        results = pl.pallas_call(
            functools.partial(kernel, sizes, (nx, ny, nz)),
            name="adjoint_window",
            out_shape=(
                pltpu.VMEM((19, nx - 2, ny, nz), F32),
                pltpu.VMEM((nx, ny, nz), F32),
                pltpu.VMEM((8, nz), F32),
                pltpu.VMEM((19, nx, padded, nz), F32),
                pltpu.VMEM((nx, ny, nz), jnp.int32),
                pltpu.VMEM((FACTORS, nx, ny, nz), F32),
                pltpu.VMEM((22, nx, ny, nz), F32),
                pltpu.VMEM((2, 5, padded, nz), F32),
                pltpu.VMEM((2, padded, nz), F32),
                pltpu.VMEM((4, 8, nz), F32),
            ),
            in_specs=[hbm] * 4,
            out_specs=(vmem,) * 10,
            scratch_shapes=[
                pltpu.VMEM((19, nx, padded, nz), F32),
                pltpu.VMEM((2, 19, nx, ny, nz), F32),
                pltpu.VMEM((nx, ny, nz), F32),
                pltpu.VMEM((22, nx, ny, nz), F32),
                pltpu.VMEM((19, nx, ny, nz), F32),
                pltpu.VMEM((2, 2, 5, ny, nz), F32),
                pltpu.VMEM((2, 2, row_tiles, nz), F32),
                pltpu.VMEM((2, 2, ny, nz), F32),
                pltpu.VMEM((2, 4, 1, nz), F32),
                pltpu.VMEM((2, 4, 8, nz), F32),
                pltpu.VMEM((2, 4, 1, nz), F32),
                pltpu.VMEM((2, 5, padded, nz), F32),
                pltpu.VMEM((2, 2, row_tiles, nz), F32),
                pltpu.VMEM((2, padded, nz), F32),
                pltpu.VMEM((2, 4, 1, nz), F32),
                pltpu.VMEM((4, 8, nz), F32),
                pltpu.VMEM((2, 4, 1, nz), F32),
                pltpu.VMEM((2, 2, 19, nx, 8, nz), F32),
                pltpu.VMEM((2, 1, nz), F32),
                pltpu.VMEM((2 * sizes[2] + sizes[0] // 2 * sizes[1], 1, nz), F32),
                pltpu.VMEM((1024, 1, nz), F32),
                pltpu.SemaphoreType.DMA((5,)),
                pltpu.SemaphoreType.DMA((1,)),
                pltpu.SemaphoreType.DMA((2, 3)),
                pltpu.SemaphoreType.DMA((3,)),
            ],
            compiler_params=pltpu.CompilerParams(
                collective_id=0, has_side_effects=True, vmem_limit_bytes=16 << 20
            ),
        )(*arguments)
        adjoint, gradient, drag = pl.pallas_call(
            functools.partial(finish, (nx, ny, nz)),
            name="finish",
            out_shape=(
                jax.ShapeDtypeStruct((19, nx, ny, nz), F32),
                jax.ShapeDtypeStruct((nx, ny, nz), F32),
                jax.ShapeDtypeStruct((1, 1), F32),
            ),
            in_specs=[vmem] * 10,
            out_specs=(hbm, hbm, hbm),
            scratch_shapes=[
                pltpu.VMEM((2, 19, ny, nz), F32),
                pltpu.VMEM((nx, ny, nz), F32),
                pltpu.VMEM((1, 1), F32),
                pltpu.SemaphoreType.DMA((5,)),
            ],
            compiler_params=pltpu.CompilerParams(vmem_limit_bytes=2 << 20),
        )(*results)
        return adjoint, gradient, drag.reshape(())

    return jax.shard_map(
        body,
        mesh=mesh,
        in_specs=(
            P(None, None, "gx", "gy", "gz"),
            P(None, "gx", "gy", "gz"),
            P("gx", "gy", "gz"),
            P("gx", "gy", "gz"),
        ),
        out_specs=(P(None, "gx", "gy", "gz"), P("gx", "gy", "gz"), P()),
        check_vma=False,
    )
```

```python
import functools

import jax
import jax.numpy as jnp
import numpy as np
from jax import lax
from jax.experimental import pallas as pl
from jax.experimental.pallas import tpu as pltpu
from jax.sharding import PartitionSpec as P

MESH = pl.DeviceIdType.MESH
F32 = jnp.float32

VELOCITY = (
    (0, 0, 0),
    (1, 0, 0),
    (-1, 0, 0),
    (0, 1, 0),
    (0, -1, 0),
    (0, 0, 1),
    (0, 0, -1),
    (1, 1, 0),
    (-1, -1, 0),
    (1, -1, 0),
    (-1, 1, 0),
    (1, 0, 1),
    (-1, 0, -1),
    (1, 0, -1),
    (-1, 0, 1),
    (0, 1, 1),
    (0, -1, -1),
    (0, 1, -1),
    (0, -1, 1),
)
ALONG = tuple(
    {sign: tuple(i for i in range(19) if VELOCITY[i][dim] == sign) for sign in (1, -1)} for dim in range(3)
)
FACES = ((1, 2), (3, 4), (5, 6))
EDGES = (((0, 1), (7, 8), (9, 10)), ((0, 2), (11, 12), (13, 14)), ((1, 2), (15, 16), (17, 18)))


def orthonormal_rows(monomials):
    rows = []
    for column in range(monomials.shape[1]):
        vector = monomials[:, column] * 1.0
        for sweep in range(2):
            for earlier in rows:
                vector = vector - np.dot(earlier, vector) * earlier
        vector = vector / np.sqrt(np.dot(vector, vector))
        rows.append(vector)
    return np.stack(rows)


def coefficients():
    vel = np.array(VELOCITY) * 1.0
    speeds = np.sum(np.abs(vel), axis=1)
    weights = np.where(speeds == 0, 1.0 / 3.0, np.where(speeds == 1, 1.0 / 18.0, 1.0 / 36.0))
    x, y, z = vel[:, 0], vel[:, 1], vel[:, 2]
    columns = [np.ones(19), x, y, z, x * x, y * y, z * z, x * y, x * z, y * z]
    columns += [x * y * y, x * z * z, y * x * x, y * z * z, z * x * x, z * y * y]
    columns += [x * x * y * y, x * x * z * z, y * y * z * z]
    basis = orthonormal_rows(np.stack(columns, axis=1))
    rates = np.array([0.0] * 4 + [1.6] * 6 + [1.2] * 9)
    relax = basis.T @ np.diag(rates) @ basis
    kept = 1.2 * np.eye(19) - relax
    scalar = relax @ weights
    square = relax @ (weights * x * x)
    first = relax @ (weights * x)
    face = (kept[1] + kept[2]) / 2 - kept[0]
    return dict(
        s0=(scalar[0], scalar[1], scalar[7]),
        s1=(first[1], first[7]),
        s2=(square[0], square[3], square[15], square[1] - square[3], square[7] - square[15]),
        s2_mixed=(relax @ (weights * x * y))[7],
        even=(kept[0][0], kept[0][1], kept[0][7]),
        odd=kept[1][1] / 2 - kept[1][2] / 2,
        square=(face[0], face[3], face[15], face[1] - face[3], face[7] - face[15]),
        mixed=(kept[7][7] + kept[8][7] - kept[9][7] - kept[10][7]) / 4,
    )


COEF = {name: tuple(np.asarray(v, np.float64).reshape(-1).tolist()) for name, v in coefficients().items()}


def pair_sums(members):
    face_sum = [members[a] + members[b] for a, b in FACES]
    face_diff = [members[a] - members[b] for a, b in FACES]
    edge = []
    for dims, (a, b), (c, d) in EDGES:
        edge.append((members[a] + members[b], members[a] - members[b], members[c] + members[d], members[c] - members[d]))
    plane = [e[0] + e[2] for e in edge]
    mixed = [e[0] - e[2] for e in edge]
    lean = [(e[1] + e[3], e[1] - e[3]) for e in edge]
    edge_square = [plane[0] + plane[1], plane[0] + plane[2], plane[1] + plane[2]]
    edge_diff = [lean[0][0] + lean[1][0], lean[0][1] + lean[2][0], lean[1][1] + lean[2][1]]
    face_total = face_sum[0] + face_sum[1] + face_sum[2]
    edge_total = plane[0] + plane[1] + plane[2]
    return face_sum, face_diff, edge, mixed, edge_square, edge_diff, face_total, edge_total


def primal_terms(state):
    face_sum, face_diff, edge, mixed, edge_square, edge_diff, face_total, edge_total = pair_sums(state)
    rho = state[0] + face_total + edge_total
    inverse = 1.0 / rho
    flux = [face_diff[a] + edge_diff[a] for a in range(3)]
    vel = [flux[a] * inverse for a in range(3)]
    third = rho * (1.0 / 3.0)
    press = [face_sum[a] + edge_square[a] - third - flux[a] * vel[a] for a in range(3)]
    total = press[0] + press[1] + press[2]
    centre = total * (2.0 / 21.0)
    stress = [0.4 * (press[a] * (1.0 / 6.0) + centre) for a in range(3)]
    shear = [0.1 * (mixed[e] - flux[dims[0]] * vel[dims[1]]) for e, (dims, _, _) in enumerate(EDGES)]
    flat = (stress[0] + stress[1] + stress[2]) * (-10.0 / 19.0)
    usq = vel[0] * vel[0] + vel[1] * vel[1] + vel[2] * vel[2]
    still = rho * (1.0 - 1.5 * usq)
    rest = 1.2 * state[0] + flat - 0.4 * still
    even, odd = [], []
    for a in range(3):
        feq_even = still + (4.5 * flux[a]) * vel[a]
        even.append(0.6 * face_sum[a] + (flat + stress[a]) - (1.2 / 18.0) * feq_even)
        odd.append(-0.4 * face_diff[a] - (3.6 / 18.0) * flux[a])
    for e, (dims, _, _) in enumerate(EDGES):
        p, q = dims
        bend = flat + stress[p] + stress[q]
        for sign, total_pair, diff_pair in ((1, edge[e][0], edge[e][1]), (-1, edge[e][2], edge[e][3])):
            along_flux = flux[p] + flux[q] if sign == 1 else flux[p] - flux[q]
            along_vel = vel[p] + vel[q] if sign == 1 else vel[p] - vel[q]
            feq_even = still + (4.5 * along_flux) * along_vel
            twist = bend + shear[e] if sign == 1 else bend - shear[e]
            even.append(0.6 * total_pair + twist - (1.2 / 36.0) * feq_even)
            odd.append(-0.4 * diff_pair - (3.6 / 36.0) * along_flux)
    return vel, flux[0], [rest] + even + odd


class Nothing:
    def __add__(self, other):
        return other

    __radd__ = __add__

    def __sub__(self, other):
        return -other

    def __rsub__(self, other):
        return other

    def __mul__(self, other):
        return self

    __rmul__ = __mul__

    def __neg__(self):
        return self


FACTORS = 6


def blocking_factors(blocking):
    open_part = 1.0 - blocking
    return [
        blocking,
        open_part,
        COEF["square"][3] * open_part,
        COEF["mixed"][0] * open_part,
        0.6 * blocking - 0.1,
        -0.1 - 0.4 * blocking,
    ]


def pull_back(read, vel, factors, source=True):
    c = COEF
    blocking, open_part, open_square, open_mixed, keep_sum, keep_diff = factors
    face_sum, face_diff, edge, mixed, edge_square, edge_diff, face_total, edge_total = pair_sums(read)
    rest = read[0]
    twice = face_total + 2.0 * edge_total
    count = rest + (face_total + edge_total)

    def by_class(f):
        return f[0] * count + (f[1] - f[0]) * twice

    s0 = c["s0"][0] * rest + c["s0"][1] * face_total + c["s0"][2] * edge_total
    s2_flat = by_class([9.0 * f for f in c["s2"][:3]])
    s2 = [s2_flat + (9.0 * c["s2"][3]) * face_sum[a] + (9.0 * c["s2"][4]) * edge_square[a] for a in range(3)]
    xy, xz, yz = [(9.0 * c["s2_mixed"][0]) * mixed[e] for e in range(3)]
    s0_thrice = 3.0 * s0
    bend = [
        (s2[0] - s0_thrice) * vel[0] + xy * vel[1] + xz * vel[2],
        xy * vel[0] + (s2[1] - s0_thrice) * vel[1] + yz * vel[2],
        xz * vel[0] + yz * vel[1] + (s2[2] - s0_thrice) * vel[2],
    ]
    density = s0 - 0.5 * (vel[0] * bend[0] + vel[1] * bend[1] + vel[2] * bend[2])
    by_face, by_edge = c["odd"][0] + 3.0 * c["s1"][0], c["odd"][0] + 3.0 * c["s1"][1]
    momentum = [open_part * (by_face * face_diff[a] + by_edge * edge_diff[a] + bend[a]) for a in range(3)]
    if source:
        momentum[0] = momentum[0] + blocking
    even = open_part * (by_class(c["even"]) + density)
    flat = open_part * by_class(c["square"][:3])
    square = [open_square * (face_sum[a] + edge_square[a]) for a in range(3)]
    cross = [open_mixed * mixed[e] for e in range(3)]
    at_face = even + flat
    at_edge = at_face + flat
    out = [None] * 19
    out[0] = (keep_sum + keep_sum) * rest + even
    for a, (i, j) in enumerate(FACES):
        half = keep_sum * face_sum[a] + (at_face + square[a])
        tilt = keep_diff * face_diff[a] + momentum[a]
        out[i], out[j] = half + tilt, half - tilt
    for e, (dims, same, cross_pair) in enumerate(EDGES):
        p, q = dims
        level = at_edge + (square[p] + square[q])
        half = keep_sum * edge[e][0] + (level + cross[e])
        tilt = keep_diff * edge[e][1] + (momentum[p] + momentum[q])
        out[same[0]], out[same[1]] = half + tilt, half - tilt
        half = keep_sum * edge[e][2] + (level - cross[e])
        tilt = keep_diff * edge[e][3] + (momentum[p] - momentum[q])
        out[cross_pair[0]], out[cross_pair[1]] = half + tilt, half - tilt
    sums = list(face_sum) + [s for e in edge for s in (e[0], e[2])]
    diffs = list(face_diff) + [d for e in edge for d in (e[1], e[3])]
    return out, [rest] + sums + diffs


def slot(sign):
    return 0 if sign == 1 else 1


def read_cells(cells, face, columns, corner, extent, x, h):
    nx, ny, nz = extent
    lane = lax.broadcasted_iota(jnp.int32, (8, nz), 1)
    read = []
    for i, (dx, dy, dz) in enumerate(VELOCITY):
        from_x = x + dx
        outside = not 0 <= from_x < nx
        rows = slice(BODY + 8 * h + dy, BODY + 8 * h + dy + 8)
        if outside:
            value = face[slot(dx), ALONG[0][dx].index(i), rows, :]
        else:
            value = cells[i, from_x, rows, :]
        if dz:
            last = nz - 1 if dz == 1 else 0
            if outside:
                column = corner[slot(dx) * 2 + slot(dz)]
                turn = (last - h) % nz
            else:
                column = columns[slot(dz), rows, :]
                turn = (last - ALONG[2][dz].index(i) * nx - from_x) % nz
            column = pltpu.roll(column, turn, 1) if turn else column
            value = jnp.where(lane == last, column, pltpu.roll(value, nz - 1 if dz == 1 else 1, 1))
        read.append(value)
    return read


def one_level(cells, face, columns, corner, terms, factors, extent, x, h):
    rows = slice(8 * h, 8 * h + 8)
    read = read_cells(cells, face, columns, corner, extent, x, h)
    vel = [terms[a, x, rows, :] for a in range(3)]
    return pull_back(read, vel, [factors[j, x, rows, :] for j in range(FACTORS)])


def corner_members(dy):
    return ((member_at((0, dy, dy)), dy), (member_at((0, dy, -dy)), -dy))


def corner_tile(extent, dy):
    return (extent[1] // 8 - 1, 7) if dy == 1 else (0, 0)


def corner_change(got, extent, dy, x):
    nx, ny, nz = extent
    lane = lax.broadcasted_iota(jnp.int32, (8, nz), 1)
    row = lax.broadcasted_iota(jnp.int32, (8, nz), 0)
    change = jnp.zeros((8, nz), F32)
    for i, dz in corner_members(dy):
        last = nz - 1 if dz == 1 else 0
        turn = (last - ALONG[2][dz].index(i) * nx - x) % nz
        value = jnp.broadcast_to(got[slot(dy) * 2 + slot(dz)], (8, nz))
        value = pltpu.roll(value, turn, 1) if turn else value
        change = jnp.where(lane == last, value, change)
    return jnp.where(row == corner_tile(extent, dy)[1], change, 0.0)


def corner_response(terms, factors, extent, dy, x):
    nx, ny, nz = extent
    h, at = corner_tile(extent, dy)
    rows = slice(8 * h, 8 * h + 8)
    lane = lax.broadcasted_iota(jnp.int32, (8, nz), 1)
    row = lax.broadcasted_iota(jnp.int32, (8, nz), 0)
    read = [Nothing()] * 19
    for i, dz in corner_members(dy):
        read[i] = jnp.where((row == at) & (lane == (nz - 1 if dz == 1 else 0)), 1.0, 0.0)
    vel = [terms[a, x, rows, :] for a in range(3)]
    return pull_back(read, vel, [factors[j, x, rows, :] for j in range(FACTORS)], source=False)[0]


def corner_weight(terms, extent, dy, x):
    nx, ny, nz = extent
    h = corner_tile(extent, dy)[0]
    rows = slice(8 * h, 8 * h + 8)
    lane = lax.broadcasted_iota(jnp.int32, (8, nz), 1)
    even, odd = 3 + 1 + 3 + 4, 3 + 1 + 9 + 3 + 4
    same, cross = [
        terms[even + n, x, rows, :] + terms[odd + n, x, rows, :]
        if dy == 1
        else terms[even + n, x, rows, :] - terms[odd + n, x, rows, :]
        for n in range(2)
    ]
    return jnp.where(lane == (nz - 1 if dy == 1 else 0), same, cross)


def weigh(terms, weighed, x, rows):
    total = weighed[0] * terms[3, x, rows, :]
    for j in range(1, 19):
        total = total + weighed[j] * terms[3 + j, x, rows, :]
    return total


def member_at(velocity):
    return VELOCITY.index(velocity)


BODY = 8


def kernel(
    mesh_sizes,
    extent,
    primal,
    adjoint,
    porosity,
    solid,
    out_inner,
    out_grad,
    out_drag,
    level_one,
    marks,
    factors,
    terms_last,
    face_last,
    columns_last,
    corner_last,
    level_two,
    states,
    porous,
    terms_first,
    sums,
    face_send,
    rows_send,
    columns_send,
    xy_send,
    xz_send,
    yz_send,
    face_first,
    rows_recv,
    columns_first,
    xy_recv,
    corner_first,
    yz_recv,
    response,
    drag_row,
    drag_slots,
    meter,
    load_sem,
    send_sem,
    recv_sem,
    drag_sem,
    relay_sem,
):
    sx, sy, sz = mesh_sizes
    nx, ny, nz = extent
    halves = ny // 8
    terms = (terms_first, terms_last)
    face_recv = (face_first, face_last)
    columns_recv = (columns_first, columns_last)
    xz_recv = (corner_first, corner_last)
    body = pl.ds(BODY, ny)
    inner = tuple(range(1, nx - 1))
    outer = (0, nx - 1)
    me = (lax.axis_index("gx"), lax.axis_index("gy"), lax.axis_index("gz"))
    loads = [
        pltpu.make_async_copy(adjoint, level_two.at[:, :, body, :], load_sem.at[0]),
        pltpu.make_async_copy(primal, states, load_sem.at[1]),
        pltpu.make_async_copy(porosity, porous, load_sem.at[2]),
        pltpu.make_async_copy(solid, marks, load_sem.at[3]),
    ]
    for load in loads:
        load.start()

    stepped = tuple(
        {
            0: me[d],
            1: jnp.where(me[d] == mesh_sizes[d] - 1, 0, me[d] + 1),
            -1: jnp.where(me[d] == 0, mesh_sizes[d] - 1, me[d] - 1),
        }
        for d in range(3)
    )

    def shifted(offset):
        return tuple(stepped[d][offset[d]] for d in range(3))

    faces = [tuple(s if d == dim else 0 for d in range(3)) for dim in range(3) for s in (1, -1)]
    edges = [
        tuple(s if d == p else t if d == q else 0 for d in range(3))
        for p, q in ((1, 2), (0, 2), (0, 1))
        for s in (1, -1)
        for t in (1, -1)
    ]
    around = edges + faces
    corner_part = [d for d in edges if not d[0]]
    near_part = [d for d in faces if not d[0]]
    side_part = [d for d in around if d[0]]

    pairs = sx // 2
    pair = sum(jnp.where(me[0] >= 2 * n, 1, 0) for n in range(1, pairs)) if pairs > 1 else 0
    core = me[0] - 2 * pair

    def ahead(index, count, size):
        moved = index + count
        return jnp.where(moved >= size, moved - size, moved) if count else index

    first_group = [(c, z) for c in range(2) for z in range(sz) if (c, z) != (0, 0)]
    second_group = [(h, y) for h in range(pairs) for y in range(sy) if (h, y) != (0, 0)]

    def first_partner(c, z):
        return (pair * 2 + ahead(core, c, 2), me[1], ahead(me[2], z, sz))

    def second_partner(h, y):
        return (ahead(pair, h, pairs) * 2 + core, ahead(me[1], y, sy), me[2])

    barrier = pltpu.get_barrier_semaphore()
    def ring(count, size):
        return min(count % size, -count % size)

    def first_hops(c, z):
        return ring(z, sz)

    def second_hops(h, y):
        if y % 2 == 0:
            return 2 * h + ring(y // 2, sy // 2)
        return 1 + max(ring(y // 2, sy // 2), ring(y // 2 + 1, sy // 2))

    first_near = [o for o in first_group if first_hops(*o) <= 3]
    first_far = [o for o in first_group if first_hops(*o) > 3]
    second_near = [o for o in second_group if second_hops(*o) <= 3]
    second_far = [o for o in second_group if second_hops(*o) > 3]
    signals = [(first_hops(*o), first_partner(*o)) for o in first_near if o not in ((0, 1), (0, sz - 1))]
    signals += [(second_hops(*o), second_partner(*o)) for o in second_near if o not in ((0, 1), (0, sy - 1))]
    for offset in around:
        signals.append((2 * abs(offset[0]) + 1.5 * abs(offset[1]) + abs(offset[2]), shifted(offset)))
    targets = [entry[1] for entry in sorted(signals, key=lambda entry: -entry[0])]
    for target in targets:
        pl.semaphore_signal(barrier, inc=1, device_id=target, device_id_type=MESH)

    for sign in (1, -1):
        for k, i in enumerate(ALONG[0][sign]):
            source = adjoint.at[i, 0 if sign == 1 else nx - 1]
            pltpu.make_async_copy(source, face_send.at[0, slot(sign), k], load_sem.at[4]).start()

    lane = lax.broadcasted_iota(jnp.int32, (8, nz), 1)

    def pack(step, cells, planes, again):
        for sign in (1, -1):
            at = slot(sign)
            for h in range(halves):
                rows = slice(8 * h, 8 * h + 8)
                packed = columns_send[step, at, rows, :] if again else jnp.zeros((8, nz), F32)
                for k, i in enumerate(ALONG[2][sign]):
                    for x in planes:
                        spot = k * nx + x
                        column = cells[i, x, BODY + 8 * h : BODY + 8 * h + 8, :]
                        turn = (spot if sign == 1 else spot + 1) % nz
                        column = pltpu.roll(column, turn, 1) if turn else column
                        packed = jnp.where(lane == spot, column, packed)
                columns_send[step, at, rows, :] = packed
            edge_row = BODY if sign == 1 else BODY + ny - 1
            for k, i in enumerate(ALONG[1][sign]):
                for x in planes:
                    rows_send[step, at, k * nx + x : k * nx + x + 1, :] = cells[i, x, edge_row : edge_row + 1, :]

    def pack_edges(step, cells):
        for p in (1, -1):
            near = 0 if p == 1 else nx - 1
            for q in (1, -1):
                i = member_at((p, q, 0))
                row = BODY if q == 1 else BODY + ny - 1
                xy_send[step, slot(p) * 2 + slot(q)] = cells[i, near, row : row + 1, :]
                i = member_at((p, 0, q))
                packed = None
                for h in range(halves):
                    column = cells[i, near, BODY + 8 * h : BODY + 8 * h + 8, :]
                    turn = (h if q == 1 else h + 1) % nz
                    column = pltpu.roll(column, turn, 1) if turn else column
                    packed = column if packed is None else jnp.where(lane == h, column, packed)
                xz_send[step, slot(p) * 2 + slot(q)] = packed

    def pack_corners(step, cells):
        for p in (1, -1):
            row = BODY if p == 1 else BODY + ny - 1
            for q in (1, -1):
                i = member_at((0, p, q))
                packed = None
                for x in range(nx):
                    spot = ALONG[2][q].index(i) * nx + x
                    corner = cells[i, x, row : row + 1, :]
                    turn = (spot if q == 1 else spot + 1) % nz
                    corner = pltpu.roll(corner, turn, 1) if turn else corner
                    packed = corner if packed is None else jnp.where(lane[0:1] == spot, corner, packed)
                yz_send[step, slot(p) * 2 + slot(q)] = packed

    def message(step, direction):
        dx, dy, dz = direction
        if dx and not dy and not dz:
            source = face_send.at[step, slot(dx)]
            target = face_recv[step].at[slot(dx), :, body, :]
        elif dy and not dx and not dz:
            source = rows_send.at[step, slot(dy)]
            target = rows_recv.at[step, slot(dy)]
        elif dz and not dx and not dy:
            source = columns_send.at[step, slot(dz)]
            target = columns_recv[step].at[slot(dz), body, :]
        elif not dz:
            source = xy_send.at[step, slot(dx) * 2 + slot(dy)]
            target = xy_recv.at[step, slot(dx) * 2 + slot(dy)]
        elif not dy:
            source = xz_send.at[step, slot(dx) * 2 + slot(dz)]
            target = xz_recv[step].at[slot(dx) * 2 + slot(dz)]
        else:
            source = yz_send.at[step, slot(dy) * 2 + slot(dz)]
            target = yz_recv.at[step, slot(dy) * 2 + slot(dz)]
        copy = pltpu.make_async_remote_copy(
            src_ref=source,
            dst_ref=target,
            send_sem=send_sem.at[0],
            recv_sem=recv_sem.at[step, 1 if dx else 2 if dy and dz else 0],
            device_id=shifted(tuple(-d for d in direction)),
            device_id_type=MESH,
        )
        return copy

    def send(step, directions):
        for direction in directions:
            message(step, direction).start()

    def await_rows(rows, semaphore):
        whole = meter.at[pl.ds(0, rows)]
        pltpu.make_async_copy(whole, whole, semaphore).wait()

    def halo_row(sign):
        return BODY + ny if sign == 1 else BODY - 1

    def insert_rows(step, cells):
        for sign in (1, -1):
            row = halo_row(sign)
            for k, i in enumerate(ALONG[1][sign]):
                for x in range(nx):
                    if 0 <= x - VELOCITY[i][0] < nx:
                        got = rows_recv[step, slot(sign), k * nx + x : k * nx + x + 1, :]
                        cells[i, x, row : row + 1, :] = got

    def insert_edges(step):
        for dx in (1, -1):
            for dy in (1, -1):
                k = ALONG[0][dx].index(member_at((dx, dy, 0)))
                row = halo_row(dy)
                face_recv[step][slot(dx), k, row : row + 1, :] = xy_recv[step, slot(dx) * 2 + slot(dy)]

    def level(step, cells, x, h):
        return one_level(cells, face_recv[step], columns_recv[step], xz_recv[step], terms[step], factors, extent, x, h)

    nothing = jnp.zeros((1, nz), F32)
    for columns in columns_recv:
        for at in range(2):
            columns[at, BODY - 1 : BODY, :] = nothing
            columns[at, BODY + ny : BODY + ny + 1, :] = nothing
    loads[0].wait()
    pack(0, level_two, range(nx), False)
    pack_edges(0, level_two)
    pack_corners(0, level_two)
    for load in loads[1:]:
        load.wait()
    total = jnp.zeros((8, nz), F32)
    for x in range(nx):
        for h in range(halves):
            rows = slice(8 * h, 8 * h + 8)
            closed = jnp.where(marks[x, rows, :] == 0, porous[x, rows, :], 1.0)
            for j, value in enumerate(blocking_factors(closed)):
                factors[j, x, rows, :] = value
            flux = None
            for t in range(2):
                gain = sum(states[t, i, x, rows, :] for i in ALONG[0][1])
                loss = sum(states[t, i, x, rows, :] for i in ALONG[0][-1])
                flux = gain - loss if flux is None else flux + (gain - loss)
            out_grad[x, rows, :] = flux
            total = total + closed * flux
    drag_row[0] = jnp.sum(total, axis=0, keepdims=True)
    faces_in = face_send.at[0]
    pltpu.make_async_copy(faces_in, faces_in, load_sem.at[4]).wait()

    pl.semaphore_wait(barrier, len(targets))

    send(0, around)
    pl.semaphore_signal(relay_sem.at[0], inc=1, device_id=first_partner(0, sz - 2), device_id_type=MESH)
    pl.semaphore_signal(relay_sem.at[1], inc=1, device_id=second_partner(1, 0), device_id_type=MESH)
    near_rows = sum(message_rows(d, extent) for d in near_part)
    side_rows = sum(message_rows(d, extent) for d in side_part)
    corner_rows = sum(message_rows(d, extent) for d in corner_part)

    mine_first = core * sz + me[2]
    mine_second = pair * sy + me[1]
    drag_first = drag_slots.at[pl.ds(0, 2 * sz)]
    drag_second = drag_slots.at[pl.ds(2 * sz, pairs * sy)]

    def drag_send(stage, target, mine, group, partner):
        for offset in group:
            pltpu.make_async_remote_copy(
                src_ref=drag_row.at[stage],
                dst_ref=target.at[mine],
                send_sem=drag_sem.at[2],
                recv_sem=drag_sem.at[stage],
                device_id=partner(*offset),
                device_id_type=MESH,
            ).start()

    drag_first[mine_first] = drag_row[0]
    drag_send(0, drag_first, mine_first, first_near, first_partner)

    for step, t in ((0, 1), (1, 0)):
        for x in range(nx):
            for h in range(halves):
                rows = slice(8 * h, 8 * h + 8)
                vel, _, weights = primal_terms([states[t, i, x, rows, :] for i in range(19)])
                for j, value in enumerate(vel + weights):
                    terms[step][j, x, rows, :] = value

    for step in range(2):
        for x in range(nx) if step == 0 else inner:
            for dy in (1, -1):
                for i, value in enumerate(corner_response(terms[step], factors, extent, dy, x)):
                    response[step, slot(dy), i, x] = value

    def first_level(x):
        for h in range(halves):
            fresh, weighed = level(0, level_two, x, h)
            rows = slice(8 * h, 8 * h + 8)
            for i in range(19):
                level_one[i, x, BODY + 8 * h : BODY + 8 * h + 8, :] = fresh[i]
                sums[i, x, rows, :] = weighed[i]
            for sign, near in ((1, 0), (-1, nx - 1)):
                if x == near:
                    for k, i in enumerate(ALONG[0][sign]):
                        face_send[1, slot(sign), k, rows, :] = fresh[i]

    def first_corners(x, changes, members):
        for dy in (1, -1):
            h = corner_tile(extent, dy)[0]
            for i in members:
                rows = slice(BODY + 8 * h, BODY + 8 * h + 8)
                value = level_one[i, x, rows, :] + changes[x, dy] * response[0, slot(dy), i, x]
                level_one[i, x, rows, :] = value
                for sign, near in ((1, 0), (-1, nx - 1)):
                    if x == near and i in ALONG[0][sign]:
                        face_send[1, slot(sign), ALONG[0][sign].index(i), 8 * h : 8 * h + 8, :] = value

    pl.semaphore_wait(relay_sem.at[0], 1)
    pl.semaphore_wait(relay_sem.at[1], 1)
    drag_send(0, drag_first, mine_first, first_far, first_partner)
    await_rows(near_rows, recv_sem.at[0, 0])
    insert_rows(0, level_two)
    for x in inner:
        first_level(x)
    await_rows(side_rows, recv_sem.at[0, 1])
    insert_edges(0)
    for x in outer:
        first_level(x)
    await_rows(corner_rows, recv_sem.at[0, 2])
    changes = {(x, dy): corner_change(yz_recv[0], extent, dy, x) for x in range(nx) for dy in (1, -1)}
    at_corner = tuple(member_at((0, p, q)) for p in (1, -1) for q in (1, -1))
    elsewhere = tuple(i for i in range(19) if i not in at_corner)
    for x in range(nx):
        first_corners(x, changes, at_corner)
    pack_corners(1, level_one)
    send(1, corner_part)
    for x in outer:
        first_corners(x, changes, elsewhere)
    pack_edges(1, level_one)
    send(1, side_part)
    for x in inner:
        first_corners(x, changes, elsewhere)
    pack(1, level_one, range(nx), False)
    send(1, near_part)

    await_rows(len(first_group), drag_sem.at[0])
    drag_row[1] = jnp.sum(drag_first[...], axis=0)
    drag_second[mine_second] = drag_row[1]
    drag_send(1, drag_second, mine_second, second_far + second_near, second_partner)

    for x in range(nx):
        for h in range(halves):
            rows = slice(8 * h, 8 * h + 8)
            weighed = [sums[j, x, rows, :] for j in range(19)]
            total = out_grad[x, rows, :] + weigh(terms[0], weighed, x, rows)
            for dy in (1, -1):
                if h == corner_tile(extent, dy)[0]:
                    change = corner_change(yz_recv[0], extent, dy, x)
                    total = total + change * corner_weight(terms[0], extent, dy, x)
            out_grad[x, rows, :] = total

    def second_level(x):
        for h in range(halves):
            rows = slice(8 * h, 8 * h + 8)
            fresh, weighed = level(1, level_one, x, h)
            for i in range(19):
                out_inner[i, x - 1, rows, :] = fresh[i]
            total = out_grad[x, rows, :] + weigh(terms[1], weighed, x, rows)
            out_grad[x, rows, :] = jnp.where(marks[x, rows, :] == 0, total, 0.0)

    await_rows(near_rows, recv_sem.at[1, 0])
    insert_rows(1, level_one)
    for x in inner:
        second_level(x)
    await_rows(side_rows, recv_sem.at[1, 1])
    insert_edges(1)
    await_rows(corner_rows, recv_sem.at[1, 2])
    for x in inner:
        for dy in (1, -1):
            h = corner_tile(extent, dy)[0]
            rows = slice(8 * h, 8 * h + 8)
            change = corner_change(yz_recv[1], extent, dy, x)
            for i in range(19):
                out_inner[i, x - 1, rows, :] = out_inner[i, x - 1, rows, :] + change * response[1, slot(dy), i, x]
            slope = change * corner_weight(terms[1], extent, dy, x)
            out_grad[x, rows, :] = out_grad[x, rows, :] + jnp.where(marks[x, rows, :] == 0, slope, 0.0)
    for sign in (1, -1):
        row = halo_row(sign)
        for t in (1, -1):
            columns_recv[1][slot(t), row : row + 1, :] = yz_recv[1, slot(sign) * 2 + slot(t)]

    await_rows(len(second_group), drag_sem.at[1])
    everyone = jnp.sum(drag_second[...], axis=0)
    cells_in_all = nx * ny * nz * sx * sy * sz
    out_drag[...] = jnp.broadcast_to(jnp.sum(everyone, axis=1, keepdims=True) * (1.0 / cells_in_all), (8, nz))

    await_rows(2 * (near_rows + side_rows + corner_rows), send_sem.at[0])
    await_rows(len(first_group) + len(second_group), drag_sem.at[2])


def message_rows(direction, extent):
    nx, ny, nz = extent
    dx, dy, dz = (d != 0 for d in direction)
    if dx + dy + dz == 1:
        return 5 * ny if dx else -(-5 * nx // 8) * 8 if dy else ny
    return 8 if dx and dz else 1


def finish(
    extent,
    inner,
    grad,
    drag,
    cells,
    marks,
    factors,
    terms,
    face,
    columns,
    corner,
    out_adjoint,
    out_grad,
    out_drag,
    outer,
    grad_whole,
    total,
    sem,
):
    nx, ny, nz = extent
    copies = [pltpu.make_async_copy(inner, out_adjoint.at[:, pl.ds(1, nx - 2)], sem.at[0])]
    copies[0].start()
    total[...] = drag[0:1, 0:1]
    copies.append(pltpu.make_async_copy(total, out_drag, sem.at[1]))
    copies[1].start()
    for n, x in enumerate((0, nx - 1)):
        for h in range(ny // 8):
            rows = slice(8 * h, 8 * h + 8)
            fresh, weighed = one_level(cells, face, columns, corner, terms, factors, extent, x, h)
            for i in range(19):
                outer[n, i, rows, :] = fresh[i]
            slope = grad[x, rows, :] + weigh(terms, weighed, x, rows)
            grad_whole[x, rows, :] = jnp.where(marks[x, rows, :] == 0, slope, 0.0)
        copies.append(pltpu.make_async_copy(outer.at[n], out_adjoint.at[:, x], sem.at[2 + n]))
        copies[-1].start()
    for x in range(1, nx - 1):
        grad_whole[x] = grad[x]
    copies.append(pltpu.make_async_copy(grad_whole, out_grad, sem.at[4]))
    copies[-1].start()
    for copy in copies:
        copy.wait()


def solution(mesh):
    sizes = tuple(mesh.shape[name] for name in ("gx", "gy", "gz"))

    def body(primal_states, adjoint_last, porosity, solid_mask):
        nx, ny, nz = porosity.shape
        padded = ny + 16
        row_tiles = -(-5 * nx // 8) * 8
        hbm = pl.BlockSpec(memory_space=pltpu.HBM)
        vmem = pl.BlockSpec(memory_space=pltpu.VMEM)
        arguments = [
            pltpu.with_memory_space_constraint(v, pltpu.HBM)
            for v in (primal_states, adjoint_last, porosity, solid_mask)
        ]
        results = pl.pallas_call(
            functools.partial(kernel, sizes, (nx, ny, nz)),
            name="adjoint_window",
            out_shape=(
                pltpu.VMEM((19, nx - 2, ny, nz), F32),
                pltpu.VMEM((nx, ny, nz), F32),
                pltpu.VMEM((8, nz), F32),
                pltpu.VMEM((19, nx, padded, nz), F32),
                pltpu.VMEM((nx, ny, nz), jnp.int32),
                pltpu.VMEM((FACTORS, nx, ny, nz), F32),
                pltpu.VMEM((22, nx, ny, nz), F32),
                pltpu.VMEM((2, 5, padded, nz), F32),
                pltpu.VMEM((2, padded, nz), F32),
                pltpu.VMEM((4, 8, nz), F32),
            ),
            in_specs=[hbm] * 4,
            out_specs=(vmem,) * 10,
            scratch_shapes=[
                pltpu.VMEM((19, nx, padded, nz), F32),
                pltpu.VMEM((2, 19, nx, ny, nz), F32),
                pltpu.VMEM((nx, ny, nz), F32),
                pltpu.VMEM((22, nx, ny, nz), F32),
                pltpu.VMEM((19, nx, ny, nz), F32),
                pltpu.VMEM((2, 2, 5, ny, nz), F32),
                pltpu.VMEM((2, 2, row_tiles, nz), F32),
                pltpu.VMEM((2, 2, ny, nz), F32),
                pltpu.VMEM((2, 4, 1, nz), F32),
                pltpu.VMEM((2, 4, 8, nz), F32),
                pltpu.VMEM((2, 4, 1, nz), F32),
                pltpu.VMEM((2, 5, padded, nz), F32),
                pltpu.VMEM((2, 2, row_tiles, nz), F32),
                pltpu.VMEM((2, padded, nz), F32),
                pltpu.VMEM((2, 4, 1, nz), F32),
                pltpu.VMEM((4, 8, nz), F32),
                pltpu.VMEM((2, 4, 1, nz), F32),
                pltpu.VMEM((2, 2, 19, nx, 8, nz), F32),
                pltpu.VMEM((2, 1, nz), F32),
                pltpu.VMEM((2 * sizes[2] + sizes[0] // 2 * sizes[1], 1, nz), F32),
                pltpu.VMEM((1024, 1, nz), F32),
                pltpu.SemaphoreType.DMA((5,)),
                pltpu.SemaphoreType.DMA((1,)),
                pltpu.SemaphoreType.DMA((2, 3)),
                pltpu.SemaphoreType.DMA((3,)),
                pltpu.SemaphoreType.REGULAR((2,)),
            ],
            compiler_params=pltpu.CompilerParams(
                collective_id=0, has_side_effects=True, vmem_limit_bytes=16 << 20
            ),
        )(*arguments)
        adjoint, gradient, drag = pl.pallas_call(
            functools.partial(finish, (nx, ny, nz)),
            name="finish",
            out_shape=(
                jax.ShapeDtypeStruct((19, nx, ny, nz), F32),
                jax.ShapeDtypeStruct((nx, ny, nz), F32),
                jax.ShapeDtypeStruct((1, 1), F32),
            ),
            in_specs=[vmem] * 10,
            out_specs=(hbm, hbm, hbm),
            scratch_shapes=[
                pltpu.VMEM((2, 19, ny, nz), F32),
                pltpu.VMEM((nx, ny, nz), F32),
                pltpu.VMEM((1, 1), F32),
                pltpu.SemaphoreType.DMA((5,)),
            ],
            compiler_params=pltpu.CompilerParams(vmem_limit_bytes=2 << 20),
        )(*results)
        return adjoint, gradient, drag.reshape(())

    return jax.shard_map(
        body,
        mesh=mesh,
        in_specs=(
            P(None, None, "gx", "gy", "gz"),
            P(None, "gx", "gy", "gz"),
            P("gx", "gy", "gz"),
            P("gx", "gy", "gz"),
        ),
        out_specs=(P(None, "gx", "gy", "gz"), P("gx", "gy", "gz"), P()),
        check_vma=False,
    )
```

```python
import functools

import jax
import jax.numpy as jnp
import numpy as np
from jax import lax
from jax.experimental import pallas as pl
from jax.experimental.pallas import tpu as pltpu
from jax.sharding import PartitionSpec as P

MESH = pl.DeviceIdType.MESH
F32 = jnp.float32

VELOCITY = (
    (0, 0, 0),
    (1, 0, 0),
    (-1, 0, 0),
    (0, 1, 0),
    (0, -1, 0),
    (0, 0, 1),
    (0, 0, -1),
    (1, 1, 0),
    (-1, -1, 0),
    (1, -1, 0),
    (-1, 1, 0),
    (1, 0, 1),
    (-1, 0, -1),
    (1, 0, -1),
    (-1, 0, 1),
    (0, 1, 1),
    (0, -1, -1),
    (0, 1, -1),
    (0, -1, 1),
)
ALONG = tuple(
    {sign: tuple(i for i in range(19) if VELOCITY[i][dim] == sign) for sign in (1, -1)} for dim in range(3)
)
FACES = ((1, 2), (3, 4), (5, 6))
EDGES = (((0, 1), (7, 8), (9, 10)), ((0, 2), (11, 12), (13, 14)), ((1, 2), (15, 16), (17, 18)))


def orthonormal_rows(monomials):
    rows = []
    for column in range(monomials.shape[1]):
        vector = monomials[:, column] * 1.0
        for sweep in range(2):
            for earlier in rows:
                vector = vector - np.dot(earlier, vector) * earlier
        vector = vector / np.sqrt(np.dot(vector, vector))
        rows.append(vector)
    return np.stack(rows)


def coefficients():
    vel = np.array(VELOCITY) * 1.0
    speeds = np.sum(np.abs(vel), axis=1)
    weights = np.where(speeds == 0, 1.0 / 3.0, np.where(speeds == 1, 1.0 / 18.0, 1.0 / 36.0))
    x, y, z = vel[:, 0], vel[:, 1], vel[:, 2]
    columns = [np.ones(19), x, y, z, x * x, y * y, z * z, x * y, x * z, y * z]
    columns += [x * y * y, x * z * z, y * x * x, y * z * z, z * x * x, z * y * y]
    columns += [x * x * y * y, x * x * z * z, y * y * z * z]
    basis = orthonormal_rows(np.stack(columns, axis=1))
    rates = np.array([0.0] * 4 + [1.6] * 6 + [1.2] * 9)
    relax = basis.T @ np.diag(rates) @ basis
    kept = 1.2 * np.eye(19) - relax
    scalar = relax @ weights
    square = relax @ (weights * x * x)
    first = relax @ (weights * x)
    face = (kept[1] + kept[2]) / 2 - kept[0]
    return dict(
        s0=(scalar[0], scalar[1], scalar[7]),
        s1=(first[1], first[7]),
        s2=(square[0], square[3], square[15], square[1] - square[3], square[7] - square[15]),
        s2_mixed=(relax @ (weights * x * y))[7],
        even=(kept[0][0], kept[0][1], kept[0][7]),
        odd=kept[1][1] / 2 - kept[1][2] / 2,
        square=(face[0], face[3], face[15], face[1] - face[3], face[7] - face[15]),
        mixed=(kept[7][7] + kept[8][7] - kept[9][7] - kept[10][7]) / 4,
    )


COEF = {name: tuple(np.asarray(v, np.float64).reshape(-1).tolist()) for name, v in coefficients().items()}


def pair_sums(members):
    face_sum = [members[a] + members[b] for a, b in FACES]
    face_diff = [members[a] - members[b] for a, b in FACES]
    edge = []
    for dims, (a, b), (c, d) in EDGES:
        edge.append((members[a] + members[b], members[a] - members[b], members[c] + members[d], members[c] - members[d]))
    plane = [e[0] + e[2] for e in edge]
    mixed = [e[0] - e[2] for e in edge]
    lean = [(e[1] + e[3], e[1] - e[3]) for e in edge]
    edge_square = [plane[0] + plane[1], plane[0] + plane[2], plane[1] + plane[2]]
    edge_diff = [lean[0][0] + lean[1][0], lean[0][1] + lean[2][0], lean[1][1] + lean[2][1]]
    face_total = face_sum[0] + face_sum[1] + face_sum[2]
    edge_total = plane[0] + plane[1] + plane[2]
    return face_sum, face_diff, edge, mixed, edge_square, edge_diff, face_total, edge_total


def primal_terms(state):
    face_sum, face_diff, edge, mixed, edge_square, edge_diff, face_total, edge_total = pair_sums(state)
    rho = state[0] + face_total + edge_total
    inverse = 1.0 / rho
    flux = [face_diff[a] + edge_diff[a] for a in range(3)]
    vel = [flux[a] * inverse for a in range(3)]
    third = rho * (1.0 / 3.0)
    press = [face_sum[a] + edge_square[a] - third - flux[a] * vel[a] for a in range(3)]
    total = press[0] + press[1] + press[2]
    centre = total * (2.0 / 21.0)
    stress = [0.4 * (press[a] * (1.0 / 6.0) + centre) for a in range(3)]
    shear = [0.1 * (mixed[e] - flux[dims[0]] * vel[dims[1]]) for e, (dims, _, _) in enumerate(EDGES)]
    flat = (stress[0] + stress[1] + stress[2]) * (-10.0 / 19.0)
    usq = vel[0] * vel[0] + vel[1] * vel[1] + vel[2] * vel[2]
    still = rho * (1.0 - 1.5 * usq)
    rest = 1.2 * state[0] + flat - 0.4 * still
    even, odd = [], []
    for a in range(3):
        feq_even = still + (4.5 * flux[a]) * vel[a]
        even.append(0.6 * face_sum[a] + (flat + stress[a]) - (1.2 / 18.0) * feq_even)
        odd.append(-0.4 * face_diff[a] - (3.6 / 18.0) * flux[a])
    for e, (dims, _, _) in enumerate(EDGES):
        p, q = dims
        bend = flat + stress[p] + stress[q]
        for sign, total_pair, diff_pair in ((1, edge[e][0], edge[e][1]), (-1, edge[e][2], edge[e][3])):
            along_flux = flux[p] + flux[q] if sign == 1 else flux[p] - flux[q]
            along_vel = vel[p] + vel[q] if sign == 1 else vel[p] - vel[q]
            feq_even = still + (4.5 * along_flux) * along_vel
            twist = bend + shear[e] if sign == 1 else bend - shear[e]
            even.append(0.6 * total_pair + twist - (1.2 / 36.0) * feq_even)
            odd.append(-0.4 * diff_pair - (3.6 / 36.0) * along_flux)
    return vel, flux[0], [rest] + even + odd


class Nothing:
    def __add__(self, other):
        return other

    __radd__ = __add__

    def __sub__(self, other):
        return -other

    def __rsub__(self, other):
        return other

    def __mul__(self, other):
        return self

    __rmul__ = __mul__

    def __neg__(self):
        return self


FACTORS = 6


def blocking_factors(blocking):
    open_part = 1.0 - blocking
    return [
        blocking,
        open_part,
        COEF["square"][3] * open_part,
        COEF["mixed"][0] * open_part,
        0.6 * blocking - 0.1,
        -0.1 - 0.4 * blocking,
    ]


def pull_back(read, vel, factors, source=True):
    c = COEF
    blocking, open_part, open_square, open_mixed, keep_sum, keep_diff = factors
    face_sum, face_diff, edge, mixed, edge_square, edge_diff, face_total, edge_total = pair_sums(read)
    rest = read[0]
    twice = face_total + 2.0 * edge_total
    count = rest + (face_total + edge_total)

    def by_class(f):
        return f[0] * count + (f[1] - f[0]) * twice

    s0 = c["s0"][0] * rest + c["s0"][1] * face_total + c["s0"][2] * edge_total
    s2_flat = by_class([9.0 * f for f in c["s2"][:3]])
    s2 = [s2_flat + (9.0 * c["s2"][3]) * face_sum[a] + (9.0 * c["s2"][4]) * edge_square[a] for a in range(3)]
    xy, xz, yz = [(9.0 * c["s2_mixed"][0]) * mixed[e] for e in range(3)]
    s0_thrice = 3.0 * s0
    bend = [
        (s2[0] - s0_thrice) * vel[0] + xy * vel[1] + xz * vel[2],
        xy * vel[0] + (s2[1] - s0_thrice) * vel[1] + yz * vel[2],
        xz * vel[0] + yz * vel[1] + (s2[2] - s0_thrice) * vel[2],
    ]
    density = s0 - 0.5 * (vel[0] * bend[0] + vel[1] * bend[1] + vel[2] * bend[2])
    by_face, by_edge = c["odd"][0] + 3.0 * c["s1"][0], c["odd"][0] + 3.0 * c["s1"][1]
    momentum = [open_part * (by_face * face_diff[a] + by_edge * edge_diff[a] + bend[a]) for a in range(3)]
    if source:
        momentum[0] = momentum[0] + blocking
    even = open_part * (by_class(c["even"]) + density)
    flat = open_part * by_class(c["square"][:3])
    square = [open_square * (face_sum[a] + edge_square[a]) for a in range(3)]
    cross = [open_mixed * mixed[e] for e in range(3)]
    at_face = even + flat
    at_edge = at_face + flat
    out = [None] * 19
    out[0] = (keep_sum + keep_sum) * rest + even
    for a, (i, j) in enumerate(FACES):
        half = keep_sum * face_sum[a] + (at_face + square[a])
        tilt = keep_diff * face_diff[a] + momentum[a]
        out[i], out[j] = half + tilt, half - tilt
    for e, (dims, same, cross_pair) in enumerate(EDGES):
        p, q = dims
        level = at_edge + (square[p] + square[q])
        half = keep_sum * edge[e][0] + (level + cross[e])
        tilt = keep_diff * edge[e][1] + (momentum[p] + momentum[q])
        out[same[0]], out[same[1]] = half + tilt, half - tilt
        half = keep_sum * edge[e][2] + (level - cross[e])
        tilt = keep_diff * edge[e][3] + (momentum[p] - momentum[q])
        out[cross_pair[0]], out[cross_pair[1]] = half + tilt, half - tilt
    sums = list(face_sum) + [s for e in edge for s in (e[0], e[2])]
    diffs = list(face_diff) + [d for e in edge for d in (e[1], e[3])]
    return out, [rest] + sums + diffs


def slot(sign):
    return 0 if sign == 1 else 1


def read_cells(cells, face, columns, corner, extent, x, h):
    nx, ny, nz = extent
    lane = lax.broadcasted_iota(jnp.int32, (8, nz), 1)
    read = []
    for i, (dx, dy, dz) in enumerate(VELOCITY):
        from_x = x + dx
        outside = not 0 <= from_x < nx
        rows = slice(BODY + 8 * h + dy, BODY + 8 * h + dy + 8)
        if outside:
            value = face[slot(dx), ALONG[0][dx].index(i), rows, :]
        else:
            value = cells[i, from_x, rows, :]
        if dz:
            last = nz - 1 if dz == 1 else 0
            if outside:
                column = corner[slot(dx) * 2 + slot(dz)]
                turn = (last - h) % nz
            else:
                column = columns[slot(dz), rows, :]
                turn = (last - ALONG[2][dz].index(i) * nx - from_x) % nz
            column = pltpu.roll(column, turn, 1) if turn else column
            value = jnp.where(lane == last, column, pltpu.roll(value, nz - 1 if dz == 1 else 1, 1))
        read.append(value)
    return read


def one_level(cells, face, columns, corner, terms, factors, extent, x, h):
    rows = slice(8 * h, 8 * h + 8)
    read = read_cells(cells, face, columns, corner, extent, x, h)
    vel = [terms[a, x, rows, :] for a in range(3)]
    return pull_back(read, vel, [factors[j, x, rows, :] for j in range(FACTORS)])


def corner_members(dy):
    return ((member_at((0, dy, dy)), dy), (member_at((0, dy, -dy)), -dy))


def corner_tile(extent, dy):
    return (extent[1] // 8 - 1, 7) if dy == 1 else (0, 0)


def corner_change(got, extent, dy, x):
    nx, ny, nz = extent
    lane = lax.broadcasted_iota(jnp.int32, (8, nz), 1)
    row = lax.broadcasted_iota(jnp.int32, (8, nz), 0)
    change = jnp.zeros((8, nz), F32)
    for i, dz in corner_members(dy):
        last = nz - 1 if dz == 1 else 0
        turn = (last - ALONG[2][dz].index(i) * nx - x) % nz
        value = jnp.broadcast_to(got[slot(dy) * 2 + slot(dz)], (8, nz))
        value = pltpu.roll(value, turn, 1) if turn else value
        change = jnp.where(lane == last, value, change)
    return jnp.where(row == corner_tile(extent, dy)[1], change, 0.0)


def corner_response(terms, factors, extent, dy, x):
    nx, ny, nz = extent
    h, at = corner_tile(extent, dy)
    rows = slice(8 * h, 8 * h + 8)
    lane = lax.broadcasted_iota(jnp.int32, (8, nz), 1)
    row = lax.broadcasted_iota(jnp.int32, (8, nz), 0)
    read = [Nothing()] * 19
    for i, dz in corner_members(dy):
        read[i] = jnp.where((row == at) & (lane == (nz - 1 if dz == 1 else 0)), 1.0, 0.0)
    vel = [terms[a, x, rows, :] for a in range(3)]
    return pull_back(read, vel, [factors[j, x, rows, :] for j in range(FACTORS)], source=False)[0]


def corner_weight(terms, extent, dy, x):
    nx, ny, nz = extent
    h = corner_tile(extent, dy)[0]
    rows = slice(8 * h, 8 * h + 8)
    lane = lax.broadcasted_iota(jnp.int32, (8, nz), 1)
    even, odd = 3 + 1 + 3 + 4, 3 + 1 + 9 + 3 + 4
    same, cross = [
        terms[even + n, x, rows, :] + terms[odd + n, x, rows, :]
        if dy == 1
        else terms[even + n, x, rows, :] - terms[odd + n, x, rows, :]
        for n in range(2)
    ]
    return jnp.where(lane == (nz - 1 if dy == 1 else 0), same, cross)


def weigh(terms, weighed, x, rows):
    total = weighed[0] * terms[3, x, rows, :]
    for j in range(1, 19):
        total = total + weighed[j] * terms[3 + j, x, rows, :]
    return total


def member_at(velocity):
    return VELOCITY.index(velocity)


BODY = 8


def kernel(
    mesh_sizes,
    extent,
    primal,
    adjoint,
    porosity,
    solid,
    out_inner,
    out_grad,
    out_drag,
    level_one,
    marks,
    factors,
    terms_last,
    face_last,
    columns_last,
    corner_last,
    level_two,
    states,
    porous,
    terms_first,
    sums,
    face_send,
    rows_send,
    columns_send,
    xy_send,
    xz_send,
    yz_send,
    face_first,
    rows_recv,
    columns_first,
    xy_recv,
    corner_first,
    yz_recv,
    response,
    drag_row,
    drag_slots,
    meter,
    load_sem,
    send_sem,
    recv_sem,
    drag_sem,
    relay_sem,
):
    sx, sy, sz = mesh_sizes
    nx, ny, nz = extent
    halves = ny // 8
    terms = (terms_first, terms_last)
    face_recv = (face_first, face_last)
    columns_recv = (columns_first, columns_last)
    xz_recv = (corner_first, corner_last)
    body = pl.ds(BODY, ny)
    inner = tuple(range(1, nx - 1))
    outer = (0, nx - 1)
    me = (lax.axis_index("gx"), lax.axis_index("gy"), lax.axis_index("gz"))
    loads = [
        pltpu.make_async_copy(adjoint, level_two.at[:, :, body, :], load_sem.at[0]),
        pltpu.make_async_copy(primal, states, load_sem.at[1]),
        pltpu.make_async_copy(porosity, porous, load_sem.at[2]),
        pltpu.make_async_copy(solid, marks, load_sem.at[3]),
    ]
    for load in loads:
        load.start()

    stepped = tuple(
        {
            0: me[d],
            1: jnp.where(me[d] == mesh_sizes[d] - 1, 0, me[d] + 1),
            -1: jnp.where(me[d] == 0, mesh_sizes[d] - 1, me[d] - 1),
        }
        for d in range(3)
    )

    def shifted(offset):
        return tuple(stepped[d][offset[d]] for d in range(3))

    faces = [tuple(s if d == dim else 0 for d in range(3)) for dim in range(3) for s in (1, -1)]
    edges = [
        tuple(s if d == p else t if d == q else 0 for d in range(3))
        for p, q in ((1, 2), (0, 2), (0, 1))
        for s in (1, -1)
        for t in (1, -1)
    ]
    around = edges + faces
    corner_part = [d for d in edges if not d[0]]
    near_part = [d for d in faces if not d[0]]
    side_part = [d for d in around if d[0]]

    pairs = sx // 2
    pair = sum(jnp.where(me[0] >= 2 * n, 1, 0) for n in range(1, pairs)) if pairs > 1 else 0
    core = me[0] - 2 * pair

    def ahead(index, count, size):
        moved = index + count
        return jnp.where(moved >= size, moved - size, moved) if count else index

    first_group = [(c, z) for c in range(2) for z in range(sz) if (c, z) != (0, 0)]
    second_group = [(h, y) for h in range(pairs) for y in range(sy) if (h, y) != (0, 0)]

    def first_partner(c, z):
        return (pair * 2 + ahead(core, c, 2), me[1], ahead(me[2], z, sz))

    def second_partner(h, y):
        return (ahead(pair, h, pairs) * 2 + core, ahead(me[1], y, sy), me[2])

    barrier = pltpu.get_barrier_semaphore()
    def ring(count, size):
        return min(count % size, -count % size)

    def first_hops(c, z):
        return ring(z, sz)

    def second_hops(h, y):
        if y % 2 == 0:
            return 2 * h + ring(y // 2, sy // 2)
        return 1 + max(ring(y // 2, sy // 2), ring(y // 2 + 1, sy // 2))

    first_near = [o for o in first_group if first_hops(*o) <= 3]
    first_far = [o for o in first_group if first_hops(*o) > 3]
    second_near = [o for o in second_group if second_hops(*o) <= 3]
    second_far = [o for o in second_group if second_hops(*o) > 3]
    signals = [(first_hops(*o), first_partner(*o)) for o in first_near if o not in ((0, 1), (0, sz - 1))]
    signals += [(second_hops(*o), second_partner(*o)) for o in second_near if o not in ((0, 1), (0, sy - 1))]
    for offset in around:
        signals.append((2 * abs(offset[0]) + 1.5 * abs(offset[1]) + abs(offset[2]), shifted(offset)))
    targets = [entry[1] for entry in sorted(signals, key=lambda entry: -entry[0])]
    for target in targets:
        pl.semaphore_signal(barrier, inc=1, device_id=target, device_id_type=MESH)

    for sign in (1, -1):
        for k, i in enumerate(ALONG[0][sign]):
            source = adjoint.at[i, 0 if sign == 1 else nx - 1]
            pltpu.make_async_copy(source, face_send.at[0, slot(sign), k], load_sem.at[4]).start()

    lane = lax.broadcasted_iota(jnp.int32, (8, nz), 1)

    def pack(step, cells, planes, again):
        for sign in (1, -1):
            at = slot(sign)
            for h in range(halves):
                rows = slice(8 * h, 8 * h + 8)
                packed = columns_send[step, at, rows, :] if again else jnp.zeros((8, nz), F32)
                for k, i in enumerate(ALONG[2][sign]):
                    for x in planes:
                        spot = k * nx + x
                        column = cells[i, x, BODY + 8 * h : BODY + 8 * h + 8, :]
                        turn = (spot if sign == 1 else spot + 1) % nz
                        column = pltpu.roll(column, turn, 1) if turn else column
                        packed = jnp.where(lane == spot, column, packed)
                columns_send[step, at, rows, :] = packed
            edge_row = BODY if sign == 1 else BODY + ny - 1
            for k, i in enumerate(ALONG[1][sign]):
                for x in planes:
                    rows_send[step, at, k * nx + x : k * nx + x + 1, :] = cells[i, x, edge_row : edge_row + 1, :]

    def pack_edges(step, cells):
        for p in (1, -1):
            near = 0 if p == 1 else nx - 1
            for q in (1, -1):
                i = member_at((p, q, 0))
                row = BODY if q == 1 else BODY + ny - 1
                xy_send[step, slot(p) * 2 + slot(q)] = cells[i, near, row : row + 1, :]
                i = member_at((p, 0, q))
                packed = None
                for h in range(halves):
                    column = cells[i, near, BODY + 8 * h : BODY + 8 * h + 8, :]
                    turn = (h if q == 1 else h + 1) % nz
                    column = pltpu.roll(column, turn, 1) if turn else column
                    packed = column if packed is None else jnp.where(lane == h, column, packed)
                xz_send[step, slot(p) * 2 + slot(q)] = packed

    def pack_corners(step, cells):
        for p in (1, -1):
            row = BODY if p == 1 else BODY + ny - 1
            for q in (1, -1):
                i = member_at((0, p, q))
                packed = None
                for x in range(nx):
                    spot = ALONG[2][q].index(i) * nx + x
                    corner = cells[i, x, row : row + 1, :]
                    turn = (spot if q == 1 else spot + 1) % nz
                    corner = pltpu.roll(corner, turn, 1) if turn else corner
                    packed = corner if packed is None else jnp.where(lane[0:1] == spot, corner, packed)
                yz_send[step, slot(p) * 2 + slot(q)] = packed

    def message(step, direction):
        dx, dy, dz = direction
        if dx and not dy and not dz:
            source = face_send.at[step, slot(dx)]
            target = face_recv[step].at[slot(dx), :, body, :]
        elif dy and not dx and not dz:
            source = rows_send.at[step, slot(dy)]
            target = rows_recv.at[step, slot(dy)]
        elif dz and not dx and not dy:
            source = columns_send.at[step, slot(dz)]
            target = columns_recv[step].at[slot(dz), body, :]
        elif not dz:
            source = xy_send.at[step, slot(dx) * 2 + slot(dy)]
            target = xy_recv.at[step, slot(dx) * 2 + slot(dy)]
        elif not dy:
            source = xz_send.at[step, slot(dx) * 2 + slot(dz)]
            target = xz_recv[step].at[slot(dx) * 2 + slot(dz)]
        else:
            source = yz_send.at[step, slot(dy) * 2 + slot(dz)]
            target = yz_recv.at[step, slot(dy) * 2 + slot(dz)]
        copy = pltpu.make_async_remote_copy(
            src_ref=source,
            dst_ref=target,
            send_sem=send_sem.at[0],
            recv_sem=recv_sem.at[step, 1 if dx else 2 if dy and dz else 0],
            device_id=shifted(tuple(-d for d in direction)),
            device_id_type=MESH,
        )
        return copy

    def send(step, directions):
        for direction in directions:
            message(step, direction).start()

    def await_rows(rows, semaphore):
        whole = meter.at[pl.ds(0, rows)]
        pltpu.make_async_copy(whole, whole, semaphore).wait()

    def halo_row(sign):
        return BODY + ny if sign == 1 else BODY - 1

    def insert_rows(step, cells):
        for sign in (1, -1):
            row = halo_row(sign)
            for k, i in enumerate(ALONG[1][sign]):
                for x in range(nx):
                    if 0 <= x - VELOCITY[i][0] < nx:
                        got = rows_recv[step, slot(sign), k * nx + x : k * nx + x + 1, :]
                        cells[i, x, row : row + 1, :] = got

    def insert_edges(step):
        for dx in (1, -1):
            for dy in (1, -1):
                k = ALONG[0][dx].index(member_at((dx, dy, 0)))
                row = halo_row(dy)
                face_recv[step][slot(dx), k, row : row + 1, :] = xy_recv[step, slot(dx) * 2 + slot(dy)]

    def level(step, cells, x, h):
        return one_level(cells, face_recv[step], columns_recv[step], xz_recv[step], terms[step], factors, extent, x, h)

    nothing = jnp.zeros((1, nz), F32)
    for columns in columns_recv:
        for at in range(2):
            columns[at, BODY - 1 : BODY, :] = nothing
            columns[at, BODY + ny : BODY + ny + 1, :] = nothing
    loads[0].wait()
    pack(0, level_two, range(nx), False)
    pack_edges(0, level_two)
    pack_corners(0, level_two)
    for load in loads[1:]:
        load.wait()
    total = jnp.zeros((8, nz), F32)
    for x in range(nx):
        for h in range(halves):
            rows = slice(8 * h, 8 * h + 8)
            closed = jnp.where(marks[x, rows, :] == 0, porous[x, rows, :], 1.0)
            for j, value in enumerate(blocking_factors(closed)):
                factors[j, x, rows, :] = value
            flux = None
            for t in range(2):
                gain = sum(states[t, i, x, rows, :] for i in ALONG[0][1])
                loss = sum(states[t, i, x, rows, :] for i in ALONG[0][-1])
                flux = gain - loss if flux is None else flux + (gain - loss)
            out_grad[x, rows, :] = flux
            total = total + closed * flux
    drag_row[0] = jnp.sum(total, axis=0, keepdims=True)
    faces_in = face_send.at[0]
    pltpu.make_async_copy(faces_in, faces_in, load_sem.at[4]).wait()

    pl.semaphore_wait(barrier, len(targets))

    send(0, side_part)
    send(0, corner_part)
    send(0, near_part)
    pl.semaphore_signal(relay_sem.at[0], inc=1, device_id=first_partner(0, sz - 2), device_id_type=MESH)
    pl.semaphore_signal(relay_sem.at[1], inc=1, device_id=second_partner(1, 0), device_id_type=MESH)
    near_rows = sum(message_rows(d, extent) for d in near_part)
    side_rows = sum(message_rows(d, extent) for d in side_part)
    corner_rows = sum(message_rows(d, extent) for d in corner_part)

    mine_first = core * sz + me[2]
    mine_second = pair * sy + me[1]
    drag_first = drag_slots.at[pl.ds(0, 2 * sz)]
    drag_second = drag_slots.at[pl.ds(2 * sz, pairs * sy)]

    def drag_send(stage, target, mine, group, partner):
        for offset in group:
            pltpu.make_async_remote_copy(
                src_ref=drag_row.at[stage],
                dst_ref=target.at[mine],
                send_sem=drag_sem.at[2],
                recv_sem=drag_sem.at[stage],
                device_id=partner(*offset),
                device_id_type=MESH,
            ).start()

    drag_first[mine_first] = drag_row[0]
    drag_send(0, drag_first, mine_first, first_near, first_partner)

    for step, t in ((0, 1), (1, 0)):
        for x in range(nx):
            for h in range(halves):
                rows = slice(8 * h, 8 * h + 8)
                vel, _, weights = primal_terms([states[t, i, x, rows, :] for i in range(19)])
                for j, value in enumerate(vel + weights):
                    terms[step][j, x, rows, :] = value

    for step in range(2):
        for x in range(nx) if step == 0 else inner:
            for dy in (1, -1):
                for i, value in enumerate(corner_response(terms[step], factors, extent, dy, x)):
                    response[step, slot(dy), i, x] = value

    def first_level(x):
        for h in range(halves):
            fresh, weighed = level(0, level_two, x, h)
            rows = slice(8 * h, 8 * h + 8)
            for i in range(19):
                level_one[i, x, BODY + 8 * h : BODY + 8 * h + 8, :] = fresh[i]
                sums[i, x, rows, :] = weighed[i]
            for sign, near in ((1, 0), (-1, nx - 1)):
                if x == near:
                    for k, i in enumerate(ALONG[0][sign]):
                        face_send[1, slot(sign), k, rows, :] = fresh[i]

    def first_corners(x, changes, members):
        for dy in (1, -1):
            h = corner_tile(extent, dy)[0]
            for i in members:
                rows = slice(BODY + 8 * h, BODY + 8 * h + 8)
                value = level_one[i, x, rows, :] + changes[x, dy] * response[0, slot(dy), i, x]
                level_one[i, x, rows, :] = value
                for sign, near in ((1, 0), (-1, nx - 1)):
                    if x == near and i in ALONG[0][sign]:
                        face_send[1, slot(sign), ALONG[0][sign].index(i), 8 * h : 8 * h + 8, :] = value

    pl.semaphore_wait(relay_sem.at[0], 1)
    pl.semaphore_wait(relay_sem.at[1], 1)
    drag_send(0, drag_first, mine_first, first_far, first_partner)
    await_rows(near_rows, recv_sem.at[0, 0])
    insert_rows(0, level_two)
    for x in inner:
        first_level(x)
    await_rows(side_rows, recv_sem.at[0, 1])
    insert_edges(0)
    for x in outer:
        first_level(x)
    await_rows(corner_rows, recv_sem.at[0, 2])
    changes = {(x, dy): corner_change(yz_recv[0], extent, dy, x) for x in range(nx) for dy in (1, -1)}
    at_corner = tuple(member_at((0, p, q)) for p in (1, -1) for q in (1, -1))
    elsewhere = tuple(i for i in range(19) if i not in at_corner)
    for x in range(nx):
        first_corners(x, changes, at_corner)
    pack_corners(1, level_one)
    for x in outer:
        first_corners(x, changes, elsewhere)
    pack_edges(1, level_one)
    send(1, side_part)
    send(1, corner_part)
    for x in inner:
        first_corners(x, changes, elsewhere)
    pack(1, level_one, range(nx), False)
    send(1, near_part)

    await_rows(len(first_group), drag_sem.at[0])
    drag_row[1] = jnp.sum(drag_first[...], axis=0)
    drag_second[mine_second] = drag_row[1]
    drag_send(1, drag_second, mine_second, second_far + second_near, second_partner)

    for x in range(nx):
        for h in range(halves):
            rows = slice(8 * h, 8 * h + 8)
            weighed = [sums[j, x, rows, :] for j in range(19)]
            total = out_grad[x, rows, :] + weigh(terms[0], weighed, x, rows)
            for dy in (1, -1):
                if h == corner_tile(extent, dy)[0]:
                    change = corner_change(yz_recv[0], extent, dy, x)
                    total = total + change * corner_weight(terms[0], extent, dy, x)
            out_grad[x, rows, :] = total

    def second_level(x):
        for h in range(halves):
            rows = slice(8 * h, 8 * h + 8)
            fresh, weighed = level(1, level_one, x, h)
            for i in range(19):
                out_inner[i, x - 1, rows, :] = fresh[i]
            total = out_grad[x, rows, :] + weigh(terms[1], weighed, x, rows)
            out_grad[x, rows, :] = jnp.where(marks[x, rows, :] == 0, total, 0.0)

    await_rows(near_rows, recv_sem.at[1, 0])
    insert_rows(1, level_one)
    for x in inner:
        second_level(x)
    await_rows(side_rows, recv_sem.at[1, 1])
    insert_edges(1)
    await_rows(corner_rows, recv_sem.at[1, 2])
    for x in inner:
        for dy in (1, -1):
            h = corner_tile(extent, dy)[0]
            rows = slice(8 * h, 8 * h + 8)
            change = corner_change(yz_recv[1], extent, dy, x)
            for i in range(19):
                out_inner[i, x - 1, rows, :] = out_inner[i, x - 1, rows, :] + change * response[1, slot(dy), i, x]
            slope = change * corner_weight(terms[1], extent, dy, x)
            out_grad[x, rows, :] = out_grad[x, rows, :] + jnp.where(marks[x, rows, :] == 0, slope, 0.0)
    for sign in (1, -1):
        row = halo_row(sign)
        for t in (1, -1):
            columns_recv[1][slot(t), row : row + 1, :] = yz_recv[1, slot(sign) * 2 + slot(t)]

    await_rows(len(second_group), drag_sem.at[1])
    everyone = jnp.sum(drag_second[...], axis=0)
    cells_in_all = nx * ny * nz * sx * sy * sz
    out_drag[...] = jnp.broadcast_to(jnp.sum(everyone, axis=1, keepdims=True) * (1.0 / cells_in_all), (8, nz))

    await_rows(2 * (near_rows + side_rows + corner_rows), send_sem.at[0])
    await_rows(len(first_group) + len(second_group), drag_sem.at[2])


def message_rows(direction, extent):
    nx, ny, nz = extent
    dx, dy, dz = (d != 0 for d in direction)
    if dx + dy + dz == 1:
        return 5 * ny if dx else -(-5 * nx // 8) * 8 if dy else ny
    return 8 if dx and dz else 1


def finish(
    extent,
    inner,
    grad,
    drag,
    cells,
    marks,
    factors,
    terms,
    face,
    columns,
    corner,
    out_adjoint,
    out_grad,
    out_drag,
    outer,
    grad_whole,
    total,
    sem,
):
    nx, ny, nz = extent
    copies = [pltpu.make_async_copy(inner, out_adjoint.at[:, pl.ds(1, nx - 2)], sem.at[0])]
    copies[0].start()
    total[...] = drag[0:1, 0:1]
    copies.append(pltpu.make_async_copy(total, out_drag, sem.at[1]))
    copies[1].start()
    for n, x in enumerate((0, nx - 1)):
        for h in range(ny // 8):
            rows = slice(8 * h, 8 * h + 8)
            fresh, weighed = one_level(cells, face, columns, corner, terms, factors, extent, x, h)
            for i in range(19):
                outer[n, i, rows, :] = fresh[i]
            slope = grad[x, rows, :] + weigh(terms, weighed, x, rows)
            grad_whole[x, rows, :] = jnp.where(marks[x, rows, :] == 0, slope, 0.0)
        copies.append(pltpu.make_async_copy(outer.at[n], out_adjoint.at[:, x], sem.at[2 + n]))
        copies[-1].start()
    for x in range(1, nx - 1):
        grad_whole[x] = grad[x]
    copies.append(pltpu.make_async_copy(grad_whole, out_grad, sem.at[4]))
    copies[-1].start()
    for copy in copies:
        copy.wait()


def solution(mesh):
    sizes = tuple(mesh.shape[name] for name in ("gx", "gy", "gz"))

    def body(primal_states, adjoint_last, porosity, solid_mask):
        nx, ny, nz = porosity.shape
        padded = ny + 16
        row_tiles = -(-5 * nx // 8) * 8
        hbm = pl.BlockSpec(memory_space=pltpu.HBM)
        vmem = pl.BlockSpec(memory_space=pltpu.VMEM)
        arguments = [
            pltpu.with_memory_space_constraint(v, pltpu.HBM)
            for v in (primal_states, adjoint_last, porosity, solid_mask)
        ]
        results = pl.pallas_call(
            functools.partial(kernel, sizes, (nx, ny, nz)),
            name="adjoint_window",
            out_shape=(
                pltpu.VMEM((19, nx - 2, ny, nz), F32),
                pltpu.VMEM((nx, ny, nz), F32),
                pltpu.VMEM((8, nz), F32),
                pltpu.VMEM((19, nx, padded, nz), F32),
                pltpu.VMEM((nx, ny, nz), jnp.int32),
                pltpu.VMEM((FACTORS, nx, ny, nz), F32),
                pltpu.VMEM((22, nx, ny, nz), F32),
                pltpu.VMEM((2, 5, padded, nz), F32),
                pltpu.VMEM((2, padded, nz), F32),
                pltpu.VMEM((4, 8, nz), F32),
            ),
            in_specs=[hbm] * 4,
            out_specs=(vmem,) * 10,
            scratch_shapes=[
                pltpu.VMEM((19, nx, padded, nz), F32),
                pltpu.VMEM((2, 19, nx, ny, nz), F32),
                pltpu.VMEM((nx, ny, nz), F32),
                pltpu.VMEM((22, nx, ny, nz), F32),
                pltpu.VMEM((19, nx, ny, nz), F32),
                pltpu.VMEM((2, 2, 5, ny, nz), F32),
                pltpu.VMEM((2, 2, row_tiles, nz), F32),
                pltpu.VMEM((2, 2, ny, nz), F32),
                pltpu.VMEM((2, 4, 1, nz), F32),
                pltpu.VMEM((2, 4, 8, nz), F32),
                pltpu.VMEM((2, 4, 1, nz), F32),
                pltpu.VMEM((2, 5, padded, nz), F32),
                pltpu.VMEM((2, 2, row_tiles, nz), F32),
                pltpu.VMEM((2, padded, nz), F32),
                pltpu.VMEM((2, 4, 1, nz), F32),
                pltpu.VMEM((4, 8, nz), F32),
                pltpu.VMEM((2, 4, 1, nz), F32),
                pltpu.VMEM((2, 2, 19, nx, 8, nz), F32),
                pltpu.VMEM((2, 1, nz), F32),
                pltpu.VMEM((2 * sizes[2] + sizes[0] // 2 * sizes[1], 1, nz), F32),
                pltpu.VMEM((1024, 1, nz), F32),
                pltpu.SemaphoreType.DMA((5,)),
                pltpu.SemaphoreType.DMA((1,)),
                pltpu.SemaphoreType.DMA((2, 3)),
                pltpu.SemaphoreType.DMA((3,)),
                pltpu.SemaphoreType.REGULAR((2,)),
            ],
            compiler_params=pltpu.CompilerParams(
                collective_id=0, has_side_effects=True, vmem_limit_bytes=16 << 20
            ),
        )(*arguments)
        adjoint, gradient, drag = pl.pallas_call(
            functools.partial(finish, (nx, ny, nz)),
            name="finish",
            out_shape=(
                jax.ShapeDtypeStruct((19, nx, ny, nz), F32),
                jax.ShapeDtypeStruct((nx, ny, nz), F32),
                jax.ShapeDtypeStruct((1, 1), F32),
            ),
            in_specs=[vmem] * 10,
            out_specs=(hbm, hbm, hbm),
            scratch_shapes=[
                pltpu.VMEM((2, 19, ny, nz), F32),
                pltpu.VMEM((nx, ny, nz), F32),
                pltpu.VMEM((1, 1), F32),
                pltpu.SemaphoreType.DMA((5,)),
            ],
            compiler_params=pltpu.CompilerParams(vmem_limit_bytes=2 << 20),
        )(*results)
        return adjoint, gradient, drag.reshape(())

    return jax.shard_map(
        body,
        mesh=mesh,
        in_specs=(
            P(None, None, "gx", "gy", "gz"),
            P(None, "gx", "gy", "gz"),
            P("gx", "gy", "gz"),
            P("gx", "gy", "gz"),
        ),
        out_specs=(P(None, "gx", "gy", "gz"), P("gx", "gy", "gz"), P()),
        check_vma=False,
    )
```

```python
import functools

import jax
import jax.numpy as jnp
import numpy as np
from jax import lax
from jax.experimental import pallas as pl
from jax.experimental.pallas import tpu as pltpu
from jax.sharding import PartitionSpec as P

MESH = pl.DeviceIdType.MESH
F32 = jnp.float32

VELOCITY = (
    (0, 0, 0),
    (1, 0, 0),
    (-1, 0, 0),
    (0, 1, 0),
    (0, -1, 0),
    (0, 0, 1),
    (0, 0, -1),
    (1, 1, 0),
    (-1, -1, 0),
    (1, -1, 0),
    (-1, 1, 0),
    (1, 0, 1),
    (-1, 0, -1),
    (1, 0, -1),
    (-1, 0, 1),
    (0, 1, 1),
    (0, -1, -1),
    (0, 1, -1),
    (0, -1, 1),
)
ALONG = tuple(
    {sign: tuple(i for i in range(19) if VELOCITY[i][dim] == sign) for sign in (1, -1)} for dim in range(3)
)
FACES = ((1, 2), (3, 4), (5, 6))
EDGES = (((0, 1), (7, 8), (9, 10)), ((0, 2), (11, 12), (13, 14)), ((1, 2), (15, 16), (17, 18)))


def orthonormal_rows(monomials):
    rows = []
    for column in range(monomials.shape[1]):
        vector = monomials[:, column] * 1.0
        for sweep in range(2):
            for earlier in rows:
                vector = vector - np.dot(earlier, vector) * earlier
        vector = vector / np.sqrt(np.dot(vector, vector))
        rows.append(vector)
    return np.stack(rows)


def coefficients():
    vel = np.array(VELOCITY) * 1.0
    speeds = np.sum(np.abs(vel), axis=1)
    weights = np.where(speeds == 0, 1.0 / 3.0, np.where(speeds == 1, 1.0 / 18.0, 1.0 / 36.0))
    x, y, z = vel[:, 0], vel[:, 1], vel[:, 2]
    columns = [np.ones(19), x, y, z, x * x, y * y, z * z, x * y, x * z, y * z]
    columns += [x * y * y, x * z * z, y * x * x, y * z * z, z * x * x, z * y * y]
    columns += [x * x * y * y, x * x * z * z, y * y * z * z]
    basis = orthonormal_rows(np.stack(columns, axis=1))
    rates = np.array([0.0] * 4 + [1.6] * 6 + [1.2] * 9)
    relax = basis.T @ np.diag(rates) @ basis
    kept = 1.2 * np.eye(19) - relax
    scalar = relax @ weights
    square = relax @ (weights * x * x)
    first = relax @ (weights * x)
    face = (kept[1] + kept[2]) / 2 - kept[0]
    return dict(
        s0=(scalar[0], scalar[1], scalar[7]),
        s1=(first[1], first[7]),
        s2=(square[0], square[3], square[15], square[1] - square[3], square[7] - square[15]),
        s2_mixed=(relax @ (weights * x * y))[7],
        even=(kept[0][0], kept[0][1], kept[0][7]),
        odd=kept[1][1] / 2 - kept[1][2] / 2,
        square=(face[0], face[3], face[15], face[1] - face[3], face[7] - face[15]),
        mixed=(kept[7][7] + kept[8][7] - kept[9][7] - kept[10][7]) / 4,
    )


COEF = {name: tuple(np.asarray(v, np.float64).reshape(-1).tolist()) for name, v in coefficients().items()}


def pair_sums(members):
    face_sum = [members[a] + members[b] for a, b in FACES]
    face_diff = [members[a] - members[b] for a, b in FACES]
    edge = []
    for dims, (a, b), (c, d) in EDGES:
        edge.append((members[a] + members[b], members[a] - members[b], members[c] + members[d], members[c] - members[d]))
    plane = [e[0] + e[2] for e in edge]
    mixed = [e[0] - e[2] for e in edge]
    lean = [(e[1] + e[3], e[1] - e[3]) for e in edge]
    edge_square = [plane[0] + plane[1], plane[0] + plane[2], plane[1] + plane[2]]
    edge_diff = [lean[0][0] + lean[1][0], lean[0][1] + lean[2][0], lean[1][1] + lean[2][1]]
    face_total = face_sum[0] + face_sum[1] + face_sum[2]
    edge_total = plane[0] + plane[1] + plane[2]
    return face_sum, face_diff, edge, mixed, edge_square, edge_diff, face_total, edge_total


def primal_terms(state):
    face_sum, face_diff, edge, mixed, edge_square, edge_diff, face_total, edge_total = pair_sums(state)
    rho = state[0] + face_total + edge_total
    inverse = 1.0 / rho
    flux = [face_diff[a] + edge_diff[a] for a in range(3)]
    vel = [flux[a] * inverse for a in range(3)]
    third = rho * (1.0 / 3.0)
    press = [face_sum[a] + edge_square[a] - third - flux[a] * vel[a] for a in range(3)]
    total = press[0] + press[1] + press[2]
    centre = total * (2.0 / 21.0)
    stress = [0.4 * (press[a] * (1.0 / 6.0) + centre) for a in range(3)]
    shear = [0.1 * (mixed[e] - flux[dims[0]] * vel[dims[1]]) for e, (dims, _, _) in enumerate(EDGES)]
    flat = (stress[0] + stress[1] + stress[2]) * (-10.0 / 19.0)
    usq = vel[0] * vel[0] + vel[1] * vel[1] + vel[2] * vel[2]
    still = rho * (1.0 - 1.5 * usq)
    rest = 1.2 * state[0] + flat - 0.4 * still
    even, odd = [], []
    for a in range(3):
        feq_even = still + (4.5 * flux[a]) * vel[a]
        even.append(0.6 * face_sum[a] + (flat + stress[a]) - (1.2 / 18.0) * feq_even)
        odd.append(-0.4 * face_diff[a] - (3.6 / 18.0) * flux[a])
    for e, (dims, _, _) in enumerate(EDGES):
        p, q = dims
        bend = flat + stress[p] + stress[q]
        for sign, total_pair, diff_pair in ((1, edge[e][0], edge[e][1]), (-1, edge[e][2], edge[e][3])):
            along_flux = flux[p] + flux[q] if sign == 1 else flux[p] - flux[q]
            along_vel = vel[p] + vel[q] if sign == 1 else vel[p] - vel[q]
            feq_even = still + (4.5 * along_flux) * along_vel
            twist = bend + shear[e] if sign == 1 else bend - shear[e]
            even.append(0.6 * total_pair + twist - (1.2 / 36.0) * feq_even)
            odd.append(-0.4 * diff_pair - (3.6 / 36.0) * along_flux)
    return vel, flux[0], [rest] + even + odd


class Nothing:
    def __add__(self, other):
        return other

    __radd__ = __add__

    def __sub__(self, other):
        return -other

    def __rsub__(self, other):
        return other

    def __mul__(self, other):
        return self

    __rmul__ = __mul__

    def __neg__(self):
        return self


FACTORS = 6


def blocking_factors(blocking):
    open_part = 1.0 - blocking
    return [
        blocking,
        open_part,
        COEF["square"][3] * open_part,
        COEF["mixed"][0] * open_part,
        0.6 * blocking - 0.1,
        -0.1 - 0.4 * blocking,
    ]


def pull_back(read, vel, factors, source=True):
    c = COEF
    blocking, open_part, open_square, open_mixed, keep_sum, keep_diff = factors
    face_sum, face_diff, edge, mixed, edge_square, edge_diff, face_total, edge_total = pair_sums(read)
    rest = read[0]
    twice = face_total + 2.0 * edge_total
    count = rest + (face_total + edge_total)

    def by_class(f):
        return f[0] * count + (f[1] - f[0]) * twice

    s0 = c["s0"][0] * rest + c["s0"][1] * face_total + c["s0"][2] * edge_total
    s2_flat = by_class([9.0 * f for f in c["s2"][:3]])
    s2 = [s2_flat + (9.0 * c["s2"][3]) * face_sum[a] + (9.0 * c["s2"][4]) * edge_square[a] for a in range(3)]
    xy, xz, yz = [(9.0 * c["s2_mixed"][0]) * mixed[e] for e in range(3)]
    s0_thrice = 3.0 * s0
    bend = [
        (s2[0] - s0_thrice) * vel[0] + xy * vel[1] + xz * vel[2],
        xy * vel[0] + (s2[1] - s0_thrice) * vel[1] + yz * vel[2],
        xz * vel[0] + yz * vel[1] + (s2[2] - s0_thrice) * vel[2],
    ]
    density = s0 - 0.5 * (vel[0] * bend[0] + vel[1] * bend[1] + vel[2] * bend[2])
    by_face, by_edge = c["odd"][0] + 3.0 * c["s1"][0], c["odd"][0] + 3.0 * c["s1"][1]
    momentum = [open_part * (by_face * face_diff[a] + by_edge * edge_diff[a] + bend[a]) for a in range(3)]
    if source:
        momentum[0] = momentum[0] + blocking
    even = open_part * (by_class(c["even"]) + density)
    flat = open_part * by_class(c["square"][:3])
    square = [open_square * (face_sum[a] + edge_square[a]) for a in range(3)]
    cross = [open_mixed * mixed[e] for e in range(3)]
    at_face = even + flat
    at_edge = at_face + flat
    out = [None] * 19
    out[0] = (keep_sum + keep_sum) * rest + even
    for a, (i, j) in enumerate(FACES):
        half = keep_sum * face_sum[a] + (at_face + square[a])
        tilt = keep_diff * face_diff[a] + momentum[a]
        out[i], out[j] = half + tilt, half - tilt
    for e, (dims, same, cross_pair) in enumerate(EDGES):
        p, q = dims
        level = at_edge + (square[p] + square[q])
        half = keep_sum * edge[e][0] + (level + cross[e])
        tilt = keep_diff * edge[e][1] + (momentum[p] + momentum[q])
        out[same[0]], out[same[1]] = half + tilt, half - tilt
        half = keep_sum * edge[e][2] + (level - cross[e])
        tilt = keep_diff * edge[e][3] + (momentum[p] - momentum[q])
        out[cross_pair[0]], out[cross_pair[1]] = half + tilt, half - tilt
    sums = list(face_sum) + [s for e in edge for s in (e[0], e[2])]
    diffs = list(face_diff) + [d for e in edge for d in (e[1], e[3])]
    return out, [rest] + sums + diffs


def slot(sign):
    return 0 if sign == 1 else 1


def read_cells(cells, face, columns, corner, extent, x, h):
    nx, ny, nz = extent
    lane = lax.broadcasted_iota(jnp.int32, (8, nz), 1)
    read = []
    for i, (dx, dy, dz) in enumerate(VELOCITY):
        from_x = x + dx
        outside = not 0 <= from_x < nx
        rows = slice(BODY + 8 * h + dy, BODY + 8 * h + dy + 8)
        if outside:
            value = face[slot(dx), ALONG[0][dx].index(i), rows, :]
        else:
            value = cells[i, from_x, rows, :]
        if dz:
            last = nz - 1 if dz == 1 else 0
            if outside:
                column = corner[slot(dx) * 2 + slot(dz)]
                turn = (last - h) % nz
            else:
                column = columns[slot(dz), rows, :]
                turn = (last - ALONG[2][dz].index(i) * nx - from_x) % nz
            column = pltpu.roll(column, turn, 1) if turn else column
            value = jnp.where(lane == last, column, pltpu.roll(value, nz - 1 if dz == 1 else 1, 1))
        read.append(value)
    return read


def one_level(cells, face, columns, corner, terms, factors, extent, x, h):
    rows = slice(8 * h, 8 * h + 8)
    read = read_cells(cells, face, columns, corner, extent, x, h)
    vel = [terms[a, x, rows, :] for a in range(3)]
    return pull_back(read, vel, [factors[j, x, rows, :] for j in range(FACTORS)])


def corner_members(dy):
    return ((member_at((0, dy, dy)), dy), (member_at((0, dy, -dy)), -dy))


def corner_tile(extent, dy):
    return (extent[1] // 8 - 1, 7) if dy == 1 else (0, 0)


def corner_change(got, extent, dy, x):
    nx, ny, nz = extent
    lane = lax.broadcasted_iota(jnp.int32, (8, nz), 1)
    row = lax.broadcasted_iota(jnp.int32, (8, nz), 0)
    change = jnp.zeros((8, nz), F32)
    for i, dz in corner_members(dy):
        last = nz - 1 if dz == 1 else 0
        turn = (last - ALONG[2][dz].index(i) * nx - x) % nz
        value = jnp.broadcast_to(got[slot(dy) * 2 + slot(dz)], (8, nz))
        value = pltpu.roll(value, turn, 1) if turn else value
        change = jnp.where(lane == last, value, change)
    return jnp.where(row == corner_tile(extent, dy)[1], change, 0.0)


def corner_response(terms, factors, extent, dy, x):
    nx, ny, nz = extent
    h, at = corner_tile(extent, dy)
    rows = slice(8 * h, 8 * h + 8)
    lane = lax.broadcasted_iota(jnp.int32, (8, nz), 1)
    row = lax.broadcasted_iota(jnp.int32, (8, nz), 0)
    read = [Nothing()] * 19
    for i, dz in corner_members(dy):
        read[i] = jnp.where((row == at) & (lane == (nz - 1 if dz == 1 else 0)), 1.0, 0.0)
    vel = [terms[a, x, rows, :] for a in range(3)]
    return pull_back(read, vel, [factors[j, x, rows, :] for j in range(FACTORS)], source=False)[0]


def corner_weight(terms, extent, dy, x):
    nx, ny, nz = extent
    h = corner_tile(extent, dy)[0]
    rows = slice(8 * h, 8 * h + 8)
    lane = lax.broadcasted_iota(jnp.int32, (8, nz), 1)
    even, odd = 3 + 1 + 3 + 4, 3 + 1 + 9 + 3 + 4
    same, cross = [
        terms[even + n, x, rows, :] + terms[odd + n, x, rows, :]
        if dy == 1
        else terms[even + n, x, rows, :] - terms[odd + n, x, rows, :]
        for n in range(2)
    ]
    return jnp.where(lane == (nz - 1 if dy == 1 else 0), same, cross)


def weigh(terms, weighed, x, rows):
    total = weighed[0] * terms[3, x, rows, :]
    for j in range(1, 19):
        total = total + weighed[j] * terms[3 + j, x, rows, :]
    return total


def member_at(velocity):
    return VELOCITY.index(velocity)


BODY = 8


def kernel(
    mesh_sizes,
    extent,
    primal,
    adjoint,
    porosity,
    solid,
    out_inner,
    out_grad,
    out_drag,
    level_one,
    marks,
    factors,
    terms_last,
    face_last,
    columns_last,
    corner_last,
    level_two,
    states,
    porous,
    terms_first,
    sums,
    face_send,
    rows_send,
    columns_send,
    xy_send,
    xz_send,
    yz_send,
    face_first,
    rows_recv,
    columns_first,
    xy_recv,
    corner_first,
    yz_recv,
    response,
    drag_row,
    drag_slots,
    meter,
    load_sem,
    send_sem,
    recv_sem,
    drag_sem,
    relay_sem,
):
    sx, sy, sz = mesh_sizes
    nx, ny, nz = extent
    halves = ny // 8
    terms = (terms_first, terms_last)
    face_recv = (face_first, face_last)
    columns_recv = (columns_first, columns_last)
    xz_recv = (corner_first, corner_last)
    body = pl.ds(BODY, ny)
    inner = tuple(range(1, nx - 1))
    outer = (0, nx - 1)
    me = (lax.axis_index("gx"), lax.axis_index("gy"), lax.axis_index("gz"))
    loads = [
        pltpu.make_async_copy(adjoint, level_two.at[:, :, body, :], load_sem.at[0]),
        pltpu.make_async_copy(primal, states, load_sem.at[1]),
        pltpu.make_async_copy(porosity, porous, load_sem.at[2]),
        pltpu.make_async_copy(solid, marks, load_sem.at[3]),
    ]
    for load in loads:
        load.start()

    stepped = tuple(
        {
            0: me[d],
            1: jnp.where(me[d] == mesh_sizes[d] - 1, 0, me[d] + 1),
            -1: jnp.where(me[d] == 0, mesh_sizes[d] - 1, me[d] - 1),
        }
        for d in range(3)
    )

    def shifted(offset):
        return tuple(stepped[d][offset[d]] for d in range(3))

    faces = [tuple(s if d == dim else 0 for d in range(3)) for dim in range(3) for s in (1, -1)]
    edges = [
        tuple(s if d == p else t if d == q else 0 for d in range(3))
        for p, q in ((1, 2), (0, 2), (0, 1))
        for s in (1, -1)
        for t in (1, -1)
    ]
    around = edges + faces
    corner_part = [d for d in edges if not d[0]]
    near_part = [d for d in faces if not d[0]]
    side_part = [d for d in around if d[0]]

    pairs = sx // 2
    pair = sum(jnp.where(me[0] >= 2 * n, 1, 0) for n in range(1, pairs)) if pairs > 1 else 0
    core = me[0] - 2 * pair

    def ahead(index, count, size):
        moved = index + count
        return jnp.where(moved >= size, moved - size, moved) if count else index

    first_group = [(c, z) for c in range(2) for z in range(sz) if (c, z) != (0, 0)]
    second_group = [(h, y) for h in range(pairs) for y in range(sy) if (h, y) != (0, 0)]

    def first_partner(c, z):
        return (pair * 2 + ahead(core, c, 2), me[1], ahead(me[2], z, sz))

    def second_partner(h, y):
        return (ahead(pair, h, pairs) * 2 + core, ahead(me[1], y, sy), me[2])

    barrier = pltpu.get_barrier_semaphore()
    def ring(count, size):
        return min(count % size, -count % size)

    def first_hops(c, z):
        return ring(z, sz)

    def second_hops(h, y):
        if y % 2 == 0:
            return 2 * h + ring(y // 2, sy // 2)
        return 1 + max(ring(y // 2, sy // 2), ring(y // 2 + 1, sy // 2))

    first_near = [o for o in first_group if first_hops(*o) <= 3]
    first_far = [o for o in first_group if first_hops(*o) > 3]
    second_near = [o for o in second_group if second_hops(*o) <= 3]
    second_far = [o for o in second_group if second_hops(*o) > 3]
    signals = [(first_hops(*o), first_partner(*o)) for o in first_near if o not in ((0, 1), (0, sz - 1))]
    signals += [(second_hops(*o), second_partner(*o)) for o in second_near if o not in ((0, 1), (0, sy - 1))]
    for offset in around:
        signals.append((2 * abs(offset[0]) + 1.5 * abs(offset[1]) + abs(offset[2]), shifted(offset)))
    targets = [entry[1] for entry in sorted(signals, key=lambda entry: -entry[0])]
    for target in targets:
        pl.semaphore_signal(barrier, inc=1, device_id=target, device_id_type=MESH)

    for sign in (1, -1):
        for k, i in enumerate(ALONG[0][sign]):
            source = adjoint.at[i, 0 if sign == 1 else nx - 1]
            pltpu.make_async_copy(source, face_send.at[0, slot(sign), k], load_sem.at[4]).start()

    lane = lax.broadcasted_iota(jnp.int32, (8, nz), 1)

    def pack(step, cells, planes, again):
        for sign in (1, -1):
            at = slot(sign)
            for h in range(halves):
                rows = slice(8 * h, 8 * h + 8)
                packed = columns_send[step, at, rows, :] if again else jnp.zeros((8, nz), F32)
                for k, i in enumerate(ALONG[2][sign]):
                    for x in planes:
                        spot = k * nx + x
                        column = cells[i, x, BODY + 8 * h : BODY + 8 * h + 8, :]
                        turn = (spot if sign == 1 else spot + 1) % nz
                        column = pltpu.roll(column, turn, 1) if turn else column
                        packed = jnp.where(lane == spot, column, packed)
                columns_send[step, at, rows, :] = packed
            edge_row = BODY if sign == 1 else BODY + ny - 1
            for k, i in enumerate(ALONG[1][sign]):
                for x in planes:
                    rows_send[step, at, k * nx + x : k * nx + x + 1, :] = cells[i, x, edge_row : edge_row + 1, :]

    def pack_edges(step, cells):
        for p in (1, -1):
            near = 0 if p == 1 else nx - 1
            for q in (1, -1):
                i = member_at((p, q, 0))
                row = BODY if q == 1 else BODY + ny - 1
                xy_send[step, slot(p) * 2 + slot(q)] = cells[i, near, row : row + 1, :]
                i = member_at((p, 0, q))
                packed = None
                for h in range(halves):
                    column = cells[i, near, BODY + 8 * h : BODY + 8 * h + 8, :]
                    turn = (h if q == 1 else h + 1) % nz
                    column = pltpu.roll(column, turn, 1) if turn else column
                    packed = column if packed is None else jnp.where(lane == h, column, packed)
                xz_send[step, slot(p) * 2 + slot(q)] = packed

    def pack_corners(step, cells):
        for p in (1, -1):
            row = BODY if p == 1 else BODY + ny - 1
            for q in (1, -1):
                i = member_at((0, p, q))
                packed = None
                for x in range(nx):
                    spot = ALONG[2][q].index(i) * nx + x
                    corner = cells[i, x, row : row + 1, :]
                    turn = (spot if q == 1 else spot + 1) % nz
                    corner = pltpu.roll(corner, turn, 1) if turn else corner
                    packed = corner if packed is None else jnp.where(lane[0:1] == spot, corner, packed)
                yz_send[step, slot(p) * 2 + slot(q)] = packed

    def message(step, direction):
        dx, dy, dz = direction
        if dx and not dy and not dz:
            source = face_send.at[step, slot(dx)]
            target = face_recv[step].at[slot(dx), :, body, :]
        elif dy and not dx and not dz:
            source = rows_send.at[step, slot(dy)]
            target = rows_recv.at[step, slot(dy)]
        elif dz and not dx and not dy:
            source = columns_send.at[step, slot(dz)]
            target = columns_recv[step].at[slot(dz), body, :]
        elif not dz:
            source = xy_send.at[step, slot(dx) * 2 + slot(dy)]
            target = xy_recv.at[step, slot(dx) * 2 + slot(dy)]
        elif not dy:
            source = xz_send.at[step, slot(dx) * 2 + slot(dz)]
            target = xz_recv[step].at[slot(dx) * 2 + slot(dz)]
        else:
            source = yz_send.at[step, slot(dy) * 2 + slot(dz)]
            target = yz_recv.at[step, slot(dy) * 2 + slot(dz)]
        copy = pltpu.make_async_remote_copy(
            src_ref=source,
            dst_ref=target,
            send_sem=send_sem.at[0],
            recv_sem=recv_sem.at[step, 1 if dx else 2 if dy and dz else 0],
            device_id=shifted(tuple(-d for d in direction)),
            device_id_type=MESH,
        )
        return copy

    def send(step, directions):
        for direction in directions:
            message(step, direction).start()

    def await_rows(rows, semaphore):
        whole = meter.at[pl.ds(0, rows)]
        pltpu.make_async_copy(whole, whole, semaphore).wait()

    def halo_row(sign):
        return BODY + ny if sign == 1 else BODY - 1

    def insert_rows(step, cells):
        for sign in (1, -1):
            row = halo_row(sign)
            for k, i in enumerate(ALONG[1][sign]):
                for x in range(nx):
                    if 0 <= x - VELOCITY[i][0] < nx:
                        got = rows_recv[step, slot(sign), k * nx + x : k * nx + x + 1, :]
                        cells[i, x, row : row + 1, :] = got

    def insert_edges(step):
        for dx in (1, -1):
            for dy in (1, -1):
                k = ALONG[0][dx].index(member_at((dx, dy, 0)))
                row = halo_row(dy)
                face_recv[step][slot(dx), k, row : row + 1, :] = xy_recv[step, slot(dx) * 2 + slot(dy)]

    def level(step, cells, x, h):
        return one_level(cells, face_recv[step], columns_recv[step], xz_recv[step], terms[step], factors, extent, x, h)

    nothing = jnp.zeros((1, nz), F32)
    for columns in columns_recv:
        for at in range(2):
            columns[at, BODY - 1 : BODY, :] = nothing
            columns[at, BODY + ny : BODY + ny + 1, :] = nothing
    loads[0].wait()
    pack(0, level_two, range(nx), False)
    pack_edges(0, level_two)
    pack_corners(0, level_two)
    for load in loads[1:]:
        load.wait()
    total = jnp.zeros((8, nz), F32)
    for x in range(nx):
        for h in range(halves):
            rows = slice(8 * h, 8 * h + 8)
            closed = jnp.where(marks[x, rows, :] == 0, porous[x, rows, :], 1.0)
            for j, value in enumerate(blocking_factors(closed)):
                factors[j, x, rows, :] = value
            flux = None
            for t in range(2):
                gain = sum(states[t, i, x, rows, :] for i in ALONG[0][1])
                loss = sum(states[t, i, x, rows, :] for i in ALONG[0][-1])
                flux = gain - loss if flux is None else flux + (gain - loss)
            out_grad[x, rows, :] = flux
            total = total + closed * flux
    drag_row[0] = jnp.sum(total, axis=0, keepdims=True)
    faces_in = face_send.at[0]
    pltpu.make_async_copy(faces_in, faces_in, load_sem.at[4]).wait()

    pl.semaphore_wait(barrier, len(targets))

    send(0, side_part)
    send(0, corner_part)
    send(0, near_part)
    pl.semaphore_signal(relay_sem.at[0], inc=1, device_id=first_partner(0, sz - 2), device_id_type=MESH)
    pl.semaphore_signal(relay_sem.at[1], inc=1, device_id=second_partner(1, 0), device_id_type=MESH)
    near_rows = sum(message_rows(d, extent) for d in near_part)
    side_rows = sum(message_rows(d, extent) for d in side_part)
    corner_rows = sum(message_rows(d, extent) for d in corner_part)

    mine_first = core * sz + me[2]
    mine_second = pair * sy + me[1]
    drag_first = drag_slots.at[pl.ds(0, 2 * sz)]
    drag_second = drag_slots.at[pl.ds(2 * sz, pairs * sy)]

    def drag_send(stage, target, mine, group, partner):
        for offset in group:
            pltpu.make_async_remote_copy(
                src_ref=drag_row.at[stage],
                dst_ref=target.at[mine],
                send_sem=drag_sem.at[2],
                recv_sem=drag_sem.at[stage],
                device_id=partner(*offset),
                device_id_type=MESH,
            ).start()

    drag_first[mine_first] = drag_row[0]
    drag_send(0, drag_first, mine_first, first_near, first_partner)

    for step, t in ((0, 1), (1, 0)):
        for x in range(nx):
            for h in range(halves):
                rows = slice(8 * h, 8 * h + 8)
                vel, _, weights = primal_terms([states[t, i, x, rows, :] for i in range(19)])
                for j, value in enumerate(vel + weights):
                    terms[step][j, x, rows, :] = value

    for step in range(2):
        for x in range(nx) if step == 0 else inner:
            for dy in (1, -1):
                for i, value in enumerate(corner_response(terms[step], factors, extent, dy, x)):
                    response[step, slot(dy), i, x] = value

    def first_level(x):
        for h in range(halves):
            fresh, weighed = level(0, level_two, x, h)
            rows = slice(8 * h, 8 * h + 8)
            for i in range(19):
                level_one[i, x, BODY + 8 * h : BODY + 8 * h + 8, :] = fresh[i]
                sums[i, x, rows, :] = weighed[i]
            for sign, near in ((1, 0), (-1, nx - 1)):
                if x == near:
                    for k, i in enumerate(ALONG[0][sign]):
                        face_send[1, slot(sign), k, rows, :] = fresh[i]

    def first_corners(x, changes, members):
        for dy in (1, -1):
            h = corner_tile(extent, dy)[0]
            for i in members:
                rows = slice(BODY + 8 * h, BODY + 8 * h + 8)
                value = level_one[i, x, rows, :] + changes[x, dy] * response[0, slot(dy), i, x]
                level_one[i, x, rows, :] = value
                for sign, near in ((1, 0), (-1, nx - 1)):
                    if x == near and i in ALONG[0][sign]:
                        face_send[1, slot(sign), ALONG[0][sign].index(i), 8 * h : 8 * h + 8, :] = value

    pl.semaphore_wait(relay_sem.at[0], 1)
    pl.semaphore_wait(relay_sem.at[1], 1)
    drag_send(0, drag_first, mine_first, first_far, first_partner)
    await_rows(near_rows, recv_sem.at[0, 0])
    insert_rows(0, level_two)
    for x in inner:
        first_level(x)
    await_rows(side_rows, recv_sem.at[0, 1])
    insert_edges(0)
    for x in outer:
        first_level(x)
    await_rows(corner_rows, recv_sem.at[0, 2])
    changes = {(x, dy): corner_change(yz_recv[0], extent, dy, x) for x in range(nx) for dy in (1, -1)}
    at_corner = tuple(member_at((0, p, q)) for p in (1, -1) for q in (1, -1))
    elsewhere = tuple(i for i in range(19) if i not in at_corner)
    for x in range(nx):
        first_corners(x, changes, at_corner)
    pack_corners(1, level_one)
    for x in outer:
        first_corners(x, changes, elsewhere)
    pack_edges(1, level_one)
    send(1, side_part)
    send(1, corner_part)
    for x in inner:
        first_corners(x, changes, elsewhere)
    pack(1, level_one, range(nx), False)
    send(1, near_part)

    for x in range(nx):
        for h in range(halves):
            rows = slice(8 * h, 8 * h + 8)
            weighed = [sums[j, x, rows, :] for j in range(19)]
            total = out_grad[x, rows, :] + weigh(terms[0], weighed, x, rows)
            for dy in (1, -1):
                if h == corner_tile(extent, dy)[0]:
                    change = corner_change(yz_recv[0], extent, dy, x)
                    total = total + change * corner_weight(terms[0], extent, dy, x)
            out_grad[x, rows, :] = total

    await_rows(len(first_group), drag_sem.at[0])
    drag_row[1] = jnp.sum(drag_first[...], axis=0)
    drag_second[mine_second] = drag_row[1]
    drag_send(1, drag_second, mine_second, second_far + second_near, second_partner)

    def second_level(x):
        for h in range(halves):
            rows = slice(8 * h, 8 * h + 8)
            fresh, weighed = level(1, level_one, x, h)
            for i in range(19):
                out_inner[i, x - 1, rows, :] = fresh[i]
            total = out_grad[x, rows, :] + weigh(terms[1], weighed, x, rows)
            out_grad[x, rows, :] = jnp.where(marks[x, rows, :] == 0, total, 0.0)

    await_rows(near_rows, recv_sem.at[1, 0])
    insert_rows(1, level_one)
    for x in inner:
        second_level(x)
    await_rows(side_rows, recv_sem.at[1, 1])
    insert_edges(1)
    await_rows(corner_rows, recv_sem.at[1, 2])
    for x in inner:
        for dy in (1, -1):
            h = corner_tile(extent, dy)[0]
            rows = slice(8 * h, 8 * h + 8)
            change = corner_change(yz_recv[1], extent, dy, x)
            for i in range(19):
                out_inner[i, x - 1, rows, :] = out_inner[i, x - 1, rows, :] + change * response[1, slot(dy), i, x]
            slope = change * corner_weight(terms[1], extent, dy, x)
            out_grad[x, rows, :] = out_grad[x, rows, :] + jnp.where(marks[x, rows, :] == 0, slope, 0.0)
    for sign in (1, -1):
        row = halo_row(sign)
        for t in (1, -1):
            columns_recv[1][slot(t), row : row + 1, :] = yz_recv[1, slot(sign) * 2 + slot(t)]

    await_rows(len(second_group), drag_sem.at[1])
    everyone = jnp.sum(drag_second[...], axis=0)
    cells_in_all = nx * ny * nz * sx * sy * sz
    out_drag[...] = jnp.broadcast_to(jnp.sum(everyone, axis=1, keepdims=True) * (1.0 / cells_in_all), (8, nz))

    await_rows(2 * (near_rows + side_rows + corner_rows), send_sem.at[0])
    await_rows(len(first_group) + len(second_group), drag_sem.at[2])


def message_rows(direction, extent):
    nx, ny, nz = extent
    dx, dy, dz = (d != 0 for d in direction)
    if dx + dy + dz == 1:
        return 5 * ny if dx else -(-5 * nx // 8) * 8 if dy else ny
    return 8 if dx and dz else 1


def finish(
    extent,
    inner,
    grad,
    drag,
    cells,
    marks,
    factors,
    terms,
    face,
    columns,
    corner,
    out_adjoint,
    out_grad,
    out_drag,
    outer,
    grad_whole,
    total,
    sem,
):
    nx, ny, nz = extent
    copies = [pltpu.make_async_copy(inner, out_adjoint.at[:, pl.ds(1, nx - 2)], sem.at[0])]
    copies[0].start()
    total[...] = drag[0:1, 0:1]
    copies.append(pltpu.make_async_copy(total, out_drag, sem.at[1]))
    copies[1].start()
    for n, x in enumerate((0, nx - 1)):
        for h in range(ny // 8):
            rows = slice(8 * h, 8 * h + 8)
            fresh, weighed = one_level(cells, face, columns, corner, terms, factors, extent, x, h)
            for i in range(19):
                outer[n, i, rows, :] = fresh[i]
            slope = grad[x, rows, :] + weigh(terms, weighed, x, rows)
            grad_whole[x, rows, :] = jnp.where(marks[x, rows, :] == 0, slope, 0.0)
        copies.append(pltpu.make_async_copy(outer.at[n], out_adjoint.at[:, x], sem.at[2 + n]))
        copies[-1].start()
    for x in range(1, nx - 1):
        grad_whole[x] = grad[x]
    copies.append(pltpu.make_async_copy(grad_whole, out_grad, sem.at[4]))
    copies[-1].start()
    for copy in copies:
        copy.wait()


def solution(mesh):
    sizes = tuple(mesh.shape[name] for name in ("gx", "gy", "gz"))

    def body(primal_states, adjoint_last, porosity, solid_mask):
        nx, ny, nz = porosity.shape
        padded = ny + 16
        row_tiles = -(-5 * nx // 8) * 8
        hbm = pl.BlockSpec(memory_space=pltpu.HBM)
        vmem = pl.BlockSpec(memory_space=pltpu.VMEM)
        arguments = [
            pltpu.with_memory_space_constraint(v, pltpu.HBM)
            for v in (primal_states, adjoint_last, porosity, solid_mask)
        ]
        results = pl.pallas_call(
            functools.partial(kernel, sizes, (nx, ny, nz)),
            name="adjoint_window",
            out_shape=(
                pltpu.VMEM((19, nx - 2, ny, nz), F32),
                pltpu.VMEM((nx, ny, nz), F32),
                pltpu.VMEM((8, nz), F32),
                pltpu.VMEM((19, nx, padded, nz), F32),
                pltpu.VMEM((nx, ny, nz), jnp.int32),
                pltpu.VMEM((FACTORS, nx, ny, nz), F32),
                pltpu.VMEM((22, nx, ny, nz), F32),
                pltpu.VMEM((2, 5, padded, nz), F32),
                pltpu.VMEM((2, padded, nz), F32),
                pltpu.VMEM((4, 8, nz), F32),
            ),
            in_specs=[hbm] * 4,
            out_specs=(vmem,) * 10,
            scratch_shapes=[
                pltpu.VMEM((19, nx, padded, nz), F32),
                pltpu.VMEM((2, 19, nx, ny, nz), F32),
                pltpu.VMEM((nx, ny, nz), F32),
                pltpu.VMEM((22, nx, ny, nz), F32),
                pltpu.VMEM((19, nx, ny, nz), F32),
                pltpu.VMEM((2, 2, 5, ny, nz), F32),
                pltpu.VMEM((2, 2, row_tiles, nz), F32),
                pltpu.VMEM((2, 2, ny, nz), F32),
                pltpu.VMEM((2, 4, 1, nz), F32),
                pltpu.VMEM((2, 4, 8, nz), F32),
                pltpu.VMEM((2, 4, 1, nz), F32),
                pltpu.VMEM((2, 5, padded, nz), F32),
                pltpu.VMEM((2, 2, row_tiles, nz), F32),
                pltpu.VMEM((2, padded, nz), F32),
                pltpu.VMEM((2, 4, 1, nz), F32),
                pltpu.VMEM((4, 8, nz), F32),
                pltpu.VMEM((2, 4, 1, nz), F32),
                pltpu.VMEM((2, 2, 19, nx, 8, nz), F32),
                pltpu.VMEM((2, 1, nz), F32),
                pltpu.VMEM((2 * sizes[2] + sizes[0] // 2 * sizes[1], 1, nz), F32),
                pltpu.VMEM((1024, 1, nz), F32),
                pltpu.SemaphoreType.DMA((5,)),
                pltpu.SemaphoreType.DMA((1,)),
                pltpu.SemaphoreType.DMA((2, 3)),
                pltpu.SemaphoreType.DMA((3,)),
                pltpu.SemaphoreType.REGULAR((2,)),
            ],
            compiler_params=pltpu.CompilerParams(
                collective_id=0, has_side_effects=True, vmem_limit_bytes=16 << 20
            ),
        )(*arguments)
        adjoint, gradient, drag = pl.pallas_call(
            functools.partial(finish, (nx, ny, nz)),
            name="finish",
            out_shape=(
                jax.ShapeDtypeStruct((19, nx, ny, nz), F32),
                jax.ShapeDtypeStruct((nx, ny, nz), F32),
                jax.ShapeDtypeStruct((1, 1), F32),
            ),
            in_specs=[vmem] * 10,
            out_specs=(hbm, hbm, hbm),
            scratch_shapes=[
                pltpu.VMEM((2, 19, ny, nz), F32),
                pltpu.VMEM((nx, ny, nz), F32),
                pltpu.VMEM((1, 1), F32),
                pltpu.SemaphoreType.DMA((5,)),
            ],
            compiler_params=pltpu.CompilerParams(vmem_limit_bytes=2 << 20),
        )(*results)
        return adjoint, gradient, drag.reshape(())

    return jax.shard_map(
        body,
        mesh=mesh,
        in_specs=(
            P(None, None, "gx", "gy", "gz"),
            P(None, "gx", "gy", "gz"),
            P("gx", "gy", "gz"),
            P("gx", "gy", "gz"),
        ),
        out_specs=(P(None, "gx", "gy", "gz"), P("gx", "gy", "gz"), P()),
        check_vma=False,
    )
```
